128 devices in a mesh: grp: 2 (over y_lo), dev: 64 (over y_hi, x, z, core).
Axes of the slice: x: 4, y: 4 (y_hi: 2, y_lo: 2; y = y_hi * 2 + y_lo), z: 4, core: 2. Of those that a mesh axis runs over, the one named last changes fastest.
Arguments:
- weights: float32 [2, 64, 524288], P(None, None, ('grp', 'dev')), may hold values from -3 to 3
- owner_map: int32 [16], replicated, may hold values from 0 to 15, each once
- node_index: int32 [2, 64], replicated, may hold values from 0 to 7, as said below
Outputs:
- transformed: float32 [2, 64, 524288], P(None, None, ('grp', 'dev'))
The draws below stay inside these ranges and needn't reach their ends.
Inputs may be any that keep to these rules, and one draw needn't show every extreme that they name: owner_map[col] = 2 k + rx puts coarse frequency column col at column slot rx of device group k, in grp+dev order, after the middle level; every value appears once. The 64 columns (node_index[0, t], node_index[1, t]) are distinct, so every pair of Chebyshev point numbers appears once.
All inputs are finite; a program needn't handle non-finite values.
Results may differ from the reference program's by a relative error of at most 0.0003.
Values sent between devices are 32-bit elements; how exact they have to be, the bound alone decides.
A program may use at most 128 MiB of HBM per device.

```python
import math
import jax
import jax.numpy as jnp
from jax import lax

NFREQ = 4096
CHEB = 8
Q = 64
P_DEV = 4096
PAIRS = 524288
N_GRP = 2
N_DEV = 64


def draw_node_index(key, part):
    order_ids = jax.random.permutation(jax.random.fold_in(key, 7), CHEB * CHEB).astype(jnp.int32)
    return jnp.stack([order_ids // CHEB, order_ids % CHEB])


def block_scale(rng, shape, cuts, least, largest):
    factor_of = 1.0
    for position, parts in cuts:
        draws = jax.random.uniform(jax.random.fold_in(jax.random.fold_in(rng, 6), position), (parts,), jnp.float32, least / len(cuts), largest / len(cuts))
        factor_of = factor_of * jnp.repeat(jnp.exp(draws), shape[position] // parts).reshape((-1,) + (1,) * (len(shape) - 1 - position))
    return factor_of


def gaussian(stream_key, shape, width, reach, split=(), held_as=jnp.bfloat16):
    entries = width * jax.random.normal(stream_key, shape, jnp.float32)
    if split:
        entries = entries * block_scale(stream_key, shape, split, -0.22, 0.18)
    return jnp.clip(entries, -reach, reach).astype(held_as)


def setup_inputs(seed: int = 0) -> dict:
    seeds = jax.random.split(jax.random.key(seed), 4)
    weights = gaussian(seeds[0], (2, Q, PAIRS), 0.5, 3.0, ((2, 128),), jnp.float32)
    owner_map = jax.random.permutation(seeds[1], 16).astype(jnp.int32)
    node_index = draw_node_index(jax.random.fold_in(seeds[3], 71), 0)
    return dict(weights=weights, owner_map=owner_map, node_index=node_index)


TWO_PI = 2.0 * math.pi
HIGHEST = lax.Precision.HIGHEST

def cheb_points():
    counter = jnp.arange(CHEB, dtype=jnp.float32)
    return 0.5 * jnp.cos(math.pi * (2.0 * counter + 1.0) / (2.0 * CHEB))

def node_select(node_index):
    numbers = jnp.arange(CHEB, dtype=jnp.int32)[None, :]
    select_x = (node_index[0][:, None] == numbers).astype(jnp.float32)
    select_y = (node_index[1][:, None] == numbers).astype(jnp.float32)
    return (select_x, select_y)

def node_offsets(node_index):
    points = cheb_points()
    select_x, select_y = node_select(node_index)
    return (lax.optimization_barrier(jnp.sum(select_x * points[None, :], axis=1)), lax.optimization_barrier(jnp.sum(select_y * points[None, :], axis=1)))

def lagrange(places):
    points = cheb_points()
    rows_out = []
    for first_id in range(CHEB):
        product = jnp.ones_like(places)
        for other_id in range(CHEB):
            if other_id != first_id:
                product = product * (places - points[other_id]) / (points[first_id] - points[other_id])
        rows_out.append(product)
    return jnp.stack(rows_out)

def child_tables(node_index):
    select_x, select_y = node_select(node_index)
    offset_x, offset_y = node_offsets(node_index)
    tables = []
    for child_id in range(4):
        basis_x = lagrange(0.5 * offset_x + 0.5 * (child_id % 2) - 0.25)
        basis_y = lagrange(0.5 * offset_y + 0.5 * (child_id // 2) - 0.25)
        table_x = lax.optimization_barrier(jnp.sum(select_x[:, :, None] * basis_x[None, :, :], axis=1))
        table_y = lax.optimization_barrier(jnp.sum(select_y[:, :, None] * basis_y[None, :, :], axis=1))
        tables.append(table_x * table_y)
    return jnp.stack(tables)

def speeds(place_x, place_y):
    speed_one = (2.0 + jnp.sin(TWO_PI * place_x) * jnp.sin(TWO_PI * place_y)) / 16.0
    speed_two = (2.0 + jnp.cos(TWO_PI * place_x) * jnp.cos(TWO_PI * place_y)) / 16.0
    return (speed_one * speed_one, speed_two * speed_two)

def radius(speed_x, speed_y, freq_x, freq_y):
    return jnp.sqrt(speed_x * freq_x * freq_x + speed_y * freq_y * freq_y + 1.0)

def freq_phase(place_x, place_y, freq_x, freq_y, centre_x, centre_y):
    speed_x, speed_y = speeds(place_x, place_y)
    numer_part = speed_x * (freq_x - centre_x) * (freq_x + centre_x) + speed_y * (freq_y - centre_y) * (freq_y + centre_y)
    denom_part = radius(speed_x, speed_y, freq_x, freq_y) + radius(speed_x, speed_y, centre_x, centre_y)
    return TWO_PI * (place_x * (freq_x - centre_x) + place_y * (freq_y - centre_y) + numer_part / denom_part)

def space_phase(place_x, place_y, anchor_x, anchor_y, freq_x, freq_y):
    speed_x, speed_y = speeds(place_x, place_y)
    base_x, base_y = speeds(anchor_x, anchor_y)
    numer_part = (speed_x - base_x) * freq_x * freq_x + (speed_y - base_y) * freq_y * freq_y
    denom_part = radius(speed_x, speed_y, freq_x, freq_y) + radius(base_x, base_y, freq_x, freq_y)
    return TWO_PI * ((place_x - anchor_x) * freq_x + (place_y - anchor_y) * freq_y + numer_part / denom_part)

def rotate(values, phase_angle):
    cosine = jnp.cos(phase_angle)
    sine_part = jnp.sin(phase_angle)
    return jnp.stack([values[0] * cosine - values[1] * sine_part, values[0] * sine_part + values[1] * cosine])

def freq_level(pieces, space_x, space_y, box_x, box_y, level_id, offset_x, offset_y):
    width_a = 2.0 ** (-level_id)
    width_b = 2.0 ** level_id
    half_span = 0.5 * NFREQ
    centre_ax = ((space_x + 0.5) * width_a)[None, :]
    centre_ay = ((space_y + 0.5) * width_a)[None, :]
    centre_bx = ((box_x + 0.5) * width_b - half_span)[None, :]
    centre_by = ((box_y + 0.5) * width_b - half_span)[None, :]
    running = None
    for values, child_x, child_y, table_now in pieces:
        kid_x = ((2.0 * box_x + child_x + 0.5) * (0.5 * width_b) - half_span)[None, :] + 0.5 * width_b * offset_x[:, None]
        kid_y = ((2.0 * box_y + child_y + 0.5) * (0.5 * width_b) - half_span)[None, :] + 0.5 * width_b * offset_y[:, None]
        phase_angle = freq_phase(centre_ax, centre_ay, kid_x, kid_y, centre_bx, centre_by)
        product_term = jnp.einsum('ts,rsn->rtn', table_now, rotate(values, -phase_angle), precision=HIGHEST)
        running = product_term if running is None else running + product_term
    node_x = centre_bx + width_b * offset_x[:, None]
    node_y = centre_by + width_b * offset_y[:, None]
    return rotate(running, freq_phase(centre_ax, centre_ay, node_x, node_y, centre_bx, centre_by))

def space_in(values, offset_x, offset_y, parent_x, parent_y, box_x, box_y, level_id):
    width_p = 2.0 ** (1 - level_id)
    anchor_x = ((parent_x + 0.5) * width_p)[None, :]
    anchor_y = ((parent_y + 0.5) * width_p)[None, :]
    freq_x = ((box_x + 0.5) * 2.0 ** level_id - 0.5 * NFREQ)[None, :]
    freq_y = ((box_y + 0.5) * 2.0 ** level_id - 0.5 * NFREQ)[None, :]
    place_x = anchor_x + width_p * offset_x[:, None]
    place_y = anchor_y + width_p * offset_y[:, None]
    return rotate(values, -space_phase(place_x, place_y, anchor_x, anchor_y, freq_x, freq_y))

def space_out(turned_in, table_now, offset_x, offset_y, parent_x, parent_y, child_x, child_y, box_x, box_y, level_id):
    width_a = 2.0 ** (-level_id)
    mixed_state = jnp.einsum('st,rsn->rtn', table_now, turned_in, precision=HIGHEST)
    anchor_x = ((parent_x + 0.5) * 2.0 * width_a)[None, :]
    anchor_y = ((parent_y + 0.5) * 2.0 * width_a)[None, :]
    place_x = ((2.0 * parent_x + child_x + 0.5) * width_a)[None, :] + width_a * offset_x[:, None]
    place_y = ((2.0 * parent_y + child_y + 0.5) * width_a)[None, :] + width_a * offset_y[:, None]
    freq_x = ((box_x + 0.5) * 2.0 ** level_id - 0.5 * NFREQ)[None, :]
    freq_y = ((box_y + 0.5) * 2.0 ** level_id - 0.5 * NFREQ)[None, :]
    return rotate(mixed_state, space_phase(place_x, place_y, anchor_x, anchor_y, freq_x, freq_y))

def first_geometry(step_id, group_ids, low_digit, high_digit, loc_ids, across):
    column = loc_ids % across
    row_id = loc_ids // across
    if step_id == 0:
        space_x = 2 * group_ids + low_digit % 2
        space_y = low_digit // 2
        box_x = 2 * column + high_digit % 2
        box_y = 2 * row_id + high_digit // 2
    else:
        space_x = 4 * group_ids + 2 * (low_digit % 2) + high_digit % 2
        space_y = 2 * (low_digit // 2) + high_digit // 2
        box_x = column
        box_y = row_id
    return [jnp.broadcast_to(jnp.asarray(entry_value), loc_ids.shape).astype(jnp.float32) for entry_value in (space_x, space_y, box_x, box_y)]

def post_layout(loc_ids, per_source, rest_rows):
    source = loc_ids // per_source
    remain = loc_ids % per_source
    rest_x = remain // rest_rows
    rest_y = remain % rest_rows
    src_group = source // 16
    src_digits = source % 16
    low_digit = src_digits % 4
    high_digit = src_digits // 4
    middle_x = 4 * src_group + 2 * (low_digit % 2) + high_digit % 2
    middle_y = 2 * (low_digit // 2) + high_digit // 2
    return (middle_x, middle_y, rest_x, rest_y)

def second_geometry(step_id, middle_x, middle_y, column, rest_y, other_digit, grid_shape):
    if step_id == 0:
        parent_x = middle_x
        parent_y = middle_y
        box_x = 2 * column + other_digit % 2
        box_y = 2 * rest_y + other_digit // 2
    else:
        parent_x = 2 * middle_x + other_digit % 2
        parent_y = 2 * middle_y + other_digit // 2
        box_x = column
        box_y = rest_y
    return [jnp.broadcast_to(jnp.asarray(entry_value), grid_shape).astype(jnp.float32) for entry_value in (parent_x, parent_y, box_x, box_y)]

def local_levels(block_state, group_grid, other_grid, loc_grid, tables, offset_x, offset_y, first_level, across):
    node_count = block_state.shape[1]
    outer_count = block_state.shape[2]
    inner_count = block_state.shape[5]
    for step_id in range(2):
        mix_axis = 4 - step_id
        child_slabs = [lax.index_in_dim(block_state, child_id, mix_axis, keepdims=False).reshape(2, node_count, -1) for child_id in range(4)]
        results = []
        for new_digit in range(4):
            if step_id == 0:
                geometry = first_geometry(step_id, group_grid, new_digit, other_grid, loc_grid, across)
            else:
                geometry = first_geometry(step_id, group_grid, other_grid, new_digit, loc_grid, across)
            pieces = [(child_slabs[child_id], 1.0 * (child_id % 2), 1.0 * (child_id // 2), tables[child_id]) for child_id in range(4)]
            fresh_state = freq_level(pieces, geometry[0], geometry[1], geometry[2], geometry[3], first_level + 1 + step_id, offset_x, offset_y)
            results.append(fresh_state.reshape(2, node_count, outer_count, 4, inner_count))
        block_state = jnp.stack(results, axis=mix_axis)
    return block_state

def reference(weights, owner_map, node_index):
    offset_x, offset_y = node_offsets(node_index)
    tables = child_tables(node_index)
    levels = NFREQ.bit_length() - 1
    first_level = levels // 2 - 2
    across = 2 ** (levels // 2)
    devices = N_GRP * N_DEV
    groups = devices // 16
    node_count = CHEB * CHEB
    per_dev = P_DEV
    per_source = per_dev // devices
    rest_rows = per_dev // across // 4
    group_width = across // 4 // groups
    grid_shape = (groups, 4, per_dev)
    high_grid = lax.broadcasted_iota(jnp.int32, grid_shape, 0).reshape(-1)
    other_grid = lax.broadcasted_iota(jnp.int32, grid_shape, 1).reshape(-1)
    loc_grid = lax.broadcasted_iota(jnp.int32, grid_shape, 2).reshape(-1)
    pair_state = weights.reshape(2, node_count, groups, 4, 4, per_dev)
    pair_state = local_levels(pair_state, high_grid, other_grid, loc_grid, tables, offset_x, offset_y, first_level, across)
    counter = jnp.arange(16, dtype=jnp.int32)
    inverse = lax.optimization_barrier(jnp.sum(jnp.where(owner_map[None, :] == counter[:, None], counter[None, :], 0), axis=1))
    blocks = pair_state.reshape(2, node_count, groups, 4, 4, rest_rows, 2, 2, 16, 2, 2)
    blocks = jnp.transpose(blocks, (0, 1, 8, 6, 9, 7, 10, 2, 3, 4, 5))
    blocks = jnp.take(blocks, inverse, axis=2)
    blocks = blocks.reshape(2, node_count, groups, group_width, 2, 2, 2, 2, groups, 4, 4, rest_rows)
    blocks = jnp.transpose(blocks, (0, 1, 2, 4, 5, 6, 7, 8, 9, 10, 3, 11))
    pair_state = blocks.reshape(2, node_count, groups, 4, 4, per_dev)
    middle_x, middle_y, rest_x, rest_y = post_layout(loc_grid, per_source, rest_rows)
    column = jnp.take(inverse, high_grid * group_width + rest_x)
    for step_id in range(2):
        mix_axis = 4 - step_id
        level_id = first_level + 3 + step_id
        child_slabs = [lax.index_in_dim(pair_state, child_id, mix_axis, keepdims=False) for child_id in range(4)]
        summed = child_slabs[0] + child_slabs[1] + (child_slabs[2] + child_slabs[3])
        geometry = second_geometry(step_id, middle_x, middle_y, column, rest_y, other_grid, loc_grid.shape)
        turned_in = space_in(summed.reshape(2, node_count, -1), offset_x, offset_y, geometry[0], geometry[1], geometry[2], geometry[3], level_id)
        results = []
        for new_digit in range(4):
            fresh_state = space_out(turned_in, tables[new_digit], offset_x, offset_y, geometry[0], geometry[1], 1.0 * (new_digit % 2), 1.0 * (new_digit // 2), geometry[2], geometry[3], level_id)
            results.append(fresh_state.reshape(2, node_count, groups, 4, per_dev))
        pair_state = jnp.stack(results, axis=mix_axis)
    return pair_state.reshape(2, node_count, devices * per_dev)
```

```python
import functools
import math

import jax
import jax.numpy as jnp
import numpy as np
from jax import lax
from jax.experimental import pallas as pl
from jax.experimental.pallas import tpu as pltpu
from jax.sharding import PartitionSpec as P

F32 = jnp.float32
BF16 = jnp.bfloat16
HALF = 2048.0
NT_DIMS = (((1,), (1,)), ((), ()))
TN_DIMS = (((0,), (0,)), ((), ()))
NN_DIMS = (((1,), (0,)), ((), ()))


def fit(function, count):
    angle = (np.arange(64) + 0.5) * np.pi / 64
    points = 0.125 + 0.125 * np.cos(angle)
    cheb = np.polynomial.chebyshev.Chebyshev.fit(
        points, function(np.sqrt(points)), count - 1, domain=[0.0, 0.25]
    )
    return [float(c) for c in cheb.convert(kind=np.polynomial.Polynomial).coef]


SIN_COEF = fit(lambda r: np.sin(np.pi * r) / r, 5)
COS_COEF = fit(lambda r: 2.0 * np.cos(np.pi * r), 6)


def horner(coef, u):
    total = coef[-1] * u + coef[-2]
    for c in coef[-3::-1]:
        total = total * u + c
    return total


def trig(cycles):
    r = cycles - jnp.round(cycles)
    u = r * r
    s = horner(SIN_COEF, u) * r
    c2 = horner(COS_COEF, u)
    return 1.0 - 2.0 * (s * s), s * c2


def cheb_nodes():
    return 0.5 * np.cos(np.pi * (2.0 * np.arange(8) + 1.0) / 16.0)


def canon_tables():
    z = cheb_nodes()
    basis = np.zeros((2, 8, 8))
    for c in range(2):
        places = z / 2 + c / 2 - 0.25
        for i in range(8):
            value = np.ones(8)
            for k in range(8):
                if k != i:
                    value = value * (places - z[k]) / (z[i] - z[k])
            basis[c, i] = value
    return [np.kron(basis[c % 2], basis[c // 2]) for c in range(4)]


def split_np(a):
    hi = np.asarray(a, np.float32).astype(BF16)
    lo = (np.asarray(a, np.float64) - hi.astype(np.float64)).astype(np.float32).astype(BF16)
    return hi, lo


def constants():
    z = cheb_nodes().astype(np.float32)
    tables = canon_tables()
    t_in = np.concatenate(tables, axis=1)
    t_out = np.concatenate([t.T for t in tables], axis=0)
    in_h, in_l = split_np(t_in)
    out_h, out_l = split_np(t_out)
    t1 = np.concatenate([in_h, in_l], axis=0)
    t3 = np.concatenate([out_h, out_h, out_l], axis=1)
    tf = np.stack([out_h, out_l])
    ox = np.repeat(z, 8)
    oy = np.tile(z, 8)
    off = np.stack([np.broadcast_to(o[:, None], (64, 128)) for o in (ox, oy)])
    pieces = []
    rest = off.astype(np.float32)
    for _ in range(3):
        piece = rest.astype(BF16)
        pieces.append(piece)
        rest = rest - piece.astype(np.float32)
    return t1, t3, tf, np.ascontiguousarray(off, np.float32), np.stack(pieces)


def fiota(shape, axis):
    return lax.broadcasted_iota(jnp.int32, shape, axis)


def node_onehot(node_ref):
    flat = node_ref[0:1, :] * 8 + node_ref[1:2, :]
    return (fiota((64, 64), 0) == flat).astype(F32).astype(BF16)


def dot(a, b, dims=NN_DIMS):
    return lax.dot_general(a, b, dims, preferred_element_type=F32)


def split(x):
    hi = x.astype(BF16)
    return hi, (x - hi.astype(F32)).astype(BF16)


def speeds(x1, x2):
    c1, s1 = trig(x1)
    c2, s2 = trig(x2)
    one = (2.0 + s1 * s2) * 0.0625
    two = (2.0 + c1 * c2) * 0.0625
    return one * one, two * two


def freq_cycles(d1, d2, g1, g2, a1, a2, v1, v2):
    numer = v1 * d1 * (2.0 * g1 + d1) + v2 * d2 * (2.0 * g2 + d2)
    square = v1 * g1 * g1 + v2 * g2 * g2 + 1.0
    denom = jnp.sqrt(square + numer) + jnp.sqrt(square)
    return a1 * d1 + a2 * d2 + numer / denom


def space_cycles(d1, d2, p1, p2, v1, v2, w1, w2, f1, f2):
    q1 = f1 * f1
    q2 = f2 * f2
    base = w1 * q1 + w2 * q2 + 1.0
    numer = (v1 - w1) * q1 + (v2 - w2) * q2
    denom = jnp.sqrt(v1 * q1 + v2 * q2 + 1.0) + jnp.sqrt(base)
    return d1 * f1 + d2 * f2 + numer / denom


ROWS = 32
BLOCKS = [(r, l) for l in range(0, 256, 128) for r in range(0, 64, ROWS)]


def bit(value, place):
    return lax.rem(lax.div(value, 1 << place), 2)


def tofloat(value):
    return value.astype(F32)


def mid_kernel(grp, node_ref, owner_ref, x_ref, t1_ref, t3_ref, off_ref, off3_ref, z_ref,
               tab1, tab2, tabm, tab3i, tab3o, tab4i, doff, t1s, xh, xl, y1, y2, wmat, x3, v4):
    flat = lax.axis_index("grp") * lax.axis_size("dev") + lax.axis_index("dev")
    h = lax.div(flat, 16)
    ry = lax.rem(flat, 16)
    hf = tofloat(h)
    ryf = tofloat(ry)

    onehot = node_onehot(node_ref)
    for axis in range(2):
        doff[axis] = sum(dot(onehot, off3_ref[p, axis], TN_DIMS) for p in (2, 1, 0))
    for c in range(4):
        t1s[:, c * 64:(c + 1) * 64] = dot(t1_ref[:, c * 64:(c + 1) * 64], onehot).astype(BF16)

    lane = [fiota((1, 128), 1) + k for k in (0, 128)]
    bx = [tofloat(lax.rem(v, 64)) for v in lane]
    by = [4.0 * ryf + tofloat(lax.div(v, 64)) for v in lane]

    def save(tab, index, cycles, rows, lanes):
        cs, sn = trig(cycles)
        tab[index, 0, rows, lanes] = cs
        tab[index, 1, rows, lanes] = sn

    def level1(i, carry):
        c = lax.rem(i, 4)
        u2 = lax.rem(lax.div(i, 4), 4)
        u1 = lax.div(i, 16)
        a1 = (2.0 * hf + tofloat(bit(u1, 0)) + 0.5) / 32.0
        a2 = (tofloat(bit(u1, 1)) + 0.5) / 32.0
        v1, v2 = speeds(jnp.full((1, 128), a1, F32), jnp.full((1, 128), a2, F32))
        sx = 16.0 * (tofloat(bit(c, 0)) - 0.5)
        sy = 16.0 * (tofloat(bit(c, 1)) - 0.5)
        for r, l in BLOCKS:
            rows = slice(r, r + ROWS)
            k = l // 128
            g1 = 32.0 * (2.0 * bx[k] + tofloat(bit(u2, 0)) + 0.5) - HALF
            g2 = 32.0 * (2.0 * by[k] + tofloat(bit(u2, 1)) + 0.5) - HALF
            cycles = freq_cycles(sx + 16.0 * doff[0, rows], sy + 16.0 * doff[1, rows],
                                 g1, g2, a1, a2, v1, v2)
            save(tab1, i, -cycles, rows, slice(l, l + 128))
        return carry

    lax.fori_loop(0, 64, level1, 0)

    def level2(i, carry):
        u2 = lax.rem(i, 4)
        c = lax.rem(lax.div(i, 4), 4)
        u1 = lax.div(i, 16)
        a1 = (2.0 * hf + tofloat(bit(u1, 0)) + 0.5) / 32.0
        a2 = (tofloat(bit(u1, 1)) + 0.5) / 32.0
        v1, v2 = speeds(jnp.full((1, 128), a1, F32), jnp.full((1, 128), a2, F32))
        b1 = (4.0 * hf + 2.0 * tofloat(bit(u1, 0)) + tofloat(bit(u2, 0)) + 0.5) / 64.0
        b2 = (2.0 * tofloat(bit(u1, 1)) + tofloat(bit(u2, 1)) + 0.5) / 64.0
        w1, w2 = speeds(jnp.full((1, 128), b1, F32), jnp.full((1, 128), b2, F32))
        cx = tofloat(bit(c, 0))
        cy = tofloat(bit(c, 1))
        index = (u1 * 4 + u2) * 4 + c
        for r, l in BLOCKS:
            rows = slice(r, r + ROWS)
            k = l // 128
            d1 = 32.0 * off_ref[0, rows]
            d2 = 32.0 * off_ref[1, rows]
            out = freq_cycles(d1, d2, 32.0 * (2.0 * bx[k] + cx + 0.5) - HALF,
                              32.0 * (2.0 * by[k] + cy + 0.5) - HALF, a1, a2, v1, v2)
            inn = freq_cycles(d1 + 32.0 * (cx - 0.5), d2 + 32.0 * (cy - 0.5),
                              64.0 * (bx[k] + 0.5) - HALF, 64.0 * (by[k] + 0.5) - HALF,
                              b1, b2, w1, w2)
            save(tab2, index, out - inn, rows, slice(l, l + 128))
        return carry

    lax.fori_loop(0, 64, level2, 0)

    def middle(u, carry):
        u1 = lax.rem(u, 4)
        u2 = lax.div(u, 4)
        b1 = (4.0 * hf + 2.0 * tofloat(bit(u1, 0)) + tofloat(bit(u2, 0)) + 0.5) / 64.0
        b2 = (2.0 * tofloat(bit(u1, 1)) + tofloat(bit(u2, 1)) + 0.5) / 64.0
        w1, w2 = speeds(jnp.full((1, 128), b1, F32), jnp.full((1, 128), b2, F32))
        for r, l in BLOCKS:
            rows = slice(r, r + ROWS)
            k = l // 128
            out = freq_cycles(64.0 * off_ref[0, rows], 64.0 * off_ref[1, rows],
                              64.0 * (bx[k] + 0.5) - HALF, 64.0 * (by[k] + 0.5) - HALF,
                              b1, b2, w1, w2)
            save(tabm, u, out, rows, slice(l, l + 128))
        return carry

    lax.fori_loop(0, 16, middle, 0)

    n = fiota((1, 128), 1)
    nrow = fiota((128, 16), 0)
    slot = 2 * lax.div(nrow, 16) + lax.rem(nrow, 2)
    owner = (owner_ref[0:1, :] == slot).astype(F32).astype(BF16)
    numbers = fiota((8, 16), 1).astype(F32).astype(BF16)
    column = dot(numbers, owner, NT_DIMS)[0:1, :]
    erow = fiota((256, 16), 0)
    picks = (lax.rem(lax.div(erow, 4), 16) == fiota((256, 16), 1)).astype(F32).astype(BF16)
    wcol = dot(picks, owner, NT_DIMS)
    wlane = fiota((256, 128), 0)
    digit = lax.rem(lax.div(wlane, 2), 2) + 2 * lax.div(wlane, 128)
    wu = lax.rem(lax.div(fiota((256, 128), 1), 2), 8)
    for v2d in range(4):
        keep = jnp.where(digit == v2d, wcol, 0.0)

        def fill(u8, carry):
            wmat[pl.ds(u8 * 256, 256), v2d * 128:(v2d + 1) * 128] = jnp.where(
                wu == u8, keep, 0.0).astype(BF16)
            return carry

        lax.fori_loop(0, 8, fill, 0)

    u8 = lax.rem(lax.div(n, 2), 8)

    def parent(half):
        u = u8 + 8 * half
        u1 = lax.rem(u, 4)
        u2 = lax.div(u, 4)
        return (4.0 * hf + tofloat(2 * lax.rem(u1, 2) + lax.rem(u2, 2)),
                tofloat(2 * lax.div(u1, 2) + lax.div(u2, 2)))

    def level3(half, carry):
        mx, my = parent(half)
        p1 = (mx + 0.5) / 64.0
        p2 = (my + 0.5) / 64.0
        w1, w2 = speeds(p1, p2)
        for r in range(0, 64, ROWS):
            rows = slice(r, r + ROWS)
            d1 = off_ref[0, rows] / 64.0
            d2 = off_ref[1, rows] / 64.0
            s1, s2 = speeds(p1 + d1, p2 + d2)
            for v in range(4):
                f1 = 128.0 * (2.0 * column + (v % 2) + 0.5) - HALF
                f2 = 128.0 * (2.0 * ryf + (v // 2) + 0.5) - HALF
                cycles = space_cycles(d1, d2, p1, p2, s1, s2, w1, w2, f1, f2)
                save(tab3i, half * 4 + v, -cycles, rows, slice(0, 128))
        return carry

    lax.fori_loop(0, 2, level3, 0)

    def level4(i, carry):
        half = lax.div(i, 4)
        jx = tofloat(bit(lax.rem(i, 4), 0))
        jy = tofloat(bit(lax.rem(i, 4), 1))
        mx, my = parent(half)
        p1 = (mx + 0.5) / 64.0
        p2 = (my + 0.5) / 64.0
        w1, w2 = speeds(p1, p2)
        c1 = (2.0 * mx + jx + 0.5) / 128.0
        c2 = (2.0 * my + jy + 0.5) / 128.0
        z1, z2 = speeds(c1, c2)
        for r in range(0, 64, ROWS):
            rows = slice(r, r + ROWS)
            d1 = off_ref[0, rows] / 128.0
            d2 = off_ref[1, rows] / 128.0
            s1, s2 = speeds(c1 + d1, c2 + d2)
            e1 = d1 + (jx - 0.5) / 128.0
            e2 = d2 + (jy - 0.5) / 128.0
            for v in range(4):
                f1 = 128.0 * (2.0 * column + (v % 2) + 0.5) - HALF
                f2 = 128.0 * (2.0 * ryf + (v // 2) + 0.5) - HALF
                cycles = space_cycles(e1, e2, p1, p2, s1, s2, w1, w2, f1, f2)
                save(tab3o, i * 4 + v, cycles, rows, slice(0, 128))
            f1 = 256.0 * (column + 0.5) - HALF
            f2 = 256.0 * (ryf + 0.5) - HALF
            cycles = space_cycles(d1, d2, c1, c2, s1, s2, z1, z2, f1, f2)
            save(tab4i, i, -cycles, rows, slice(0, 128))
        return carry

    lax.fori_loop(0, 8, level4, 0)

    def turn(re, im, tab, index, rows, lanes):
        cs = tab[index, 0, rows, lanes]
        sn = tab[index, 1, rows, lanes]
        return re * cs - im * sn, re * sn + im * cs

    def turned(source, tab, base):
        for c in range(4):
            for r, l in BLOCKS:
                rows = slice(r, r + ROWS)
                re, im = source(c, rows, l)
                parts = turn(re, im, tab, base + c, rows, slice(l, l + 128))
                for p in range(2):
                    hi, lo = split(parts[p])
                    at = slice(c * 64 + r, c * 64 + r + ROWS)
                    to = slice(p * 256 + l, p * 256 + l + 128)
                    xh[at, to] = hi
                    xl[at, to] = lo

    def mixed(table):
        first = dot(table[...], xh[...])
        return first[:64] + first[64:] + dot(table[0:64], xl[...])

    def run1(i, carry):
        u2 = lax.rem(i, 4)
        u1 = lax.div(i, 4)

        def source(c, rows, l):
            lanes = slice(l, l + 128)
            return x_ref[u2 * 4 + c, 0, rows, lanes], x_ref[u2 * 4 + c, 1, rows, lanes]

        turned(source, tab1, (u1 * 4 + u2) * 4)
        y1[u1 * 4 + u2] = mixed(t1s)
        return carry

    lax.fori_loop(0, 16, run1, 0)

    def run2(i, carry):
        u = i
        u1 = lax.rem(u, 4)
        u2 = lax.div(u, 4)

        def source(c, rows, l):
            return (y1[u1 * 4 + c, rows, l:l + 128], y1[u1 * 4 + c, rows, 256 + l:384 + l])

        turned(source, tab2, (u1 * 4 + u2) * 4)
        out = mixed(t1_ref)
        at = pl.multiple_of(lax.rem(u, 8) * 256, 256)
        half = lax.div(u, 8)
        for r, l in BLOCKS:
            rows = slice(r, r + ROWS)
            parts = turn(out[rows, l:l + 128], out[rows, 256 + l:384 + l], tabm, u, rows,
                         slice(l, l + 128))
            for p in range(2):
                hi, lo = split(parts[p])
                y2[half, p * 64 + r:p * 64 + r + ROWS, pl.ds(at + l, 128)] = hi
                y2[half, 128 + p * 64 + r:128 + p * 64 + r + ROWS, pl.ds(at + l, 128)] = lo
        return carry

    lax.fori_loop(0, 16, run2, 0)

    def run3(half, carry):
        both = dot(y2[half], wmat[...])
        summed = both[:128] + both[128:]
        for v in range(4):
            for r in range(0, 64, ROWS):
                rows = slice(r, r + ROWS)
                l = v * 128
                parts = turn(summed[r:r + ROWS, l:l + 128],
                             summed[64 + r:64 + r + ROWS, l:l + 128], tab3i, half * 4 + v, rows,
                             slice(0, 128))
                for p in range(2):
                    hi, lo = split(parts[p])
                    to = slice((v * 2 + p) * 128, (v * 2 + p + 1) * 128)
                    x3[r:r + ROWS, to] = hi
                    x3[64 + r:64 + r + ROWS, to] = lo
                    x3[128 + r:128 + r + ROWS, to] = hi
        for j in range(4):
            out = dot(t3_ref[j * 64:(j + 1) * 64], x3[...])
            for r in range(0, 64, ROWS):
                rows = slice(r, r + ROWS)
                re = None
                for v in range(4):
                    l = v * 256
                    a, b = turn(out[rows, l:l + 128], out[rows, l + 128:l + 256], tab3o,
                                (half * 4 + j) * 4 + v, rows, slice(0, 128))
                    re = a if re is None else re + a
                    im = b if v == 0 else im + b
                re, im = turn(re, im, tab4i, half * 4 + j, rows, slice(0, 128))
                v4[r:r + ROWS] = re
                v4[64 + r:64 + r + ROWS] = im
            flipped = v4[...].T
            for k in range(8):
                z_ref[k, j, pl.ds(pl.multiple_of(half * 16, 16), 16), :] = flipped[k * 16:(k + 1) * 16]
        return carry

    lax.fori_loop(0, 2, run3, 0)


def last_kernel(node_ref, owner_ref, y_ref, tf_ref, off3_ref, o_ref, doff, tmat, yy):
    flat = lax.axis_index("grp") * lax.axis_size("dev") + lax.axis_index("dev")
    own = lax.rem(flat, 16)
    group = lax.div(flat, 16)
    v1 = lax.rem(own, 4)
    v2 = lax.div(own, 4)
    onehot = node_onehot(node_ref)
    for axis in range(2):
        doff[axis] = sum(dot(onehot, off3_ref[p, axis], TN_DIMS) for p in (2, 1, 0))
    zero = jnp.zeros((64, 64), BF16)
    at = pl.multiple_of(v2 * 64, 64)
    parts = [dot(onehot, tf_ref[p, pl.ds(at, 64), :], TN_DIMS).astype(BF16) for p in range(2)]
    for p in range(2):
        for q in range(2):
            for part in range(2):
                for src in range(2):
                    lanes = slice(src * 128 + q * 64, src * 128 + q * 64 + 64)
                    rows = slice(part * 128 + p * 64, part * 128 + p * 64 + 64)
                    use = p == q and not (part == 1 and src == 1)
                    tmat[rows, lanes] = parts[part] if use else zero
    slot_row = 2 * group + fiota((128, 16), 0) // 64 * 0
    ids = fiota((512, 16), 0)
    slot = 2 * group + lax.rem(lax.div(ids, 16), 2)
    owner = (owner_ref[0:1, :] == slot).astype(F32).astype(BF16)
    numbers = fiota((8, 16), 1).astype(F32).astype(BF16)
    column = dot(numbers, owner, NT_DIMS)[0:1, :]
    jx, jy = tofloat(lax.rem(v2, 2)), tofloat(lax.div(v2, 2))
    vx, vy = tofloat(lax.rem(v1, 2)), tofloat(lax.div(v1, 2))

    def run(h, carry):
        for part in range(16):
            block = y_ref[h * 16 + part]
            hi, lo = split(block)
            del hi, lo
            yy[pl.ds(part, 32, stride=16), :] = block
        hi, lo = split(yy[...])
        both = jnp.concatenate([hi, lo], axis=1)
        out = dot(tmat[...], both, NT_DIMS)
        out = out[:128] + out[128:]
        for l in range(0, 512, 128):
            n = fiota((1, 128), 1) + l
            u = lax.div(n, 32)
            u1 = lax.rem(u, 4)
            u2 = lax.div(u, 4)
            mx = 4.0 * tofloat(h) + tofloat(2 * lax.rem(u1, 2) + lax.rem(u2, 2))
            my = tofloat(2 * lax.div(u1, 2) + lax.div(u2, 2))
            c1 = (2.0 * mx + vx + 0.5) / 128.0
            c2 = (2.0 * my + vy + 0.5) / 128.0
            w1, w2 = speeds(c1, c2)
            f1 = 256.0 * (column[:, l:l + 128] + 0.5) - HALF
            f2 = 256.0 * (tofloat(lax.rem(n, 16)) + 0.5) - HALF
            for r in range(0, 64, ROWS):
                d1 = doff[0, r:r + ROWS] / 256.0 + (jx - 0.5) / 256.0
                d2 = doff[1, r:r + ROWS] / 256.0 + (jy - 0.5) / 256.0
                s1, s2 = speeds(c1 + d1, c2 + d2)
                cs, sn = trig(space_cycles(d1, d2, c1, c2, s1, s2, w1, w2, f1, f2))
                re = out[r:r + ROWS, l:l + 128]
                im = out[64 + r:64 + r + ROWS, l:l + 128]
                lanes = pl.ds(pl.multiple_of(h * 512 + l, 128), 128)
                o_ref[0, r:r + ROWS, lanes] = re * cs - im * sn
                o_ref[1, r:r + ROWS, lanes] = re * sn + im * cs
        return carry

    lax.fori_loop(0, 8, run, 0)


VMEM_LIMIT = 60 * 1024 * 1024


def body(weights, owner_map, node_index):
    t1, t3, tf, off, off3 = constants()
    owner = owner_map.reshape(1, 16)
    groups = [list(range(g * 16, g * 16 + 16)) for g in range(lax.axis_size("dev") // 16)]
    x = lax.all_to_all(weights.reshape(2, 64, 16, 256), "dev", 2, 0, axis_index_groups=groups)
    vmem = pl.BlockSpec(memory_space=pltpu.VMEM)
    z = pl.pallas_call(
        functools.partial(mid_kernel, 0),
        out_shape=jax.ShapeDtypeStruct((8, 4, 32, 128), F32),
        in_specs=[vmem] * 7,
        out_specs=vmem,
        scratch_shapes=[
            pltpu.VMEM((64, 2, 64, 256), F32),
            pltpu.VMEM((64, 2, 64, 256), F32),
            pltpu.VMEM((16, 2, 64, 256), F32),
            pltpu.VMEM((8, 2, 64, 128), F32),
            pltpu.VMEM((32, 2, 64, 128), F32),
            pltpu.VMEM((8, 2, 64, 128), F32),
            pltpu.VMEM((2, 64, 128), F32),
            pltpu.VMEM((128, 256), BF16),
            pltpu.VMEM((256, 512), BF16),
            pltpu.VMEM((256, 512), BF16),
            pltpu.VMEM((16, 64, 512), F32),
            pltpu.VMEM((2, 256, 2048), BF16),
            pltpu.VMEM((2048, 512), BF16),
            pltpu.VMEM((192, 1024), BF16),
            pltpu.VMEM((128, 128), F32),
        ],
        compiler_params=pltpu.CompilerParams(vmem_limit_bytes=VMEM_LIMIT),
        name="mid",
    )(node_index, owner, x, t1, t3, off, off3)
    z = jnp.broadcast_to(z[:, None], (8, 4, 4, 32, 128)).reshape(128, 32, 128)
    y = lax.all_to_all(z, ("grp", "dev"), 0, 0, tiled=True)
    return pl.pallas_call(
        last_kernel,
        out_shape=jax.ShapeDtypeStruct((2, 64, 4096), F32),
        in_specs=[vmem] * 5,
        out_specs=vmem,
        scratch_shapes=[
            pltpu.VMEM((2, 64, 128), F32),
            pltpu.VMEM((256, 256), BF16),
            pltpu.VMEM((512, 128), F32),
        ],
        compiler_params=pltpu.CompilerParams(vmem_limit_bytes=VMEM_LIMIT),
        name="last",
    )(node_index, owner, y, tf, off3)


def solution(mesh):
    in_specs = (P(None, None, ("grp", "dev")), P(), P())
    out_specs = P(None, None, ("grp", "dev"))
    return jax.shard_map(body, mesh=mesh, in_specs=in_specs, out_specs=out_specs, check_vma=False)
```

```python
import functools
import math

import jax
import jax.numpy as jnp
import numpy as np
from jax import lax
from jax.experimental import pallas as pl
from jax.experimental.pallas import tpu as pltpu
from jax.sharding import PartitionSpec as P

F32 = jnp.float32
BF16 = jnp.bfloat16
HALF = 2048.0
NT_DIMS = (((1,), (1,)), ((), ()))
TN_DIMS = (((0,), (0,)), ((), ()))
NN_DIMS = (((1,), (0,)), ((), ()))


def fit(function, count):
    angle = (np.arange(64) + 0.5) * np.pi / 64
    points = 0.125 + 0.125 * np.cos(angle)
    cheb = np.polynomial.chebyshev.Chebyshev.fit(
        points, function(np.sqrt(points)), count - 1, domain=[0.0, 0.25]
    )
    return [float(c) for c in cheb.convert(kind=np.polynomial.Polynomial).coef]


ROOT2 = math.sqrt(2.0)
SIN_COEF = fit(lambda r: ROOT2 * np.sin(np.pi * r) / r, 5)
COS_COEF = fit(lambda r: ROOT2 * np.cos(np.pi * r), 5)


def horner(coef, u):
    total = coef[-1] * u + coef[-2]
    for c in coef[-3::-1]:
        total = total * u + c
    return total


def trig(cycles):
    r = cycles - jnp.round(cycles)
    u = r * r
    s = horner(SIN_COEF, u) * r
    c = horner(COS_COEF, u)
    return 1.0 - s * s, s * c


def cheb_nodes():
    return 0.5 * np.cos(np.pi * (2.0 * np.arange(8) + 1.0) / 16.0)


def canon_tables():
    z = cheb_nodes()
    basis = np.zeros((2, 8, 8))
    for c in range(2):
        places = z / 2 + c / 2 - 0.25
        for i in range(8):
            value = np.ones(8)
            for k in range(8):
                if k != i:
                    value = value * (places - z[k]) / (z[i] - z[k])
            basis[c, i] = value
    return [np.kron(basis[c % 2], basis[c // 2]) for c in range(4)]


def split_np(a):
    hi = np.asarray(a, np.float32).astype(BF16)
    lo = (np.asarray(a, np.float64) - hi.astype(np.float64)).astype(np.float32).astype(BF16)
    return hi, lo


def constants():
    z = cheb_nodes().astype(np.float32)
    tables = canon_tables()
    t_in = np.concatenate(tables, axis=1)
    t_out = np.concatenate([t.T for t in tables], axis=0)
    in_h, in_l = split_np(t_in)
    out_h, out_l = split_np(t_out)
    t1 = np.concatenate([in_h, in_l], axis=0)
    t3 = np.concatenate([out_h, out_h, out_l], axis=1)
    tf = np.stack([out_h, out_l])
    ox = np.repeat(z, 8)
    oy = np.tile(z, 8)
    off = np.stack([np.broadcast_to(o[:, None], (64, 128)) for o in (ox, oy)])
    pieces = []
    rest = off.astype(np.float32)
    for _ in range(3):
        piece = rest.astype(BF16)
        pieces.append(piece)
        rest = rest - piece.astype(np.float32)
    return t1, t3, tf, np.ascontiguousarray(off, np.float32), np.stack(pieces)


def fiota(shape, axis):
    return lax.broadcasted_iota(jnp.int32, shape, axis)


def node_onehot(node_ref):
    flat = node_ref[0:1, :] * 8 + node_ref[1:2, :]
    return (fiota((64, 64), 0) == flat).astype(F32).astype(BF16)


def dot(a, b, dims=NN_DIMS):
    return lax.dot_general(a, b, dims, preferred_element_type=F32)


def split(x):
    hi = x.astype(BF16)
    return hi, (x - hi.astype(F32)).astype(BF16)


def from_sines(s1, c1, s2, c2):
    one = (2.0 + s1 * s2) * 0.0625
    two = (2.0 + c1 * c2) * 0.0625
    return one * one, two * two


def speeds(x1, x2):
    c1, s1 = trig(x1)
    c2, s2 = trig(x2)
    return from_sines(s1, c1, s2, c2)


def speeds_sum(row, col):
    sines = []
    for (ca, sa), (cb, sb) in zip(row, col):
        sines += [sa * cb + ca * sb, ca * cb - sa * sb]
    return from_sines(*sines)


def root(x):
    return x * lax.rsqrt(x)


def freq_columns(d1, d2, a1, a2, v1, v2):
    e1 = v1 * d1
    e2 = v2 * d2
    return 2.0 * e1, 2.0 * e2, e1 * d1 + e2 * d2, a1 * d1 + a2 * d2


def freq_row(g1, g2, v1, v2):
    square = v1 * g1 * g1 + v2 * g2 * g2 + 1.0
    return g1, g2, square, root(square)


def freq_cycles(columns, row):
    e1, e2, e0, linear = columns
    g1, g2, square, base = row
    numer = e1 * g1 + e2 * g2 + e0
    return linear + numer / (root(square + numer) + base)


def space_cycles(d1, d2, v1, v2, w1, w2, f1, f2):
    q1 = f1 * f1
    q2 = f2 * f2
    base = w1 * q1 + w2 * q2 + 1.0
    numer = (v1 - w1) * q1 + (v2 - w2) * q2
    return d1 * f1 + d2 * f2 + numer / (root(base + numer) + root(base))


ROWS = 32
BLOCKS = [(r, l) for l in range(0, 256, 128) for r in range(0, 64, ROWS)]
MESH = pl.DeviceIdType.MESH


def bit(value, place):
    return lax.rem(lax.div(value, 1 << place), 2)


def tofloat(value):
    return value.astype(F32)


def splat(value):
    return jnp.full((1, 128), value, F32)


def save(tab, index, cycles, rows, lanes):
    cs, sn = trig(cycles)
    tab[index, 0, rows, lanes] = cs
    tab[index, 1, rows, lanes] = sn


def turn(re, im, tab, index, rows, lanes):
    cs = tab[index, 0, rows, lanes]
    sn = tab[index, 1, rows, lanes]
    return re * cs - im * sn, re * sn + im * cs


def columns_of(owner_ref, slot):
    owner = (owner_ref[0:1, :] == slot).astype(F32).astype(BF16)
    numbers = fiota((8, 16), 1).astype(F32).astype(BF16)
    return dot(numbers, owner, NT_DIMS)[0:1, :], owner


def kernel(n_dev, n_all, node_ref, owner_ref, w_hbm, t1_hbm, t3_hbm, tf_hbm, off_hbm, off3_hbm,
           o_ref, x_ref, t1_ref, t3_ref, tf_ref, off_ref, off3_ref, z_ref, y_ref, tab1, tab2,
           tabm, tab3i, tab3o, tab4i, tabf, part, doff, t1s, xh, xl, y1, y2, wmat, x3, v4, tmat,
           yy, send1, recv1, send2, recv2, local):
    flat = lax.axis_index("grp") * n_dev + lax.axis_index("dev")
    h = lax.div(flat, 16)
    ry = lax.rem(flat, 16)
    hf = tofloat(h)
    ryf = tofloat(ry)

    def place(device):
        return lax.div(device, n_dev), lax.rem(device, n_dev)

    barrier = pltpu.get_barrier_semaphore()

    def greet(i, carry):
        pl.semaphore_signal(barrier, inc=1, device_id=place(lax.rem(flat + i, n_all)),
                            device_id_type=MESH)
        return carry

    lax.fori_loop(1, n_all, greet, 0)
    pl.semaphore_wait(barrier, n_all - 1)

    def chunk(m):
        return w_hbm.at[:, :, pl.ds(pl.multiple_of(m * 256, 256), 256)]

    def exchange1(i):
        m = lax.rem(ry + i, 16)
        return pltpu.make_async_remote_copy(
            src_ref=chunk(m), dst_ref=x_ref.at[ry], send_sem=send1.at[i], recv_sem=recv1.at[i],
            device_id=place(h * 16 + m), device_id_type=MESH)

    for i in range(1, 16):
        exchange1(i).start()
    own1 = pltpu.make_async_copy(chunk(ry), x_ref.at[ry], recv1.at[0])
    own1.start()
    loads = [pltpu.make_async_copy(a, b, local.at[i]) for i, (a, b) in enumerate(
        [(t1_hbm, t1_ref), (t3_hbm, t3_ref), (tf_hbm, tf_ref), (off_hbm, off_ref),
         (off3_hbm, off3_ref)])]
    for load in loads:
        load.start()
    for load in loads:
        load.wait()

    onehot = node_onehot(node_ref)
    for axis in range(2):
        doff[axis] = sum(dot(onehot, off3_ref[p, axis], TN_DIMS) for p in (2, 1, 0))
    for c in range(4):
        t1s[:, c * 64:(c + 1) * 64] = dot(t1_ref[:, c * 64:(c + 1) * 64], onehot).astype(BF16)

    lane = [fiota((1, 128), 1) + k for k in (0, 128)]
    bx = [tofloat(lax.rem(v, 64)) for v in lane]
    by = [4.0 * ryf + tofloat(lax.div(v, 64)) for v in lane]

    def level1(i, carry):
        c = lax.rem(i, 4)
        u1 = lax.div(i, 4)
        a1 = (2.0 * hf + tofloat(bit(u1, 0)) + 0.5) / 32.0
        a2 = (tofloat(bit(u1, 1)) + 0.5) / 32.0
        v1, v2 = speeds(splat(a1), splat(a2))
        sx = 16.0 * (tofloat(bit(c, 0)) - 0.5)
        sy = 16.0 * (tofloat(bit(c, 1)) - 0.5)
        cols = [freq_columns(sx + 16.0 * doff[0, r:r + ROWS], sy + 16.0 * doff[1, r:r + ROWS],
                             -a1, -a2, v1, v2) for r in range(0, 64, ROWS)]

        def inner(u2, carry):
            for l in range(0, 256, 128):
                k = l // 128
                row = freq_row(32.0 * (2.0 * bx[k] + tofloat(bit(u2, 0)) + 0.5) - HALF,
                               32.0 * (2.0 * by[k] + tofloat(bit(u2, 1)) + 0.5) - HALF, v1, v2)
                g1, g2, square, base = row
                for r in range(0, 64, ROWS):
                    e1, e2, e0, linear = cols[r // ROWS]
                    numer = e1 * g1 + e2 * g2 + e0
                    cycles = linear - numer / (root(square + numer) + base)
                    save(tab1, i * 4 + u2, cycles, slice(r, r + ROWS), slice(l, l + 128))
            return carry

        lax.fori_loop(0, 4, inner, 0)
        return carry

    lax.fori_loop(0, 16, level1, 0)

    def level2(i, carry):
        c = lax.rem(i, 4)
        u1 = lax.div(i, 4)
        a1 = (2.0 * hf + tofloat(bit(u1, 0)) + 0.5) / 32.0
        a2 = (tofloat(bit(u1, 1)) + 0.5) / 32.0
        v1, v2 = speeds(splat(a1), splat(a2))
        cx = tofloat(bit(c, 0))
        cy = tofloat(bit(c, 1))
        for l in range(0, 256, 128):
            k = l // 128
            row = freq_row(32.0 * (2.0 * bx[k] + cx + 0.5) - HALF,
                           32.0 * (2.0 * by[k] + cy + 0.5) - HALF, v1, v2)
            for r in range(0, 64, ROWS):
                cols = freq_columns(32.0 * off_ref[0, r:r + ROWS], 32.0 * off_ref[1, r:r + ROWS],
                                    a1, a2, v1, v2)
                part[r:r + ROWS, l:l + 128] = freq_cycles(cols, row)

        def inner(u2, carry):
            b1 = (4.0 * hf + 2.0 * tofloat(bit(u1, 0)) + tofloat(bit(u2, 0)) + 0.5) / 64.0
            b2 = (2.0 * tofloat(bit(u1, 1)) + tofloat(bit(u2, 1)) + 0.5) / 64.0
            w1, w2 = speeds(splat(b1), splat(b2))
            rows = [freq_row(64.0 * (bx[k] + 0.5) - HALF, 64.0 * (by[k] + 0.5) - HALF, w1, w2)
                    for k in range(2)]
            for r in range(0, 64, ROWS):
                cols = freq_columns(32.0 * (off_ref[0, r:r + ROWS] + (cx - 0.5)),
                                    32.0 * (off_ref[1, r:r + ROWS] + (cy - 0.5)), b1, b2, w1, w2)
                for l in range(0, 256, 128):
                    cycles = part[r:r + ROWS, l:l + 128] - freq_cycles(cols, rows[l // 128])
                    save(tab2, i * 4 + u2, cycles, slice(r, r + ROWS), slice(l, l + 128))
            return carry

        lax.fori_loop(0, 4, inner, 0)
        return carry

    lax.fori_loop(0, 16, level2, 0)

    def middle(u, carry):
        u1 = lax.rem(u, 4)
        u2 = lax.div(u, 4)
        b1 = (4.0 * hf + 2.0 * tofloat(bit(u1, 0)) + tofloat(bit(u2, 0)) + 0.5) / 64.0
        b2 = (2.0 * tofloat(bit(u1, 1)) + tofloat(bit(u2, 1)) + 0.5) / 64.0
        w1, w2 = speeds(splat(b1), splat(b2))
        rows = [freq_row(64.0 * (bx[k] + 0.5) - HALF, 64.0 * (by[k] + 0.5) - HALF, w1, w2)
                for k in range(2)]
        for r in range(0, 64, ROWS):
            cols = freq_columns(64.0 * off_ref[0, r:r + ROWS], 64.0 * off_ref[1, r:r + ROWS],
                                b1, b2, w1, w2)
            for l in range(0, 256, 128):
                save(tabm, u, freq_cycles(cols, rows[l // 128]), slice(r, r + ROWS),
                     slice(l, l + 128))
        return carry

    lax.fori_loop(0, 16, middle, 0)

    n = fiota((1, 128), 1)
    nrow = fiota((128, 16), 0)
    column, owner = columns_of(owner_ref, 2 * lax.div(nrow, 16) + lax.rem(nrow, 2))
    erow = fiota((256, 16), 0)
    picks = (lax.rem(lax.div(erow, 4), 16) == fiota((256, 16), 1)).astype(F32).astype(BF16)
    wcol = dot(picks, owner, NT_DIMS)
    wlane = fiota((256, 128), 0)
    digit = lax.rem(lax.div(wlane, 2), 2) + 2 * lax.div(wlane, 128)
    wu = lax.rem(lax.div(fiota((256, 128), 1), 2), 8)
    for v2d in range(4):
        keep = jnp.where(digit == v2d, wcol, 0.0)

        def fill(u8, carry):
            wmat[pl.ds(pl.multiple_of(u8 * 256, 256), 256), v2d * 128:(v2d + 1) * 128] = jnp.where(
                wu == u8, keep, 0.0).astype(BF16)
            return carry

        lax.fori_loop(0, 8, fill, 0)

    u8 = lax.rem(lax.div(n, 2), 8)

    def parent(u):
        u1 = lax.rem(u, 4)
        u2 = lax.div(u, 4)
        return (tofloat(2 * lax.rem(u1, 2) + lax.rem(u2, 2)),
                tofloat(2 * lax.div(u1, 2) + lax.div(u2, 2)))

    def level3(half, carry):
        mx, my = parent(u8 + 8 * half)
        p1 = (4.0 * hf + mx + 0.5) / 64.0
        p2 = (my + 0.5) / 64.0
        row = (trig(p1), trig(p2))
        w1, w2 = from_sines(row[0][1], row[0][0], row[1][1], row[1][0])
        for r in range(0, 64, ROWS):
            rows = slice(r, r + ROWS)
            d1 = off_ref[0, rows] / 64.0
            d2 = off_ref[1, rows] / 64.0
            s1, s2 = speeds_sum(row, (trig(d1), trig(d2)))
            for v in range(4):
                f1 = 128.0 * (2.0 * column + (v % 2) + 0.5) - HALF
                f2 = 128.0 * (2.0 * ryf + (v // 2) + 0.5) - HALF
                cycles = space_cycles(d1, d2, s1, s2, w1, w2, f1, f2)
                save(tab3i, half * 4 + v, -cycles, rows, slice(0, 128))
        return carry

    lax.fori_loop(0, 2, level3, 0)

    def level4(i, carry):
        half = lax.div(i, 4)
        jx = tofloat(bit(lax.rem(i, 4), 0))
        jy = tofloat(bit(lax.rem(i, 4), 1))
        mx, my = parent(u8 + 8 * half)
        mx = 4.0 * hf + mx
        w1, w2 = speeds((mx + 0.5) / 64.0, (my + 0.5) / 64.0)
        c1 = (2.0 * mx + jx + 0.5) / 128.0
        c2 = (2.0 * my + jy + 0.5) / 128.0
        row = (trig(c1), trig(c2))
        z1, z2 = from_sines(row[0][1], row[0][0], row[1][1], row[1][0])
        for r in range(0, 64, ROWS):
            rows = slice(r, r + ROWS)
            d1 = off_ref[0, rows] / 128.0
            d2 = off_ref[1, rows] / 128.0
            s1, s2 = speeds_sum(row, (trig(d1), trig(d2)))
            e1 = d1 + (jx - 0.5) / 128.0
            e2 = d2 + (jy - 0.5) / 128.0
            for v in range(4):
                f1 = 128.0 * (2.0 * column + (v % 2) + 0.5) - HALF
                f2 = 128.0 * (2.0 * ryf + (v // 2) + 0.5) - HALF
                cycles = space_cycles(e1, e2, s1, s2, w1, w2, f1, f2)
                save(tab3o, i * 4 + v, cycles, rows, slice(0, 128))
            f1 = 256.0 * (column + 0.5) - HALF
            f2 = 256.0 * (ryf + 0.5) - HALF
            cycles = space_cycles(d1, d2, s1, s2, z1, z2, f1, f2)
            save(tab4i, i, -cycles, rows, slice(0, 128))
        return carry

    lax.fori_loop(0, 8, level4, 0)

    own1.wait()
    for i in range(1, 16):
        exchange1(i).wait()

    def turned(source, tab, index):
        for c in range(4):
            for r, l in BLOCKS:
                rows = slice(r, r + ROWS)
                re, im = source(c, rows, l)
                parts = turn(re, im, tab, index(c), rows, slice(l, l + 128))
                for p in range(2):
                    hi, lo = split(parts[p])
                    at = slice(c * 64 + r, c * 64 + r + ROWS)
                    to = slice(p * 256 + l, p * 256 + l + 128)
                    xh[at, to] = hi
                    xl[at, to] = lo

    def mixed(table):
        first = dot(table[...], xh[...])
        return first[:64] + first[64:] + dot(table[0:64], xl[...])

    def run1(i, carry):
        u2 = lax.rem(i, 4)
        u1 = lax.div(i, 4)

        def source(c, rows, l):
            lanes = slice(l, l + 128)
            return x_ref[u2 * 4 + c, 0, rows, lanes], x_ref[u2 * 4 + c, 1, rows, lanes]

        turned(source, tab1, lambda c: (u1 * 4 + c) * 4 + u2)
        y1[u1 * 4 + u2] = mixed(t1s)
        return carry

    lax.fori_loop(0, 16, run1, 0)

    def run2(u, carry):
        u1 = lax.rem(u, 4)
        u2 = lax.div(u, 4)

        def source(c, rows, l):
            return (y1[u1 * 4 + c, rows, l:l + 128], y1[u1 * 4 + c, rows, 256 + l:384 + l])

        turned(source, tab2, lambda c: (u1 * 4 + c) * 4 + u2)
        out = mixed(t1_ref)
        at = pl.multiple_of(lax.rem(u, 8) * 256, 256)
        half = lax.div(u, 8)
        for r, l in BLOCKS:
            rows = slice(r, r + ROWS)
            parts = turn(out[rows, l:l + 128], out[rows, 256 + l:384 + l], tabm, u, rows,
                         slice(l, l + 128))
            for p in range(2):
                hi, lo = split(parts[p])
                y2[half, p * 64 + r:p * 64 + r + ROWS, pl.ds(at + l, 128)] = hi
                y2[half, 128 + p * 64 + r:128 + p * 64 + r + ROWS, pl.ds(at + l, 128)] = lo
        return carry

    lax.fori_loop(0, 16, run2, 0)

    def run3(half, carry):
        both = dot(y2[half], wmat[...])
        summed = both[:128] + both[128:]
        for v in range(4):
            for r in range(0, 64, ROWS):
                rows = slice(r, r + ROWS)
                l = v * 128
                parts = turn(summed[r:r + ROWS, l:l + 128],
                             summed[64 + r:64 + r + ROWS, l:l + 128], tab3i, half * 4 + v, rows,
                             slice(0, 128))
                for p in range(2):
                    hi, lo = split(parts[p])
                    to = slice((v * 2 + p) * 128, (v * 2 + p + 1) * 128)
                    x3[r:r + ROWS, to] = hi
                    x3[64 + r:64 + r + ROWS, to] = lo
                    x3[128 + r:128 + r + ROWS, to] = hi
        for j in range(4):
            out = dot(t3_ref[j * 64:(j + 1) * 64], x3[...])
            for r in range(0, 64, ROWS):
                rows = slice(r, r + ROWS)
                re = None
                for v in range(4):
                    l = v * 256
                    a, b = turn(out[rows, l:l + 128], out[rows, l + 128:l + 256], tab3o,
                                (half * 4 + j) * 4 + v, rows, slice(0, 128))
                    re = a if re is None else re + a
                    im = b if v == 0 else im + b
                re, im = turn(re, im, tab4i, half * 4 + j, rows, slice(0, 128))
                v4[r:r + ROWS] = re
                v4[64 + r:64 + r + ROWS] = im
            flipped = v4[...].T
            for k in range(8):
                z_ref[k, j, pl.ds(pl.multiple_of(half * 16, 16), 16), :] = flipped[k * 16:(k + 1) * 16]
        return carry

    lax.fori_loop(0, 2, run3, 0)

    def exchange2(i):
        to = lax.rem(flat + i, n_all)
        return pltpu.make_async_remote_copy(
            src_ref=z_ref.at[lax.div(to, 16), lax.rem(to, 4)], dst_ref=y_ref.at[flat],
            send_sem=send2, recv_sem=recv2.at[h], device_id=place(to), device_id_type=MESH)

    def send(i, carry):
        exchange2(i).start()
        return carry

    lax.fori_loop(1, n_all, send, 0)
    own2 = pltpu.make_async_copy(z_ref.at[h, lax.rem(flat, 4)], y_ref.at[flat], recv2.at[h])
    own2.start()

    v1d = lax.rem(ry, 4)
    v2d = lax.div(ry, 4)
    zero = jnp.zeros((64, 64), BF16)
    pieces = [dot(onehot, tf_ref[p, pl.ds(pl.multiple_of(v2d * 64, 64), 64), :],
                  TN_DIMS).astype(BF16) for p in range(2)]
    for p in range(2):
        for q in range(2):
            for piece in range(2):
                for low in range(2):
                    lanes = slice(low * 128 + q * 64, low * 128 + q * 64 + 64)
                    rows = slice(piece * 128 + p * 64, piece * 128 + p * 64 + 64)
                    use = p == q and not (piece == 1 and low == 1)
                    tmat[rows, lanes] = pieces[piece] if use else zero
    ids = fiota((512, 16), 0)
    column, _ = columns_of(owner_ref, 2 * h + lax.rem(lax.div(ids, 16), 2))
    jx, jy = tofloat(lax.rem(v2d, 2)), tofloat(lax.div(v2d, 2))
    vx, vy = tofloat(lax.rem(v1d, 2)), tofloat(lax.div(v1d, 2))
    f2 = 256.0 * (tofloat(lax.rem(n, 16)) + 0.5) - HALF

    def level5(src, carry):
        for l in range(0, 512, 128):
            mx, my = parent(lax.div(n + l, 32))
            c1 = (2.0 * (4.0 * tofloat(src) + mx) + vx + 0.5) / 128.0
            c2 = (2.0 * my + vy + 0.5) / 128.0
            row = (trig(c1), trig(c2))
            w1, w2 = from_sines(row[0][1], row[0][0], row[1][1], row[1][0])
            f1 = 256.0 * (column[:, l:l + 128] + 0.5) - HALF
            for r in range(0, 64, ROWS):
                d1 = (doff[0, r:r + ROWS] + (jx - 0.5)) / 256.0
                d2 = (doff[1, r:r + ROWS] + (jy - 0.5)) / 256.0
                s1, s2 = speeds_sum(row, (trig(d1), trig(d2)))
                save(tabf, src, space_cycles(d1, d2, s1, s2, w1, w2, f1, f2),
                     slice(r, r + ROWS), slice(l, l + 128))
        return carry

    lax.fori_loop(0, 8, level5, 0)

    def run4(src, carry):
        landed = y_ref.at[pl.ds(pl.multiple_of(src * 16, 16), 16)]
        pltpu.make_async_copy(landed, landed, recv2.at[src]).wait()
        for m in range(16):
            yy[pl.ds(m, 32, stride=16), :] = y_ref[src * 16 + m]
        hi, lo = split(yy[...])
        out = dot(tmat[...], jnp.concatenate([hi, lo], axis=1), NT_DIMS)
        out = out[:128] + out[128:]
        for l in range(0, 512, 128):
            lanes = pl.ds(pl.multiple_of(src * 512 + l, 128), 128)
            for r in range(0, 64, ROWS):
                rows = slice(r, r + ROWS)
                re, im = turn(out[r:r + ROWS, l:l + 128], out[64 + r:64 + r + ROWS, l:l + 128],
                              tabf, src, rows, slice(l, l + 128))
                o_ref[0, rows, lanes] = re
                o_ref[1, rows, lanes] = im
        return carry

    lax.fori_loop(0, 8, run4, 0)
    sent = y_ref.at[pl.ds(0, n_all - 1)]
    pltpu.make_async_copy(sent, sent, send2).wait()


VMEM_LIMIT = 62 * 1024 * 1024


def body(weights, owner_map, node_index):
    t1, t3, tf, off, off3 = constants()
    n_dev = lax.axis_size("dev")
    n_all = lax.axis_size("grp") * n_dev
    vmem = pl.BlockSpec(memory_space=pltpu.VMEM)
    hbm = pl.BlockSpec(memory_space=pl.ANY)
    dma = pltpu.SemaphoreType.DMA
    return pl.pallas_call(
        functools.partial(kernel, n_dev, n_all),
        out_shape=jax.ShapeDtypeStruct((2, 64, 4096), F32),
        in_specs=[vmem] * 2 + [hbm] * 6,
        out_specs=vmem,
        scratch_shapes=[
            pltpu.VMEM((16, 2, 64, 256), F32),
            pltpu.VMEM(t1.shape, BF16),
            pltpu.VMEM(t3.shape, BF16),
            pltpu.VMEM(tf.shape, BF16),
            pltpu.VMEM(off.shape, F32),
            pltpu.VMEM(off3.shape, BF16),
            pltpu.VMEM((8, 4, 32, 128), F32),
            pltpu.VMEM((128, 32, 128), F32),
            pltpu.VMEM((64, 2, 64, 256), F32),
            pltpu.VMEM((64, 2, 64, 256), F32),
            pltpu.VMEM((16, 2, 64, 256), F32),
            pltpu.VMEM((8, 2, 64, 128), F32),
            pltpu.VMEM((32, 2, 64, 128), F32),
            pltpu.VMEM((8, 2, 64, 128), F32),
            pltpu.VMEM((8, 2, 64, 512), F32),
            pltpu.VMEM((64, 256), F32),
            pltpu.VMEM((2, 64, 128), F32),
            pltpu.VMEM((128, 256), BF16),
            pltpu.VMEM((256, 512), BF16),
            pltpu.VMEM((256, 512), BF16),
            pltpu.VMEM((16, 64, 512), F32),
            pltpu.VMEM((2, 256, 2048), BF16),
            pltpu.VMEM((2048, 512), BF16),
            pltpu.VMEM((192, 1024), BF16),
            pltpu.VMEM((128, 128), F32),
            pltpu.VMEM((256, 256), BF16),
            pltpu.VMEM((512, 128), F32),
            dma((16,)),
            dma((16,)),
            dma(()),
            dma((8,)),
            dma((5,)),
        ],
        compiler_params=pltpu.CompilerParams(
            vmem_limit_bytes=VMEM_LIMIT, collective_id=0, has_side_effects=True),
        name="butterfly",
    )(node_index, owner_map.reshape(1, 16), weights, t1, t3, tf, off, off3)


def solution(mesh):
    in_specs = (P(None, None, ("grp", "dev")), P(), P())
    out_specs = P(None, None, ("grp", "dev"))
    return jax.shard_map(body, mesh=mesh, in_specs=in_specs, out_specs=out_specs, check_vma=False)
```

```python
import functools
import math

import jax
import jax.numpy as jnp
import numpy as np
from jax import lax
from jax.experimental import pallas as pl
from jax.experimental.pallas import tpu as pltpu
from jax.sharding import PartitionSpec as P

F32 = jnp.float32
BF16 = jnp.bfloat16
HALF = 2048.0
NT_DIMS = (((1,), (1,)), ((), ()))
TN_DIMS = (((0,), (0,)), ((), ()))
NN_DIMS = (((1,), (0,)), ((), ()))


def fit(function, count):
    angle = (np.arange(64) + 0.5) * np.pi / 64
    points = 0.125 + 0.125 * np.cos(angle)
    cheb = np.polynomial.chebyshev.Chebyshev.fit(
        points, function(np.sqrt(points)), count - 1, domain=[0.0, 0.25]
    )
    return [float(c) for c in cheb.convert(kind=np.polynomial.Polynomial).coef]


ROOT2 = math.sqrt(2.0)
SIN_COEF = fit(lambda r: ROOT2 * np.sin(np.pi * r) / r, 5)
COS_COEF = fit(lambda r: ROOT2 * np.cos(np.pi * r), 5)


def horner(coef, u):
    total = coef[-1] * u + coef[-2]
    for c in coef[-3::-1]:
        total = total * u + c
    return total


def trig(cycles):
    r = cycles - jnp.round(cycles)
    u = r * r
    s = horner(SIN_COEF, u) * r
    c = horner(COS_COEF, u)
    return 1.0 - s * s, s * c


def cheb_nodes():
    return 0.5 * np.cos(np.pi * (2.0 * np.arange(8) + 1.0) / 16.0)


def canon_tables():
    z = cheb_nodes()
    basis = np.zeros((2, 8, 8))
    for c in range(2):
        places = z / 2 + c / 2 - 0.25
        for i in range(8):
            value = np.ones(8)
            for k in range(8):
                if k != i:
                    value = value * (places - z[k]) / (z[i] - z[k])
            basis[c, i] = value
    return [np.kron(basis[c % 2], basis[c // 2]) for c in range(4)]


def split_np(a):
    hi = np.asarray(a, np.float32).astype(BF16)
    lo = (np.asarray(a, np.float64) - hi.astype(np.float64)).astype(np.float32).astype(BF16)
    return hi, lo


def constants():
    z = cheb_nodes().astype(np.float32)
    tables = canon_tables()
    t_in = np.concatenate(tables, axis=1)
    t_out = np.concatenate([t.T for t in tables], axis=0)
    in_h, in_l = split_np(t_in)
    out_h, out_l = split_np(t_out)
    t1 = np.concatenate([in_h, in_l], axis=0)
    t3 = np.concatenate([out_h, out_h, out_l], axis=1)
    tf = np.stack([out_h, out_l])
    ox = np.repeat(z, 8)
    oy = np.tile(z, 8)
    off = np.stack([np.broadcast_to(o[:, None], (64, 128)) for o in (ox, oy)])
    pieces = []
    rest = off.astype(np.float32)
    for _ in range(3):
        piece = rest.astype(BF16)
        pieces.append(piece)
        rest = rest - piece.astype(np.float32)
    return t1, t3, tf, np.ascontiguousarray(off, np.float32), np.stack(pieces)


def fiota(shape, axis):
    return lax.broadcasted_iota(jnp.int32, shape, axis)


def node_onehot(node_ref):
    flat = node_ref[0:1, :] * 8 + node_ref[1:2, :]
    return (fiota((64, 64), 0) == flat).astype(F32).astype(BF16)


def dot(a, b, dims=NN_DIMS):
    return lax.dot_general(a, b, dims, preferred_element_type=F32)


def split(x):
    hi = x.astype(BF16)
    return hi, (x - hi.astype(F32)).astype(BF16)


def from_sines(s1, c1, s2, c2):
    one = (2.0 + s1 * s2) * 0.0625
    two = (2.0 + c1 * c2) * 0.0625
    return one * one, two * two


def speeds(x1, x2):
    c1, s1 = trig(x1)
    c2, s2 = trig(x2)
    return from_sines(s1, c1, s2, c2)


def speeds_sum(row, col):
    sines = []
    for (ca, sa), (cb, sb) in zip(row, col):
        sines += [sa * cb + ca * sb, ca * cb - sa * sb]
    return from_sines(*sines)


def root(x):
    return x * lax.rsqrt(x)


def freq_columns(d1, d2, a1, a2, v1, v2):
    e1 = v1 * d1
    e2 = v2 * d2
    return 2.0 * e1, 2.0 * e2, e1 * d1 + e2 * d2, a1 * d1 + a2 * d2


def freq_row(g1, g2, v1, v2):
    square = v1 * g1 * g1 + v2 * g2 * g2 + 1.0
    return g1, g2, square, root(square)


def freq_cycles(columns, row):
    e1, e2, e0, linear = columns
    g1, g2, square, base = row
    numer = e1 * g1 + e2 * g2 + e0
    return linear + numer / (root(square + numer) + base)


def space_cycles(d1, d2, v1, v2, w1, w2, f1, f2):
    q1 = f1 * f1
    q2 = f2 * f2
    base = w1 * q1 + w2 * q2 + 1.0
    numer = (v1 - w1) * q1 + (v2 - w2) * q2
    return d1 * f1 + d2 * f2 + numer / (root(base + numer) + root(base))


ROWS = 32
MESH = pl.DeviceIdType.MESH


def bit(value, place):
    return lax.rem(lax.div(value, 1 << place), 2)


def tofloat(value):
    return value.astype(F32)


def splat(value):
    return jnp.full((1, 128), value, F32)


def save(tab, index, cycles, rows, lanes):
    cs, sn = trig(cycles)
    tab[index, 0, rows, lanes] = cs
    tab[index, 1, rows, lanes] = sn


def turn(re, im, tab, index, rows, lanes):
    cs = tab[index, 0, rows, lanes]
    sn = tab[index, 1, rows, lanes]
    return re * cs - im * sn, re * sn + im * cs


def columns_of(owner_ref, slot):
    owner = (owner_ref[0:1, :] == slot).astype(F32).astype(BF16)
    numbers = fiota((8, 16), 1).astype(F32).astype(BF16)
    return dot(numbers, owner, NT_DIMS)[0:1, :], owner


def kernel(n_dev, n_all, n_group, node_ref, owner_ref, w_hbm, t1_hbm, t3_hbm, tf_hbm, off_hbm, off3_hbm,
           o_ref, x_ref, t1_ref, t3_ref, tf_ref, off_ref, off3_ref, z_ref, y_ref, tab1, tab2,
           tabm, tab3i, tab3o, tab4i, tabf, part, doff, t1s, xh, xl, y1, y2, wmat, x3, v4, tmat,
           yy, send1, recv1, send2, recv2, local, ready):
    flat = lax.axis_index("grp") * n_dev + lax.axis_index("dev")
    h = lax.div(flat, 16)
    ry = lax.rem(flat, 16)
    hf = tofloat(h)
    ryf = tofloat(ry)

    def place(device):
        return lax.div(device, n_dev), lax.rem(device, n_dev)

    barrier = pltpu.get_barrier_semaphore()

    def tell(semaphore, device):
        pl.semaphore_signal(semaphore, inc=1, device_id=place(device), device_id_type=MESH)

    for i in range(1, 16):
        tell(barrier, h * 16 + lax.rem(ry + i, 16))
    for g in range(1, n_group):
        tell(barrier, lax.rem(h + g, n_group) * 16 + ry)
    pl.semaphore_wait(barrier, 14 + n_group)
    for g in range(1, n_group):
        tell(ready, lax.rem(h + g, n_group) * 16 + ry)

    def chunk(m, b):
        return w_hbm.at[:, :, pl.ds(pl.multiple_of(m * 256 + b * 128, 128), 128)]

    def exchange1(b, i):
        m = (lax.rem(lax.div(ry, 8) + i // 8, 2) * 8
             + lax.rem(lax.div(lax.rem(ry, 8), 2) + i // 2 % 4, 4) * 2 + lax.rem(ry + i, 2))
        return pltpu.make_async_remote_copy(
            src_ref=chunk(m, b), dst_ref=x_ref.at[b, ry], send_sem=send1.at[b * 16 + i],
            recv_sem=recv1.at[b * 16 + i], device_id=place(h * 16 + m), device_id_type=MESH)

    for b in range(2):
        for i in range(1, 16):
            exchange1(b, i).start()
    own1 = [pltpu.make_async_copy(chunk(ry, b), x_ref.at[b, ry], recv1.at[b * 16])
            for b in range(2)]
    for copy in own1:
        copy.start()
    loads = [pltpu.make_async_copy(a, b, local.at[i]) for i, (a, b) in enumerate(
        [(t1_hbm, t1_ref), (t3_hbm, t3_ref), (tf_hbm, tf_ref), (off_hbm, off_ref),
         (off3_hbm, off3_ref)])]
    for load in loads:
        load.start()
    for load in loads:
        load.wait()

    onehot = node_onehot(node_ref)
    for axis in range(2):
        doff[axis] = sum(dot(onehot, off3_ref[p, axis], TN_DIMS) for p in (2, 1, 0))
    for c in range(4):
        t1s[:, c * 64:(c + 1) * 64] = dot(t1_ref[:, c * 64:(c + 1) * 64], onehot).astype(BF16)

    lane = [fiota((1, 128), 1) + k for k in (0, 128)]
    bx = [tofloat(lax.rem(v, 64)) for v in lane]
    by = [4.0 * ryf + tofloat(lax.div(v, 64)) for v in lane]

    def level1(i, carry):
        c = lax.rem(i, 4)
        u1 = lax.div(i, 4)
        a1 = (2.0 * hf + tofloat(bit(u1, 0)) + 0.5) / 32.0
        a2 = (tofloat(bit(u1, 1)) + 0.5) / 32.0
        v1, v2 = speeds(splat(a1), splat(a2))
        sx = 16.0 * (tofloat(bit(c, 0)) - 0.5)
        sy = 16.0 * (tofloat(bit(c, 1)) - 0.5)
        cols = [freq_columns(sx + 16.0 * doff[0, r:r + ROWS], sy + 16.0 * doff[1, r:r + ROWS],
                             -a1, -a2, v1, v2) for r in range(0, 64, ROWS)]

        def inner(u2, carry):
            for l in range(0, 256, 128):
                k = l // 128
                row = freq_row(32.0 * (2.0 * bx[k] + tofloat(bit(u2, 0)) + 0.5) - HALF,
                               32.0 * (2.0 * by[k] + tofloat(bit(u2, 1)) + 0.5) - HALF, v1, v2)
                g1, g2, square, base = row
                for r in range(0, 64, ROWS):
                    e1, e2, e0, linear = cols[r // ROWS]
                    numer = e1 * g1 + e2 * g2 + e0
                    cycles = linear - numer / (root(square + numer) + base)
                    save(tab1, i * 4 + u2, cycles, slice(r, r + ROWS), slice(l, l + 128))
            return carry

        lax.fori_loop(0, 4, inner, 0)
        return carry

    lax.fori_loop(0, 16, level1, 0)

    def level2(i, carry):
        c = lax.rem(i, 4)
        u1 = lax.div(i, 4)
        a1 = (2.0 * hf + tofloat(bit(u1, 0)) + 0.5) / 32.0
        a2 = (tofloat(bit(u1, 1)) + 0.5) / 32.0
        v1, v2 = speeds(splat(a1), splat(a2))
        cx = tofloat(bit(c, 0))
        cy = tofloat(bit(c, 1))
        for l in range(0, 256, 128):
            k = l // 128
            row = freq_row(32.0 * (2.0 * bx[k] + cx + 0.5) - HALF,
                           32.0 * (2.0 * by[k] + cy + 0.5) - HALF, v1, v2)
            for r in range(0, 64, ROWS):
                cols = freq_columns(32.0 * off_ref[0, r:r + ROWS], 32.0 * off_ref[1, r:r + ROWS],
                                    a1, a2, v1, v2)
                part[r:r + ROWS, l:l + 128] = freq_cycles(cols, row)

        def inner(u2, carry):
            b1 = (4.0 * hf + 2.0 * tofloat(bit(u1, 0)) + tofloat(bit(u2, 0)) + 0.5) / 64.0
            b2 = (2.0 * tofloat(bit(u1, 1)) + tofloat(bit(u2, 1)) + 0.5) / 64.0
            w1, w2 = speeds(splat(b1), splat(b2))
            rows = [freq_row(64.0 * (bx[k] + 0.5) - HALF, 64.0 * (by[k] + 0.5) - HALF, w1, w2)
                    for k in range(2)]
            for r in range(0, 64, ROWS):
                cols = freq_columns(32.0 * (off_ref[0, r:r + ROWS] + (cx - 0.5)),
                                    32.0 * (off_ref[1, r:r + ROWS] + (cy - 0.5)), b1, b2, w1, w2)
                for l in range(0, 256, 128):
                    cycles = part[r:r + ROWS, l:l + 128] - freq_cycles(cols, rows[l // 128])
                    save(tab2, i * 4 + u2, cycles, slice(r, r + ROWS), slice(l, l + 128))
            return carry

        lax.fori_loop(0, 4, inner, 0)
        return carry

    lax.fori_loop(0, 16, level2, 0)

    def middle(u, carry):
        u1 = lax.rem(u, 4)
        u2 = lax.div(u, 4)
        b1 = (4.0 * hf + 2.0 * tofloat(bit(u1, 0)) + tofloat(bit(u2, 0)) + 0.5) / 64.0
        b2 = (2.0 * tofloat(bit(u1, 1)) + tofloat(bit(u2, 1)) + 0.5) / 64.0
        w1, w2 = speeds(splat(b1), splat(b2))
        rows = [freq_row(64.0 * (bx[k] + 0.5) - HALF, 64.0 * (by[k] + 0.5) - HALF, w1, w2)
                for k in range(2)]
        for r in range(0, 64, ROWS):
            cols = freq_columns(64.0 * off_ref[0, r:r + ROWS], 64.0 * off_ref[1, r:r + ROWS],
                                b1, b2, w1, w2)
            for l in range(0, 256, 128):
                save(tabm, u, freq_cycles(cols, rows[l // 128]), slice(r, r + ROWS),
                     slice(l, l + 128))
        return carry

    lax.fori_loop(0, 16, middle, 0)

    n = fiota((1, 128), 1)
    nrow = fiota((128, 16), 0)
    column, owner = columns_of(owner_ref, 2 * lax.div(nrow, 16) + lax.rem(nrow, 2))
    erow = fiota((128, 16), 0)
    picks = (lax.rem(lax.div(erow, 4), 16) == fiota((128, 16), 1)).astype(F32).astype(BF16)
    wcol = dot(picks, owner, NT_DIMS)
    wu = lax.rem(lax.div(fiota((128, 128), 1), 2), 8)
    for v in range(2):
        keep = jnp.where(lax.rem(lax.div(fiota((128, 128), 0), 2), 2) == v, wcol, 0.0)
        for u in range(8):
            wmat[u * 128:(u + 1) * 128, v * 128:(v + 1) * 128] = jnp.where(
                wu == u, keep, 0.0).astype(BF16)

    u8 = lax.rem(lax.div(n, 2), 8)

    def parent(u):
        u1 = lax.rem(u, 4)
        u2 = lax.div(u, 4)
        return (tofloat(2 * lax.rem(u1, 2) + lax.rem(u2, 2)),
                tofloat(2 * lax.div(u1, 2) + lax.div(u2, 2)))

    def level3(half, carry):
        mx, my = parent(u8 + 8 * half)
        p1 = (4.0 * hf + mx + 0.5) / 64.0
        p2 = (my + 0.5) / 64.0
        row = (trig(p1), trig(p2))
        w1, w2 = from_sines(row[0][1], row[0][0], row[1][1], row[1][0])
        for r in range(0, 64, ROWS):
            rows = slice(r, r + ROWS)
            d1 = off_ref[0, rows] / 64.0
            d2 = off_ref[1, rows] / 64.0
            s1, s2 = speeds_sum(row, (trig(d1), trig(d2)))
            for v in range(4):
                f1 = 128.0 * (2.0 * column + (v % 2) + 0.5) - HALF
                f2 = 128.0 * (2.0 * ryf + (v // 2) + 0.5) - HALF
                cycles = space_cycles(d1, d2, s1, s2, w1, w2, f1, f2)
                save(tab3i, half * 4 + v, -cycles, rows, slice(0, 128))
        return carry

    lax.fori_loop(0, 2, level3, 0)

    def level4(i, carry):
        half = lax.div(i, 4)
        jx = tofloat(bit(lax.rem(i, 4), 0))
        jy = tofloat(bit(lax.rem(i, 4), 1))
        mx, my = parent(u8 + 8 * half)
        mx = 4.0 * hf + mx
        w1, w2 = speeds((mx + 0.5) / 64.0, (my + 0.5) / 64.0)
        c1 = (2.0 * mx + jx + 0.5) / 128.0
        c2 = (2.0 * my + jy + 0.5) / 128.0
        row = (trig(c1), trig(c2))
        z1, z2 = from_sines(row[0][1], row[0][0], row[1][1], row[1][0])
        for r in range(0, 64, ROWS):
            rows = slice(r, r + ROWS)
            d1 = off_ref[0, rows] / 128.0
            d2 = off_ref[1, rows] / 128.0
            s1, s2 = speeds_sum(row, (trig(d1), trig(d2)))
            e1 = d1 + (jx - 0.5) / 128.0
            e2 = d2 + (jy - 0.5) / 128.0
            for v in range(4):
                f1 = 128.0 * (2.0 * column + (v % 2) + 0.5) - HALF
                f2 = 128.0 * (2.0 * ryf + (v // 2) + 0.5) - HALF
                cycles = space_cycles(e1, e2, s1, s2, w1, w2, f1, f2)
                save(tab3o, i * 4 + v, cycles, rows, slice(0, 128))
            f1 = 256.0 * (column + 0.5) - HALF
            f2 = 256.0 * (ryf + 0.5) - HALF
            cycles = space_cycles(d1, d2, s1, s2, z1, z2, f1, f2)
            save(tab4i, i, -cycles, rows, slice(0, 128))
        return carry

    lax.fori_loop(0, 8, level4, 0)

    y0 = 2 * lax.rem(lax.div(flat, n_all // 4), 2) + lax.div(flat, n_all // 2)
    x0 = lax.rem(lax.div(flat, 8), 4)
    z0 = lax.rem(lax.div(flat, 2), 4)
    c0 = lax.rem(flat, 2)

    def send_half(half):
        for odd in (1, 0):

            def send(e, carry):
                dz = lax.rem(e, 4)
                dx = lax.rem(lax.div(e, 4) + dz, 4)
                dy = 2 * lax.rem(lax.div(e, 16), 2) + odd
                yy0 = lax.rem(y0 + dy, 4)
                v = (lax.rem(x0 + dx, 4) * 8 + lax.rem(z0 + dz, 4) * 2
                     + lax.rem(c0 + lax.div(e, 32), 2))
                to = lax.rem(yy0, 2) * 64 + lax.div(yy0, 2) * 32 + v
                pltpu.make_async_remote_copy(
                    src_ref=z_ref.at[half, lax.div(to, 16), lax.rem(v, 4)],
                    dst_ref=y_ref.at[flat, half], send_sem=send2, recv_sem=recv2.at[h],
                    device_id=place(to), device_id_type=MESH).start()
                return carry

            lax.fori_loop(1 - odd, 64, send, 0)
        pltpu.make_async_copy(z_ref.at[half, h, lax.rem(flat, 4)], y_ref.at[flat, half],
                              recv2.at[h]).start()

    def stage(b):
        at = slice(b * 128, b * 128 + 128)
        whole = slice(0, 128)

        def turned(slot, source, tab, index):
            for c in range(4):
                for r in range(0, 64, ROWS):
                    rows = slice(r, r + ROWS)
                    re, im = source(c, rows)
                    parts = turn(re, im, tab, index(c), rows, at)
                    for p in range(2):
                        hi, lo = split(parts[p])
                        xh[slot, c * 64 + r:c * 64 + r + ROWS, p * 128:p * 128 + 128] = hi
                        xl[slot, c * 64 + r:c * 64 + r + ROWS, p * 128:p * 128 + 128] = lo

        def mixed(slot, table):
            first = dot(table[...], xh[slot])
            return first[:64] + first[64:] + dot(table[0:64], xl[slot])

        def run1(u2, carry):
            for u1 in range(4):
                turned(u1, lambda c, rows: (x_ref[b, u2 * 4 + c, 0, rows],
                                            x_ref[b, u2 * 4 + c, 1, rows]),
                       tab1, lambda c: (u1 * 4 + c) * 4 + u2)
                y1[u1 * 4 + u2] = mixed(u1, t1s)
            return carry

        lax.fori_loop(0, 4, run1, 0)

        def run2(half, pair):
            for slot in range(4):
                u1 = 2 * pair + slot // 2
                u2 = 2 * half + slot % 2
                u = u1 + 4 * u2
                turned(slot, lambda c, rows: (y1[u1 * 4 + c, rows, 0:128],
                                              y1[u1 * 4 + c, rows, 128:256]),
                       tab2, lambda c: (u1 * 4 + c) * 4 + u2)
                out = mixed(slot, t1_ref)
                to = pl.ds(pl.multiple_of((u1 + 4 * (slot % 2)) * 128, 128), 128)
                for r in range(0, 64, ROWS):
                    rows = slice(r, r + ROWS)
                    parts = turn(out[rows, 0:128], out[rows, 128:256], tabm, u, rows, at)
                    for p in range(2):
                        hi, lo = split(parts[p])
                        y2[p * 64 + r:p * 64 + r + ROWS, to] = hi
                        y2[128 + p * 64 + r:128 + p * 64 + r + ROWS, to] = lo

        def run3(half):
            both = dot(y2[...], wmat[...])
            summed = both[:128] + both[128:]
            for v in range(2):
                for r in range(0, 64, ROWS):
                    rows = slice(r, r + ROWS)
                    l = v * 128
                    parts = turn(summed[r:r + ROWS, l:l + 128],
                                 summed[64 + r:64 + r + ROWS, l:l + 128], tab3i,
                                 half * 4 + 2 * b + v, rows, whole)
                    for p in range(2):
                        hi, lo = split(parts[p])
                        to = slice((v * 2 + p) * 128, (v * 2 + p + 1) * 128)
                        x3[r:r + ROWS, to] = hi
                        x3[64 + r:64 + r + ROWS, to] = lo
                        x3[128 + r:128 + r + ROWS, to] = hi
            for j in range(4):
                out = dot(t3_ref[j * 64:(j + 1) * 64], x3[...])
                for r in range(0, 64, ROWS):
                    rows = slice(r, r + ROWS)
                    low = slice(64 + r, 64 + r + ROWS)
                    if b == 1:
                        re, im = v4[half * 4 + j, rows], v4[half * 4 + j, low]
                    for v in range(2):
                        l = v * 256
                        p, q = turn(out[rows, l:l + 128], out[rows, l + 128:l + 256], tab3o,
                                    (half * 4 + j) * 4 + 2 * b + v, rows, whole)
                        first = b == 0 and v == 0
                        re = p if first else re + p
                        im = q if first else im + q
                    if b == 1:
                        re, im = turn(re, im, tab4i, half * 4 + j, rows, whole)
                    v4[half * 4 + j, rows] = re
                    v4[half * 4 + j, low] = im
                if b == 1:
                    flipped = v4[half * 4 + j].T
                    for k in range(8):
                        z_ref[half, k, j] = flipped[k * 16:(k + 1) * 16]

        def run(half, carry):
            def pairs(pair, carry):
                run2(half, pair)
                return carry

            lax.fori_loop(0, 2, pairs, 0)
            run3(half)
            if b == 1:
                send_half(half)
            return carry

        lax.fori_loop(0, 2, run, 0)

    for b in range(2):
        own1[b].wait()
        for i in range(1, 16):
            exchange1(b, i).wait()
        if b == 1:
            pl.semaphore_wait(ready, n_group - 1)
        stage(b)

    v1d = lax.rem(ry, 4)
    v2d = lax.div(ry, 4)
    zero = jnp.zeros((64, 64), BF16)
    pieces = [dot(onehot, tf_ref[p, pl.ds(pl.multiple_of(v2d * 64, 64), 64), :],
                  TN_DIMS).astype(BF16) for p in range(2)]
    for p in range(2):
        for q in range(2):
            for piece in range(2):
                for low in range(2):
                    lanes = slice(low * 128 + q * 64, low * 128 + q * 64 + 64)
                    rows = slice(piece * 128 + p * 64, piece * 128 + p * 64 + 64)
                    use = p == q and not (piece == 1 and low == 1)
                    tmat[rows, lanes] = pieces[piece] if use else zero
    ids = fiota((512, 16), 0)
    column, _ = columns_of(owner_ref, 2 * h + lax.rem(lax.div(ids, 16), 2))
    jx, jy = tofloat(lax.rem(v2d, 2)), tofloat(lax.div(v2d, 2))
    vx, vy = tofloat(lax.rem(v1d, 2)), tofloat(lax.div(v1d, 2))
    f2 = 256.0 * (tofloat(lax.rem(n, 16)) + 0.5) - HALF

    def level5(src, carry):
        for l in range(0, 512, 128):
            mx, my = parent(lax.div(n + l, 32))
            c1 = (2.0 * (4.0 * tofloat(src) + mx) + vx + 0.5) / 128.0
            c2 = (2.0 * my + vy + 0.5) / 128.0
            row = (trig(c1), trig(c2))
            w1, w2 = from_sines(row[0][1], row[0][0], row[1][1], row[1][0])
            f1 = 256.0 * (column[:, l:l + 128] + 0.5) - HALF
            for r in range(0, 64, ROWS):
                d1 = (doff[0, r:r + ROWS] + (jx - 0.5)) / 256.0
                d2 = (doff[1, r:r + ROWS] + (jy - 0.5)) / 256.0
                s1, s2 = speeds_sum(row, (trig(d1), trig(d2)))
                save(tabf, src, space_cycles(d1, d2, s1, s2, w1, w2, f1, f2),
                     slice(r, r + ROWS), slice(l, l + 128))
        return carry

    lax.fori_loop(0, 8, level5, 0)

    def run4(e, carry):
        src = lax.rem(lax.div(h, 4) + 1 + lax.div(e, 4), 2) * 4 + lax.rem(h + e, 4)
        landed = y_ref.at[pl.ds(pl.multiple_of(src * 16, 16), 16)]
        pltpu.make_async_copy(landed, landed, recv2.at[src]).wait()
        for m in range(16):
            yy[pl.ds(m, 32, stride=16), :] = y_ref[src * 16 + m].reshape(32, 128)
        hi, lo = split(yy[...])
        out = dot(tmat[...], jnp.concatenate([hi, lo], axis=1), NT_DIMS)
        out = out[:128] + out[128:]
        for l in range(0, 512, 128):
            lanes = pl.ds(pl.multiple_of(src * 512 + l, 128), 128)
            for r in range(0, 64, ROWS):
                rows = slice(r, r + ROWS)
                re, im = turn(out[r:r + ROWS, l:l + 128], out[64 + r:64 + r + ROWS, l:l + 128],
                              tabf, src, rows, slice(l, l + 128))
                o_ref[0, rows, lanes] = re
                o_ref[1, rows, lanes] = im
        return carry

    lax.fori_loop(0, 8, run4, 0)
    sent = y_ref.at[pl.ds(0, n_all - 1)]
    pltpu.make_async_copy(sent, sent, send2).wait()


VMEM_LIMIT = 62 * 1024 * 1024


def body(weights, owner_map, node_index):
    t1, t3, tf, off, off3 = constants()
    n_dev = lax.axis_size("dev")
    n_all = lax.axis_size("grp") * n_dev
    vmem = pl.BlockSpec(memory_space=pltpu.VMEM)
    hbm = pl.BlockSpec(memory_space=pl.ANY)
    dma = pltpu.SemaphoreType.DMA
    return pl.pallas_call(
        functools.partial(kernel, n_dev, n_all, n_all // 16),
        out_shape=jax.ShapeDtypeStruct((2, 64, 4096), F32),
        in_specs=[vmem] * 2 + [hbm] * 6,
        out_specs=vmem,
        scratch_shapes=[
            pltpu.VMEM((2, 16, 2, 64, 128), F32),
            pltpu.VMEM(t1.shape, BF16),
            pltpu.VMEM(t3.shape, BF16),
            pltpu.VMEM(tf.shape, BF16),
            pltpu.VMEM(off.shape, F32),
            pltpu.VMEM(off3.shape, BF16),
            pltpu.VMEM((2, 8, 4, 16, 128), F32),
            pltpu.VMEM((128, 2, 16, 128), F32),
            pltpu.VMEM((64, 2, 64, 256), F32),
            pltpu.VMEM((64, 2, 64, 256), F32),
            pltpu.VMEM((16, 2, 64, 256), F32),
            pltpu.VMEM((8, 2, 64, 128), F32),
            pltpu.VMEM((32, 2, 64, 128), F32),
            pltpu.VMEM((8, 2, 64, 128), F32),
            pltpu.VMEM((8, 2, 64, 512), F32),
            pltpu.VMEM((64, 256), F32),
            pltpu.VMEM((2, 64, 128), F32),
            pltpu.VMEM((128, 256), BF16),
            pltpu.VMEM((4, 256, 256), BF16),
            pltpu.VMEM((4, 256, 256), BF16),
            pltpu.VMEM((16, 64, 256), F32),
            pltpu.VMEM((256, 1024), BF16),
            pltpu.VMEM((1024, 256), BF16),
            pltpu.VMEM((192, 512), BF16),
            pltpu.VMEM((8, 128, 128), F32),
            pltpu.VMEM((256, 256), BF16),
            pltpu.VMEM((512, 128), F32),
            dma((32,)),
            dma((32,)),
            dma(()),
            dma((8,)),
            dma((5,)),
            pltpu.SemaphoreType.REGULAR,
        ],
        compiler_params=pltpu.CompilerParams(
            vmem_limit_bytes=VMEM_LIMIT, collective_id=0, has_side_effects=True),
        name="butterfly",
    )(node_index, owner_map.reshape(1, 16), weights, t1, t3, tf, off, off3)


def solution(mesh):
    in_specs = (P(None, None, ("grp", "dev")), P(), P())
    out_specs = P(None, None, ("grp", "dev"))
    return jax.shard_map(body, mesh=mesh, in_specs=in_specs, out_specs=out_specs, check_vma=False)
```

```python
import functools
import math

import jax
import jax.numpy as jnp
import numpy as np
from jax import lax
from jax.experimental import pallas as pl
from jax.experimental.pallas import tpu as pltpu
from jax.sharding import PartitionSpec as P

F32 = jnp.float32
BF16 = jnp.bfloat16
HALF = 2048.0
NT_DIMS = (((1,), (1,)), ((), ()))
TN_DIMS = (((0,), (0,)), ((), ()))
NN_DIMS = (((1,), (0,)), ((), ()))


def fit(function, count):
    angle = (np.arange(64) + 0.5) * np.pi / 64
    points = 0.125 + 0.125 * np.cos(angle)
    cheb = np.polynomial.chebyshev.Chebyshev.fit(
        points, function(np.sqrt(points)), count - 1, domain=[0.0, 0.25]
    )
    return [float(c) for c in cheb.convert(kind=np.polynomial.Polynomial).coef]


ROOT2 = math.sqrt(2.0)
SIN_COEF = fit(lambda r: ROOT2 * np.sin(np.pi * r) / r, 5)
COS_COEF = fit(lambda r: ROOT2 * np.cos(np.pi * r), 5)


def horner(coef, u):
    total = coef[-1] * u + coef[-2]
    for c in coef[-3::-1]:
        total = total * u + c
    return total


def trig(cycles):
    r = cycles - jnp.round(cycles)
    u = r * r
    s = horner(SIN_COEF, u) * r
    c = horner(COS_COEF, u)
    return 1.0 - s * s, s * c


def cheb_nodes():
    return 0.5 * np.cos(np.pi * (2.0 * np.arange(8) + 1.0) / 16.0)


def canon_tables():
    z = cheb_nodes()
    basis = np.zeros((2, 8, 8))
    for c in range(2):
        places = z / 2 + c / 2 - 0.25
        for i in range(8):
            value = np.ones(8)
            for k in range(8):
                if k != i:
                    value = value * (places - z[k]) / (z[i] - z[k])
            basis[c, i] = value
    return [np.kron(basis[c % 2], basis[c // 2]) for c in range(4)]


def split_np(a):
    hi = np.asarray(a, np.float32).astype(BF16)
    lo = (np.asarray(a, np.float64) - hi.astype(np.float64)).astype(np.float32).astype(BF16)
    return hi, lo


def constants():
    z = cheb_nodes().astype(np.float32)
    tables = canon_tables()
    t_in = np.concatenate(tables, axis=1)
    t_out = np.concatenate([t.T for t in tables], axis=0)
    in_h, in_l = split_np(t_in)
    out_h, out_l = split_np(t_out)
    t1 = np.concatenate([in_h, in_l], axis=0)
    t3 = np.concatenate([out_h, out_h, out_l], axis=1)
    tf = np.stack([out_h, out_l])
    ox = np.repeat(z, 8)
    oy = np.tile(z, 8)
    off = np.stack([np.broadcast_to(o[:, None], (64, 128)) for o in (ox, oy)])
    pieces = []
    rest = off.astype(np.float32)
    for _ in range(3):
        piece = rest.astype(BF16)
        pieces.append(piece)
        rest = rest - piece.astype(np.float32)
    return t1, t3, tf, np.ascontiguousarray(off, np.float32), np.stack(pieces)


def fiota(shape, axis):
    return lax.broadcasted_iota(jnp.int32, shape, axis)


def node_onehot(node_ref):
    flat = node_ref[0:1, :] * 8 + node_ref[1:2, :]
    return (fiota((64, 64), 0) == flat).astype(F32).astype(BF16)


def dot(a, b, dims=NN_DIMS):
    return lax.dot_general(a, b, dims, preferred_element_type=F32)


def split(x):
    hi = x.astype(BF16)
    return hi, (x - hi.astype(F32)).astype(BF16)


def from_sines(s1, c1, s2, c2):
    one = (2.0 + s1 * s2) * 0.0625
    two = (2.0 + c1 * c2) * 0.0625
    return one * one, two * two


def speeds(x1, x2):
    c1, s1 = trig(x1)
    c2, s2 = trig(x2)
    return from_sines(s1, c1, s2, c2)


def speeds_sum(row, col):
    sines = []
    for (ca, sa), (cb, sb) in zip(row, col):
        sines += [sa * cb + ca * sb, ca * cb - sa * sb]
    return from_sines(*sines)


def root(x):
    return x * lax.rsqrt(x)


def freq_columns(d1, d2, a1, a2, v1, v2):
    e1 = v1 * d1
    e2 = v2 * d2
    linear = a2 * d2 if isinstance(a1, float) and a1 == 0.0 else a1 * d1 + a2 * d2
    return 2.0 * e1, 2.0 * e2, e1 * d1 + e2 * d2, linear


def freq_row(g1, g2, v1, v2):
    square = v1 * g1 * g1 + v2 * g2 * g2 + 1.0
    return g1, g2, square, root(square)


def freq_cycles(columns, row):
    e1, e2, e0, linear = columns
    g1, g2, square, base = row
    numer = e1 * g1 + e2 * g2 + e0
    return linear + numer / (root(square + numer) + base)


def space_cycles(d1, d2, v1, v2, w1, w2, f1, f2):
    q1 = f1 * f1
    q2 = f2 * f2
    base = w1 * q1 + w2 * q2 + 1.0
    numer = (v1 - w1) * q1 + (v2 - w2) * q2
    return d1 * f1 + d2 * f2 + numer / (root(base + numer) + root(base))


ROWS = 32
MESH = pl.DeviceIdType.MESH


def bit(value, place):
    return lax.rem(lax.div(value, 1 << place), 2)


def tofloat(value):
    return value.astype(F32)


def splat(value):
    return jnp.full((1, 128), value, F32)


def save(tab, index, cycles, rows, lanes):
    cs, sn = trig(cycles)
    tab[index, 0, rows, lanes] = cs
    tab[index, 1, rows, lanes] = sn


def turn(re, im, tab, index, rows, lanes):
    cs = tab[index, 0, rows, lanes]
    sn = tab[index, 1, rows, lanes]
    return re * cs - im * sn, re * sn + im * cs


def columns_of(owner_ref, slot):
    owner = (owner_ref[0:1, :] == slot).astype(F32).astype(BF16)
    numbers = fiota((8, 16), 1).astype(F32).astype(BF16)
    return dot(numbers, owner, NT_DIMS)[0:1, :], owner


def kernel(n_dev, n_all, n_group, node_ref, owner_ref, w_hbm, t1_hbm, t3_hbm, tf_hbm, off_hbm, off3_hbm,
           o_ref, x_ref, t1_ref, t3_ref, tf_ref, off_ref, off3_ref, z_ref, y_ref, tab1, tab2,
           tabm, tab3i, tab3o, tab4i, tabf, lin2, line, prod, part, doff, t1s, xh, xl, y1, y2, wmat, x3, v4, tmat,
           yy, send1, recv1, send2, recv2, local, ready):
    flat = lax.axis_index("grp") * n_dev + lax.axis_index("dev")
    h = lax.div(flat, 16)
    ry = lax.rem(flat, 16)
    hf = tofloat(h)
    ryf = tofloat(ry)

    def place(device):
        return lax.div(device, n_dev), lax.rem(device, n_dev)

    barrier = pltpu.get_barrier_semaphore()

    def tell(semaphore, device):
        pl.semaphore_signal(semaphore, inc=1, device_id=place(device), device_id_type=MESH)

    for i in range(1, 16):
        tell(barrier, h * 16 + lax.rem(ry + i, 16))
    for g in range(1, n_group):
        tell(barrier, lax.rem(h + g, n_group) * 16 + ry)
    pl.semaphore_wait(barrier, 14 + n_group)
    for g in range(1, n_group):
        tell(ready, lax.rem(h + g, n_group) * 16 + ry)

    def chunk(m, b):
        return w_hbm.at[:, :, pl.ds(pl.multiple_of(m * 256 + b * 128, 128), 128)]

    def exchange1(b, i):
        m = (lax.rem(lax.div(ry, 8) + i // 8, 2) * 8
             + lax.rem(lax.div(lax.rem(ry, 8), 2) + i // 2 % 4, 4) * 2 + lax.rem(ry + i, 2))
        return pltpu.make_async_remote_copy(
            src_ref=chunk(m, b), dst_ref=x_ref.at[b, ry], send_sem=send1.at[b * 16 + i],
            recv_sem=recv1.at[b * 16 + i], device_id=place(h * 16 + m), device_id_type=MESH)

    for b in range(2):
        for i in range(1, 16):
            exchange1(b, i).start()
    own1 = [pltpu.make_async_copy(chunk(ry, b), x_ref.at[b, ry], recv1.at[b * 16])
            for b in range(2)]
    for copy in own1:
        copy.start()
    loads = [pltpu.make_async_copy(a, b, local.at[i]) for i, (a, b) in enumerate(
        [(t1_hbm, t1_ref), (t3_hbm, t3_ref), (tf_hbm, tf_ref), (off_hbm, off_ref),
         (off3_hbm, off3_ref)])]
    for load in loads:
        load.start()
    for load in loads:
        load.wait()

    onehot = node_onehot(node_ref)
    for axis in range(2):
        doff[axis] = sum(dot(onehot, off3_ref[p, axis], TN_DIMS) for p in (2, 1, 0))
    for c in range(4):
        t1s[:, c * 64:(c + 1) * 64] = dot(t1_ref[:, c * 64:(c + 1) * 64], onehot).astype(BF16)

    lane = [fiota((1, 128), 1) + k for k in (0, 128)]
    bx = [tofloat(lax.rem(v, 64)) for v in lane]
    by = [4.0 * ryf + tofloat(lax.div(v, 64)) for v in lane]

    def products(index, offsets, scale, shift, width, child):
        for l in range(0, 256, 128):
            for axis, at in ((0, bx[l // 128]), (1, by[l // 128])):
                g = width * at + child - HALF
                for r in range(0, 64, ROWS):
                    d = scale * offsets[axis, r:r + ROWS] + shift
                    prod[axis, index, r:r + ROWS, l:l + 128] = d * (2.0 * g + d)

    def products1(i, carry):
        child = tofloat(lax.div(i, 2))
        products(i, doff, 16.0, 16.0 * (child - 0.5), 64.0, 32.0 * (tofloat(lax.rem(i, 2)) + 0.5))
        return carry

    def products2(i, carry):
        products(4 + i, off_ref, 32.0, 32.0 * (tofloat(i) - 0.5), 64.0, 32.0)
        products(6 + i, off_ref, 32.0, 0.0, 64.0, 32.0 * (tofloat(i) + 0.5))
        return carry

    lax.fori_loop(0, 4, products1, 0)

    def freq_rest(row, ix, iy, v1, v2, rows, lanes):
        square, base = row
        numer = v1 * prod[0, ix, rows, lanes] + v2 * prod[1, iy, rows, lanes]
        return numer / (root(square + numer) + base)

    def level1(i, carry):
        c = lax.rem(i, 4)
        u1 = lax.div(i, 4)
        a1 = (2.0 * hf + tofloat(bit(u1, 0)) + 0.5) / 32.0
        a2 = (tofloat(bit(u1, 1)) + 0.5) / 32.0
        v1, v2 = speeds(splat(a1), splat(a2))
        sx = 16.0 * (tofloat(bit(c, 0)) - 0.5)
        sy = 16.0 * (tofloat(bit(c, 1)) - 0.5)
        for r in range(0, 64, ROWS):
            line[r:r + ROWS] = -(a1 * (sx + 16.0 * doff[0, r:r + ROWS])
                                 + a2 * (sy + 16.0 * doff[1, r:r + ROWS]))

        def inner(u2, carry):
            for l in range(0, 256, 128):
                k = l // 128
                row = freq_row(32.0 * (2.0 * bx[k] + tofloat(bit(u2, 0)) + 0.5) - HALF,
                               32.0 * (2.0 * by[k] + tofloat(bit(u2, 1)) + 0.5) - HALF, v1, v2)
                for r in range(0, 64, ROWS):
                    rows = slice(r, r + ROWS)
                    lanes = slice(l, l + 128)
                    rest = freq_rest(row[2:], 2 * bit(c, 0) + bit(u2, 0),
                                     2 * bit(c, 1) + bit(u2, 1), v1, v2, rows, lanes)
                    save(tab1, i * 4 + u2, line[rows] - rest, rows, lanes)
            return carry

        lax.fori_loop(0, 4, inner, 0, unroll=2)
        return carry

    lax.fori_loop(0, 16, level1, 0)

    lax.fori_loop(0, 2, products2, 0)
    def linear2(i, carry):
        ux = tofloat(lax.div(i, 2))
        a1 = (2.0 * hf + ux + 0.5) / 32.0
        b1 = (4.0 * hf + 2.0 * ux + tofloat(lax.rem(i, 2)) + 0.5) / 64.0
        for r in range(0, 64, ROWS):
            rows = slice(r, r + ROWS)
            o = off_ref[0, rows]
            save(lin2, i, 32.0 * (a1 * o - b1 * (o - 0.5)), rows, slice(0, 128))
        return carry

    lax.fori_loop(0, 4, linear2, 0)

    mirror = fiota((ROWS, 128), 1)
    mirror = lax.div(mirror, 64) * 64 + 63 - lax.rem(mirror, 64)

    def mirrored(tab, index, other, cycles, lin, which, r, lanes):
        cs, sn = trig(cycles)
        cl = lin[which, 0, r:r + ROWS]
        sl = lin[which, 1, r:r + ROWS]
        p, q, s, t = cs * cl, sn * sl, sn * cl, cs * sl
        tab[index, 0, r:r + ROWS, lanes] = p - q
        tab[index, 1, r:r + ROWS, lanes] = s + t
        for part_id, value in enumerate((p + q, s - t)):
            value = jnp.take_along_axis(value, mirror, axis=1, mode="promise_in_bounds")
            for k in range(0, ROWS, 8):
                to = 56 - r - k
                tab[other, part_id, to:to + 8, lanes] = value[k:k + 8]

    def level2(i, carry):
        u1 = lax.div(i, 2)
        a1 = (2.0 * hf + tofloat(bit(u1, 0)) + 0.5) / 32.0
        a2 = (tofloat(bit(u1, 1)) + 0.5) / 32.0
        v1, v2 = speeds(splat(a1), splat(a2))
        cy = tofloat(lax.rem(i, 2))
        cyi = lax.rem(i, 2)
        for r in range(0, 64, ROWS):
            rows = slice(r, r + ROWS)
            for l in range(0, 256, 128):
                k = l // 128
                lanes = slice(l, l + 128)
                row = freq_row(32.0 * (2.0 * bx[k] + 0.5) - HALF,
                               32.0 * (2.0 * by[k] + cy + 0.5) - HALF, v1, v2)
                part[rows, lanes] = (a2 * (32.0 * off_ref[1, rows])
                                     + freq_rest(row[2:], 6, 6 + cyi, v1, v2, rows, lanes))
        index = (u1 * 4 + 2 * cyi) * 4

        def inner(u2, carry):
            b1 = (4.0 * hf + 2.0 * tofloat(bit(u1, 0)) + tofloat(bit(u2, 0)) + 0.5) / 64.0
            b2 = (2.0 * tofloat(bit(u1, 1)) + tofloat(bit(u2, 1)) + 0.5) / 64.0
            w1, w2 = speeds(splat(b1), splat(b2))
            for l in range(0, 256, 128):
                k = l // 128
                lanes = slice(l, l + 128)
                row = freq_row(64.0 * (bx[k] + 0.5) - HALF, 64.0 * (by[k] + 0.5) - HALF, w1, w2)
                for r in range(0, 64, ROWS):
                    rows = slice(r, r + ROWS)
                    rest = freq_rest(row[2:], 4, 4 + cyi, w1, w2, rows, lanes)
                    down = (b2 * 32.0) * (off_ref[1, rows] + (cy - 0.5))
                    mirrored(tab2, index + u2, index + 4 + u2, part[rows, lanes] - down - rest,
                             lin2, bit(u1, 0) * 2 + bit(u2, 0), r, lanes)
            return carry

        lax.fori_loop(0, 4, inner, 0, unroll=2)
        return carry

    lax.fori_loop(0, 8, level2, 0)

    def middle(u, carry):
        u1 = lax.rem(u, 4)
        u2 = lax.div(u, 4)
        b1 = (4.0 * hf + 2.0 * tofloat(bit(u1, 0)) + tofloat(bit(u2, 0)) + 0.5) / 64.0
        b2 = (2.0 * tofloat(bit(u1, 1)) + tofloat(bit(u2, 1)) + 0.5) / 64.0
        w1, w2 = speeds(splat(b1), splat(b2))
        rows = [freq_row(64.0 * (bx[k] + 0.5) - HALF, 64.0 * (by[k] + 0.5) - HALF, w1, w2)
                for k in range(2)]
        for r in range(0, 64, ROWS):
            cols = freq_columns(64.0 * off_ref[0, r:r + ROWS], 64.0 * off_ref[1, r:r + ROWS],
                                b1, b2, w1, w2)
            for l in range(0, 256, 128):
                save(tabm, u, freq_cycles(cols, rows[l // 128]), slice(r, r + ROWS),
                     slice(l, l + 128))
        return carry

    lax.fori_loop(0, 16, middle, 0, unroll=2)

    n = fiota((1, 128), 1)
    nrow = fiota((128, 16), 0)
    column, owner = columns_of(owner_ref, 2 * lax.div(nrow, 16) + lax.rem(nrow, 2))
    erow = fiota((128, 16), 0)
    picks = (lax.rem(lax.div(erow, 4), 16) == fiota((128, 16), 1)).astype(F32).astype(BF16)
    wcol = dot(picks, owner, NT_DIMS)
    wu = lax.rem(lax.div(fiota((128, 128), 1), 2), 8)
    for v in range(2):
        keep = jnp.where(lax.rem(lax.div(fiota((128, 128), 0), 2), 2) == v, wcol, 0.0)
        for u in range(8):
            wmat[u * 128:(u + 1) * 128, v * 128:(v + 1) * 128] = jnp.where(
                wu == u, keep, 0.0).astype(BF16)

    u8 = lax.rem(lax.div(n, 2), 8)

    def parent(u):
        u1 = lax.rem(u, 4)
        u2 = lax.div(u, 4)
        return (tofloat(2 * lax.rem(u1, 2) + lax.rem(u2, 2)),
                tofloat(2 * lax.div(u1, 2) + lax.div(u2, 2)))

    def level3(half, carry):
        mx, my = parent(u8 + 8 * half)
        p1 = (4.0 * hf + mx + 0.5) / 64.0
        p2 = (my + 0.5) / 64.0
        row = (trig(p1), trig(p2))
        w1, w2 = from_sines(row[0][1], row[0][0], row[1][1], row[1][0])
        for r in range(0, 64, ROWS):
            rows = slice(r, r + ROWS)
            d1 = off_ref[0, rows] / 64.0
            d2 = off_ref[1, rows] / 64.0
            s1, s2 = speeds_sum(row, (trig(d1), trig(d2)))
            for v in range(4):
                f1 = 128.0 * (2.0 * column + (v % 2) + 0.5) - HALF
                f2 = 128.0 * (2.0 * ryf + (v // 2) + 0.5) - HALF
                cycles = space_cycles(d1, d2, s1, s2, w1, w2, f1, f2)
                save(tab3i, half * 4 + v, -cycles, rows, slice(0, 128))
        return carry

    lax.fori_loop(0, 2, level3, 0)

    def level4(i, carry):
        half = lax.div(i, 4)
        jx = tofloat(bit(lax.rem(i, 4), 0))
        jy = tofloat(bit(lax.rem(i, 4), 1))
        mx, my = parent(u8 + 8 * half)
        mx = 4.0 * hf + mx
        w1, w2 = speeds((mx + 0.5) / 64.0, (my + 0.5) / 64.0)
        c1 = (2.0 * mx + jx + 0.5) / 128.0
        c2 = (2.0 * my + jy + 0.5) / 128.0
        row = (trig(c1), trig(c2))
        z1, z2 = from_sines(row[0][1], row[0][0], row[1][1], row[1][0])
        for r in range(0, 64, ROWS):
            rows = slice(r, r + ROWS)
            d1 = off_ref[0, rows] / 128.0
            d2 = off_ref[1, rows] / 128.0
            s1, s2 = speeds_sum(row, (trig(d1), trig(d2)))
            e1 = d1 + (jx - 0.5) / 128.0
            e2 = d2 + (jy - 0.5) / 128.0
            for v in range(4):
                f1 = 128.0 * (2.0 * column + (v % 2) + 0.5) - HALF
                f2 = 128.0 * (2.0 * ryf + (v // 2) + 0.5) - HALF
                cycles = space_cycles(e1, e2, s1, s2, w1, w2, f1, f2)
                save(tab3o, i * 4 + v, cycles, rows, slice(0, 128))
            f1 = 256.0 * (column + 0.5) - HALF
            f2 = 256.0 * (ryf + 0.5) - HALF
            cycles = space_cycles(d1, d2, s1, s2, z1, z2, f1, f2)
            save(tab4i, i, -cycles, rows, slice(0, 128))
        return carry

    lax.fori_loop(0, 8, level4, 0)

    y0 = 2 * lax.rem(lax.div(flat, n_all // 4), 2) + lax.div(flat, n_all // 2)
    x0 = lax.rem(lax.div(flat, 8), 4)
    z0 = lax.rem(lax.div(flat, 2), 4)
    c0 = lax.rem(flat, 2)

    def send_half(half):
        for odd in (1, 0):

            def send(e, carry):
                dz = lax.rem(e, 4)
                dx = lax.rem(lax.div(e, 4) + dz, 4)
                dy = 2 * lax.rem(lax.div(e, 16), 2) + odd
                yy0 = lax.rem(y0 + dy, 4)
                v = (lax.rem(x0 + dx, 4) * 8 + lax.rem(z0 + dz, 4) * 2
                     + lax.rem(c0 + lax.div(e, 32), 2))
                to = lax.rem(yy0, 2) * 64 + lax.div(yy0, 2) * 32 + v
                pltpu.make_async_remote_copy(
                    src_ref=z_ref.at[half, lax.div(to, 16), lax.rem(v, 4)],
                    dst_ref=y_ref.at[flat, half], send_sem=send2, recv_sem=recv2.at[h],
                    device_id=place(to), device_id_type=MESH).start()
                return carry

            lax.fori_loop(1 - odd, 64, send, 0)
        pltpu.make_async_copy(z_ref.at[half, h, lax.rem(flat, 4)], y_ref.at[flat, half],
                              recv2.at[h]).start()

    def stage(b):
        at = slice(b * 128, b * 128 + 128)
        whole = slice(0, 128)

        def turned(slot, source, tab, index):
            for c in range(4):
                for r in range(0, 64, ROWS):
                    rows = slice(r, r + ROWS)
                    re, im = source(c, rows)
                    parts = turn(re, im, tab, index(c), rows, at)
                    for p in range(2):
                        hi, lo = split(parts[p])
                        xh[slot, c * 64 + r:c * 64 + r + ROWS, p * 128:p * 128 + 128] = hi
                        xl[slot, c * 64 + r:c * 64 + r + ROWS, p * 128:p * 128 + 128] = lo

        def mixed(slot, table):
            first = dot(table[...], xh[slot])
            return first[:64] + first[64:] + dot(table[0:64], xl[slot])

        def run1(u2, carry):
            for u1 in range(4):
                turned(u1, lambda c, rows: (x_ref[b, u2 * 4 + c, 0, rows],
                                            x_ref[b, u2 * 4 + c, 1, rows]),
                       tab1, lambda c: (u1 * 4 + c) * 4 + u2)
                y1[u1 * 4 + u2] = mixed(u1, t1s)
            return carry

        lax.fori_loop(0, 4, run1, 0)

        def run2(half, pair):
            for slot in range(4):
                u1 = 2 * pair + slot // 2
                u2 = 2 * half + slot % 2
                u = u1 + 4 * u2
                turned(slot, lambda c, rows: (y1[u1 * 4 + c, rows, 0:128],
                                              y1[u1 * 4 + c, rows, 128:256]),
                       tab2, lambda c: (u1 * 4 + c) * 4 + u2)
                out = mixed(slot, t1_ref)
                to = pl.ds(pl.multiple_of((u1 + 4 * (slot % 2)) * 128, 128), 128)
                for r in range(0, 64, ROWS):
                    rows = slice(r, r + ROWS)
                    parts = turn(out[rows, 0:128], out[rows, 128:256], tabm, u, rows, at)
                    for p in range(2):
                        hi, lo = split(parts[p])
                        y2[p * 64 + r:p * 64 + r + ROWS, to] = hi
                        y2[128 + p * 64 + r:128 + p * 64 + r + ROWS, to] = lo

        def run3(half):
            both = dot(y2[...], wmat[...])
            summed = both[:128] + both[128:]
            for v in range(2):
                for r in range(0, 64, ROWS):
                    rows = slice(r, r + ROWS)
                    l = v * 128
                    parts = turn(summed[r:r + ROWS, l:l + 128],
                                 summed[64 + r:64 + r + ROWS, l:l + 128], tab3i,
                                 half * 4 + 2 * b + v, rows, whole)
                    for p in range(2):
                        hi, lo = split(parts[p])
                        to = slice((v * 2 + p) * 128, (v * 2 + p + 1) * 128)
                        x3[r:r + ROWS, to] = hi
                        x3[64 + r:64 + r + ROWS, to] = lo
                        x3[128 + r:128 + r + ROWS, to] = hi
            for j in range(4):
                out = dot(t3_ref[j * 64:(j + 1) * 64], x3[...])
                for r in range(0, 64, ROWS):
                    rows = slice(r, r + ROWS)
                    low = slice(64 + r, 64 + r + ROWS)
                    if b == 1:
                        re, im = v4[half * 4 + j, rows], v4[half * 4 + j, low]
                    for v in range(2):
                        l = v * 256
                        p, q = turn(out[rows, l:l + 128], out[rows, l + 128:l + 256], tab3o,
                                    (half * 4 + j) * 4 + 2 * b + v, rows, whole)
                        first = b == 0 and v == 0
                        re = p if first else re + p
                        im = q if first else im + q
                    if b == 1:
                        re, im = turn(re, im, tab4i, half * 4 + j, rows, whole)
                    v4[half * 4 + j, rows] = re
                    v4[half * 4 + j, low] = im
                if b == 1:
                    flipped = v4[half * 4 + j].T
                    for k in range(8):
                        z_ref[half, k, j] = flipped[k * 16:(k + 1) * 16]

        def run(half, carry):
            def pairs(pair, carry):
                run2(half, pair)
                return carry

            lax.fori_loop(0, 2, pairs, 0)
            run3(half)
            if b == 1:
                send_half(half)
            return carry

        lax.fori_loop(0, 2, run, 0)

    for b in range(2):
        own1[b].wait()
        for i in range(1, 16):
            exchange1(b, i).wait()
        if b == 1:
            pl.semaphore_wait(ready, n_group - 1)
        stage(b)

    v1d = lax.rem(ry, 4)
    v2d = lax.div(ry, 4)
    zero = jnp.zeros((64, 64), BF16)
    pieces = [dot(onehot, tf_ref[p, pl.ds(pl.multiple_of(v2d * 64, 64), 64), :],
                  TN_DIMS).astype(BF16) for p in range(2)]
    for p in range(2):
        for q in range(2):
            for piece in range(2):
                for low in range(2):
                    lanes = slice(low * 128 + q * 64, low * 128 + q * 64 + 64)
                    rows = slice(piece * 128 + p * 64, piece * 128 + p * 64 + 64)
                    use = p == q and not (piece == 1 and low == 1)
                    tmat[rows, lanes] = pieces[piece] if use else zero
    ids = fiota((512, 16), 0)
    column, _ = columns_of(owner_ref, 2 * h + lax.rem(lax.div(ids, 16), 2))
    jx, jy = tofloat(lax.rem(v2d, 2)), tofloat(lax.div(v2d, 2))
    vx, vy = tofloat(lax.rem(v1d, 2)), tofloat(lax.div(v1d, 2))
    f2 = 256.0 * (tofloat(lax.rem(n, 16)) + 0.5) - HALF

    def level5(src, carry):
        for l in range(0, 512, 128):
            mx, my = parent(lax.div(n + l, 32))
            c1 = (2.0 * (4.0 * tofloat(src) + mx) + vx + 0.5) / 128.0
            c2 = (2.0 * my + vy + 0.5) / 128.0
            row = (trig(c1), trig(c2))
            w1, w2 = from_sines(row[0][1], row[0][0], row[1][1], row[1][0])
            f1 = 256.0 * (column[:, l:l + 128] + 0.5) - HALF
            for r in range(0, 64, ROWS):
                d1 = (doff[0, r:r + ROWS] + (jx - 0.5)) / 256.0
                d2 = (doff[1, r:r + ROWS] + (jy - 0.5)) / 256.0
                s1, s2 = speeds_sum(row, (trig(d1), trig(d2)))
                save(tabf, src, space_cycles(d1, d2, s1, s2, w1, w2, f1, f2),
                     slice(r, r + ROWS), slice(l, l + 128))
        return carry

    lax.fori_loop(0, 8, level5, 0)

    def run4(e, carry):
        src = lax.rem(lax.div(h, 4) + 1 + lax.div(e, 4), 2) * 4 + lax.rem(h + e, 4)
        landed = y_ref.at[pl.ds(pl.multiple_of(src * 16, 16), 16)]
        pltpu.make_async_copy(landed, landed, recv2.at[src]).wait()
        for m in range(16):
            yy[pl.ds(m, 32, stride=16), :] = y_ref[src * 16 + m].reshape(32, 128)
        hi, lo = split(yy[...])
        out = dot(tmat[...], jnp.concatenate([hi, lo], axis=1), NT_DIMS)
        out = out[:128] + out[128:]
        for l in range(0, 512, 128):
            lanes = pl.ds(pl.multiple_of(src * 512 + l, 128), 128)
            for r in range(0, 64, ROWS):
                rows = slice(r, r + ROWS)
                re, im = turn(out[r:r + ROWS, l:l + 128], out[64 + r:64 + r + ROWS, l:l + 128],
                              tabf, src, rows, slice(l, l + 128))
                o_ref[0, rows, lanes] = re
                o_ref[1, rows, lanes] = im
        return carry

    lax.fori_loop(0, 8, run4, 0)
    sent = y_ref.at[pl.ds(0, n_all - 1)]
    pltpu.make_async_copy(sent, sent, send2).wait()


VMEM_LIMIT = 62 * 1024 * 1024


def body(weights, owner_map, node_index):
    t1, t3, tf, off, off3 = constants()
    n_dev = lax.axis_size("dev")
    n_all = lax.axis_size("grp") * n_dev
    vmem = pl.BlockSpec(memory_space=pltpu.VMEM)
    hbm = pl.BlockSpec(memory_space=pl.ANY)
    dma = pltpu.SemaphoreType.DMA
    return pl.pallas_call(
        functools.partial(kernel, n_dev, n_all, n_all // 16),
        out_shape=jax.ShapeDtypeStruct((2, 64, 4096), F32),
        in_specs=[vmem] * 2 + [hbm] * 6,
        out_specs=vmem,
        scratch_shapes=[
            pltpu.VMEM((2, 16, 2, 64, 128), F32),
            pltpu.VMEM(t1.shape, BF16),
            pltpu.VMEM(t3.shape, BF16),
            pltpu.VMEM(tf.shape, BF16),
            pltpu.VMEM(off.shape, F32),
            pltpu.VMEM(off3.shape, BF16),
            pltpu.VMEM((2, 8, 4, 16, 128), F32),
            pltpu.VMEM((128, 2, 16, 128), F32),
            pltpu.VMEM((64, 2, 64, 256), F32),
            pltpu.VMEM((64, 2, 64, 256), F32),
            pltpu.VMEM((16, 2, 64, 256), F32),
            pltpu.VMEM((8, 2, 64, 128), F32),
            pltpu.VMEM((32, 2, 64, 128), F32),
            pltpu.VMEM((8, 2, 64, 128), F32),
            pltpu.VMEM((8, 2, 64, 512), F32),
            pltpu.VMEM((4, 2, 64, 128), F32),
            pltpu.VMEM((64, 128), F32),
            pltpu.VMEM((2, 8, 64, 256), F32),
            pltpu.VMEM((64, 256), F32),
            pltpu.VMEM((2, 64, 128), F32),
            pltpu.VMEM((128, 256), BF16),
            pltpu.VMEM((4, 256, 256), BF16),
            pltpu.VMEM((4, 256, 256), BF16),
            pltpu.VMEM((16, 64, 256), F32),
            pltpu.VMEM((256, 1024), BF16),
            pltpu.VMEM((1024, 256), BF16),
            pltpu.VMEM((192, 512), BF16),
            pltpu.VMEM((8, 128, 128), F32),
            pltpu.VMEM((256, 256), BF16),
            pltpu.VMEM((512, 128), F32),
            dma((32,)),
            dma((32,)),
            dma(()),
            dma((8,)),
            dma((5,)),
            pltpu.SemaphoreType.REGULAR,
        ],
        compiler_params=pltpu.CompilerParams(
            vmem_limit_bytes=VMEM_LIMIT, collective_id=0, has_side_effects=True),
        name="butterfly",
    )(node_index, owner_map.reshape(1, 16), weights, t1, t3, tf, off, off3)


def solution(mesh):
    in_specs = (P(None, None, ("grp", "dev")), P(), P())
    out_specs = P(None, None, ("grp", "dev"))
    return jax.shard_map(body, mesh=mesh, in_specs=in_specs, out_specs=out_specs, check_vma=False)
```

```python
import functools
import math

import jax
import jax.numpy as jnp
import numpy as np
from jax import lax
from jax.experimental import pallas as pl
from jax.experimental.pallas import tpu as pltpu
from jax.sharding import PartitionSpec as P

F32 = jnp.float32
BF16 = jnp.bfloat16
HALF = 2048.0
NT_DIMS = (((1,), (1,)), ((), ()))
TN_DIMS = (((0,), (0,)), ((), ()))
NN_DIMS = (((1,), (0,)), ((), ()))


def fit(function, count):
    angle = (np.arange(64) + 0.5) * np.pi / 64
    points = 0.125 + 0.125 * np.cos(angle)
    cheb = np.polynomial.chebyshev.Chebyshev.fit(
        points, function(np.sqrt(points)), count - 1, domain=[0.0, 0.25]
    )
    return [float(c) for c in cheb.convert(kind=np.polynomial.Polynomial).coef]


ROOT2 = math.sqrt(2.0)
SIN_COEF = fit(lambda r: ROOT2 * np.sin(np.pi * r) / r, 5)
COS_COEF = fit(lambda r: ROOT2 * np.cos(np.pi * r), 5)


def horner(coef, u):
    total = coef[-1] * u + coef[-2]
    for c in coef[-3::-1]:
        total = total * u + c
    return total


def trig(cycles):
    r = cycles - jnp.round(cycles)
    u = r * r
    s = horner(SIN_COEF, u) * r
    c = horner(COS_COEF, u)
    return 1.0 - s * s, s * c


def cheb_nodes():
    return 0.5 * np.cos(np.pi * (2.0 * np.arange(8) + 1.0) / 16.0)


def canon_tables():
    z = cheb_nodes()
    basis = np.zeros((2, 8, 8))
    for c in range(2):
        places = z / 2 + c / 2 - 0.25
        for i in range(8):
            value = np.ones(8)
            for k in range(8):
                if k != i:
                    value = value * (places - z[k]) / (z[i] - z[k])
            basis[c, i] = value
    return [np.kron(basis[c % 2], basis[c // 2]) for c in range(4)]


def split_np(a):
    hi = np.asarray(a, np.float32).astype(BF16)
    lo = (np.asarray(a, np.float64) - hi.astype(np.float64)).astype(np.float32).astype(BF16)
    return hi, lo


def constants():
    z = cheb_nodes().astype(np.float32)
    tables = canon_tables()
    t_in = np.concatenate(tables, axis=1)
    t_out = np.concatenate([t.T for t in tables], axis=0)
    in_h, in_l = split_np(t_in)
    out_h, out_l = split_np(t_out)
    t1 = np.concatenate([in_h, in_l], axis=0)
    t3 = np.concatenate([out_h, out_h, out_l], axis=1)
    tf = np.stack([out_h, out_l])
    ox = np.repeat(z, 8)
    oy = np.tile(z, 8)
    off = np.stack([np.broadcast_to(o[:, None], (64, 128)) for o in (ox, oy)])
    pieces = []
    rest = off.astype(np.float32)
    for _ in range(3):
        piece = rest.astype(BF16)
        pieces.append(piece)
        rest = rest - piece.astype(np.float32)
    return t1, t3, tf, np.ascontiguousarray(off, np.float32), np.stack(pieces)


def fiota(shape, axis):
    return lax.broadcasted_iota(jnp.int32, shape, axis)


def node_onehot(node_ref):
    flat = node_ref[0:1, :] * 8 + node_ref[1:2, :]
    return (fiota((64, 64), 0) == flat).astype(F32).astype(BF16)


def dot(a, b, dims=NN_DIMS):
    return lax.dot_general(a, b, dims, preferred_element_type=F32)


def split(x):
    hi = x.astype(BF16)
    return hi, (x - hi.astype(F32)).astype(BF16)


def from_sines(s1, c1, s2, c2):
    one = (2.0 + s1 * s2) * 0.0625
    two = (2.0 + c1 * c2) * 0.0625
    return one * one, two * two


def speeds(x1, x2):
    c1, s1 = trig(x1)
    c2, s2 = trig(x2)
    return from_sines(s1, c1, s2, c2)


def speeds_sum(row, col):
    sines = []
    for (ca, sa), (cb, sb) in zip(row, col):
        sines += [sa * cb + ca * sb, ca * cb - sa * sb]
    return from_sines(*sines)


def root(x):
    return x * lax.rsqrt(x)


def freq_columns(d1, d2, a1, a2, v1, v2):
    e1 = v1 * d1
    e2 = v2 * d2
    linear = a2 * d2 if isinstance(a1, float) and a1 == 0.0 else a1 * d1 + a2 * d2
    return 2.0 * e1, 2.0 * e2, e1 * d1 + e2 * d2, linear


def freq_row(g1, g2, v1, v2):
    square = v1 * g1 * g1 + v2 * g2 * g2 + 1.0
    return g1, g2, square, root(square)


def freq_cycles(columns, row):
    e1, e2, e0, linear = columns
    g1, g2, square, base = row
    numer = e1 * g1 + e2 * g2 + e0
    return linear + numer / (root(square + numer) + base)


def space_cycles(d1, d2, v1, v2, w1, w2, f1, f2):
    q1 = f1 * f1
    q2 = f2 * f2
    base = w1 * q1 + w2 * q2 + 1.0
    numer = (v1 - w1) * q1 + (v2 - w2) * q2
    return d1 * f1 + d2 * f2 + numer / (root(base + numer) + root(base))


ROWS = 32
MESH = pl.DeviceIdType.MESH


def bit(value, place):
    return lax.rem(lax.div(value, 1 << place), 2)


def tofloat(value):
    return value.astype(F32)


def splat(value):
    return jnp.full((1, 128), value, F32)


def save(tab, index, cycles, rows, lanes):
    cs, sn = trig(cycles)
    tab[index, 0, rows, lanes] = cs
    tab[index, 1, rows, lanes] = sn


def turn(re, im, tab, index, rows, lanes):
    cs = tab[index, 0, rows, lanes]
    sn = tab[index, 1, rows, lanes]
    return re * cs - im * sn, re * sn + im * cs


def columns_of(owner_ref, slot):
    owner = (owner_ref[0:1, :] == slot).astype(F32).astype(BF16)
    numbers = fiota((8, 16), 1).astype(F32).astype(BF16)
    return dot(numbers, owner, NT_DIMS)[0:1, :], owner


def kernel(n_dev, n_all, n_group, node_ref, owner_ref, w_hbm, t1_hbm, t3_hbm, tf_hbm, off_hbm, off3_hbm,
           o_ref, x_ref, t1_ref, t3_ref, tf_ref, off_ref, off3_ref, z_ref, y_ref, tab1, tab2,
           tabm, tab3i, tab3o, tab4i, tabf, lin2, line, prod, part, doff, t1s, xh, xl, y1, y2, wmat, x3, v4, tmat,
           yy, send1, recv1, send2, recv2, local, ready):
    flat = lax.axis_index("grp") * n_dev + lax.axis_index("dev")
    h = lax.div(flat, 16)
    ry = lax.rem(flat, 16)
    hf = tofloat(h)
    ryf = tofloat(ry)

    def place(device):
        return lax.div(device, n_dev), lax.rem(device, n_dev)

    barrier = pltpu.get_barrier_semaphore()

    def tell(semaphore, device):
        pl.semaphore_signal(semaphore, inc=1, device_id=place(device), device_id_type=MESH)

    for i in range(1, 16):
        tell(barrier, h * 16 + lax.rem(ry + i, 16))
    for g in range(1, n_group):
        tell(barrier, lax.rem(h + g, n_group) * 16 + ry)
    loads = [pltpu.make_async_copy(a, b, local.at[i]) for i, (a, b) in enumerate(
        [(t1_hbm, t1_ref), (t3_hbm, t3_ref), (tf_hbm, tf_ref), (off_hbm, off_ref),
         (off3_hbm, off3_ref)])]
    for load in loads:
        load.start()
    for load in loads:
        load.wait()

    onehot = node_onehot(node_ref)
    for axis in range(2):
        doff[axis] = sum(dot(onehot, off3_ref[p, axis], TN_DIMS) for p in (2, 1, 0))
    for c in range(4):
        t1s[:, c * 64:(c + 1) * 64] = dot(t1_ref[:, c * 64:(c + 1) * 64], onehot).astype(BF16)

    lane = [fiota((1, 128), 1) + k for k in (0, 128)]
    bx = [tofloat(lax.rem(v, 64)) for v in lane]
    by = [4.0 * ryf + tofloat(lax.div(v, 64)) for v in lane]

    def products(index, offsets, scale, shift, width, child):
        for l in range(0, 256, 128):
            for axis, at in ((0, bx[l // 128]), (1, by[l // 128])):
                g = width * at + child - HALF
                for r in range(0, 64, ROWS):
                    d = scale * offsets[axis, r:r + ROWS] + shift
                    prod[axis, index, r:r + ROWS, l:l + 128] = d * (2.0 * g + d)

    def products1(i, carry):
        child = tofloat(lax.div(i, 2))
        products(i, doff, 16.0, 16.0 * (child - 0.5), 64.0, 32.0 * (tofloat(lax.rem(i, 2)) + 0.5))
        return carry

    def products2(i, carry):
        products(4 + i, off_ref, 32.0, 32.0 * (tofloat(i) - 0.5), 64.0, 32.0)
        products(6 + i, off_ref, 32.0, 0.0, 64.0, 32.0 * (tofloat(i) + 0.5))
        return carry

    lax.fori_loop(0, 4, products1, 0)
    lax.fori_loop(0, 2, products2, 0)

    def linear2(i, carry):
        ux = tofloat(lax.div(i, 2))
        a1 = (2.0 * hf + ux + 0.5) / 32.0
        b1 = (4.0 * hf + 2.0 * ux + tofloat(lax.rem(i, 2)) + 0.5) / 64.0
        for r in range(0, 64, ROWS):
            rows = slice(r, r + ROWS)
            o = off_ref[0, rows]
            save(lin2, i, 32.0 * (a1 * o - b1 * (o - 0.5)), rows, slice(0, 128))
        return carry

    lax.fori_loop(0, 4, linear2, 0)

    n = fiota((1, 128), 1)
    nrow = fiota((128, 16), 0)
    column, owner = columns_of(owner_ref, 2 * lax.div(nrow, 16) + lax.rem(nrow, 2))
    erow = fiota((128, 16), 0)
    picks = (lax.rem(lax.div(erow, 4), 16) == fiota((128, 16), 1)).astype(F32).astype(BF16)
    wcol = dot(picks, owner, NT_DIMS)
    wu = lax.rem(lax.div(fiota((128, 128), 1), 2), 8)
    for v in range(2):
        keep = jnp.where(lax.rem(lax.div(fiota((128, 128), 0), 2), 2) == v, wcol, 0.0)
        for u in range(8):
            wmat[u * 128:(u + 1) * 128, v * 128:(v + 1) * 128] = jnp.where(
                wu == u, keep, 0.0).astype(BF16)

    u8 = lax.rem(lax.div(n, 2), 8)

    def parent(u):
        u1 = lax.rem(u, 4)
        u2 = lax.div(u, 4)
        return (tofloat(2 * lax.rem(u1, 2) + lax.rem(u2, 2)),
                tofloat(2 * lax.div(u1, 2) + lax.div(u2, 2)))

    pl.semaphore_wait(barrier, 14 + n_group)
    for g in range(1, n_group):
        tell(ready, lax.rem(h + g, n_group) * 16 + ry)

    def chunk(m, b):
        return w_hbm.at[:, :, pl.ds(pl.multiple_of(m * 256 + b * 128, 128), 128)]

    def exchange1(b, i):
        m = (lax.rem(lax.div(ry, 8) + i // 8, 2) * 8
             + lax.rem(lax.div(lax.rem(ry, 8), 2) + i // 2 % 4, 4) * 2 + lax.rem(ry + i, 2))
        return pltpu.make_async_remote_copy(
            src_ref=chunk(m, b), dst_ref=x_ref.at[b, ry], send_sem=send1.at[b * 16 + i],
            recv_sem=recv1.at[b * 16 + i], device_id=place(h * 16 + m), device_id_type=MESH)

    for b in range(2):
        for i in range(1, 16):
            exchange1(b, i).start()
    own1 = [pltpu.make_async_copy(chunk(ry, b), x_ref.at[b, ry], recv1.at[b * 16])
            for b in range(2)]
    for copy in own1:
        copy.start()

    def freq_rest(row, ix, iy, v1, v2, rows, lanes):
        square, base = row
        numer = v1 * prod[0, ix, rows, lanes] + v2 * prod[1, iy, rows, lanes]
        return numer / (root(square + numer) + base)

    def level1(i, carry):
        c = lax.rem(i, 4)
        u1 = lax.div(i, 4)
        a1 = (2.0 * hf + tofloat(bit(u1, 0)) + 0.5) / 32.0
        a2 = (tofloat(bit(u1, 1)) + 0.5) / 32.0
        v1, v2 = speeds(splat(a1), splat(a2))
        sx = 16.0 * (tofloat(bit(c, 0)) - 0.5)
        sy = 16.0 * (tofloat(bit(c, 1)) - 0.5)
        for r in range(0, 64, ROWS):
            line[r:r + ROWS] = -(a1 * (sx + 16.0 * doff[0, r:r + ROWS])
                                 + a2 * (sy + 16.0 * doff[1, r:r + ROWS]))

        def inner(u2, carry):
            for l in range(0, 256, 128):
                k = l // 128
                row = freq_row(32.0 * (2.0 * bx[k] + tofloat(bit(u2, 0)) + 0.5) - HALF,
                               32.0 * (2.0 * by[k] + tofloat(bit(u2, 1)) + 0.5) - HALF, v1, v2)
                for r in range(0, 64, ROWS):
                    rows = slice(r, r + ROWS)
                    lanes = slice(l, l + 128)
                    rest = freq_rest(row[2:], 2 * bit(c, 0) + bit(u2, 0),
                                     2 * bit(c, 1) + bit(u2, 1), v1, v2, rows, lanes)
                    save(tab1, i * 4 + u2, line[rows] - rest, rows, lanes)
            return carry

        lax.fori_loop(0, 4, inner, 0, unroll=2)
        return carry

    lax.fori_loop(0, 16, level1, 0)

    mirror = fiota((ROWS, 128), 1)
    mirror = lax.div(mirror, 64) * 64 + 63 - lax.rem(mirror, 64)

    def mirrored(tab, index, other, cycles, lin, which, r, lanes):
        cs, sn = trig(cycles)
        cl = lin[which, 0, r:r + ROWS]
        sl = lin[which, 1, r:r + ROWS]
        p, q, s, t = cs * cl, sn * sl, sn * cl, cs * sl
        tab[index, 0, r:r + ROWS, lanes] = p - q
        tab[index, 1, r:r + ROWS, lanes] = s + t
        for part_id, value in enumerate((p + q, s - t)):
            value = jnp.take_along_axis(value, mirror, axis=1, mode="promise_in_bounds")
            for k in range(0, ROWS, 8):
                to = 56 - r - k
                tab[other, part_id, to:to + 8, lanes] = value[k:k + 8]

    def level2(i, carry):
        u1 = lax.div(i, 2)
        a1 = (2.0 * hf + tofloat(bit(u1, 0)) + 0.5) / 32.0
        a2 = (tofloat(bit(u1, 1)) + 0.5) / 32.0
        v1, v2 = speeds(splat(a1), splat(a2))
        cy = tofloat(lax.rem(i, 2))
        cyi = lax.rem(i, 2)
        for r in range(0, 64, ROWS):
            rows = slice(r, r + ROWS)
            for l in range(0, 256, 128):
                k = l // 128
                lanes = slice(l, l + 128)
                row = freq_row(32.0 * (2.0 * bx[k] + 0.5) - HALF,
                               32.0 * (2.0 * by[k] + cy + 0.5) - HALF, v1, v2)
                part[rows, lanes] = (a2 * (32.0 * off_ref[1, rows])
                                     + freq_rest(row[2:], 6, 6 + cyi, v1, v2, rows, lanes))
        index = (u1 * 4 + 2 * cyi) * 4

        def inner(u2, carry):
            b1 = (4.0 * hf + 2.0 * tofloat(bit(u1, 0)) + tofloat(bit(u2, 0)) + 0.5) / 64.0
            b2 = (2.0 * tofloat(bit(u1, 1)) + tofloat(bit(u2, 1)) + 0.5) / 64.0
            w1, w2 = speeds(splat(b1), splat(b2))
            for l in range(0, 256, 128):
                k = l // 128
                lanes = slice(l, l + 128)
                row = freq_row(64.0 * (bx[k] + 0.5) - HALF, 64.0 * (by[k] + 0.5) - HALF, w1, w2)
                for r in range(0, 64, ROWS):
                    rows = slice(r, r + ROWS)
                    rest = freq_rest(row[2:], 4, 4 + cyi, w1, w2, rows, lanes)
                    down = (b2 * 32.0) * (off_ref[1, rows] + (cy - 0.5))
                    mirrored(tab2, index + u2, index + 4 + u2, part[rows, lanes] - down - rest,
                             lin2, bit(u1, 0) * 2 + bit(u2, 0), r, lanes)
            return carry

        lax.fori_loop(0, 4, inner, 0, unroll=2)
        return carry

    lax.fori_loop(0, 8, level2, 0)

    def middle(u, carry):
        u1 = lax.rem(u, 4)
        u2 = lax.div(u, 4)
        b1 = (4.0 * hf + 2.0 * tofloat(bit(u1, 0)) + tofloat(bit(u2, 0)) + 0.5) / 64.0
        b2 = (2.0 * tofloat(bit(u1, 1)) + tofloat(bit(u2, 1)) + 0.5) / 64.0
        w1, w2 = speeds(splat(b1), splat(b2))
        rows = [freq_row(64.0 * (bx[k] + 0.5) - HALF, 64.0 * (by[k] + 0.5) - HALF, w1, w2)
                for k in range(2)]
        for r in range(0, 64, ROWS):
            cols = freq_columns(64.0 * off_ref[0, r:r + ROWS], 64.0 * off_ref[1, r:r + ROWS],
                                b1, b2, w1, w2)
            for l in range(0, 256, 128):
                save(tabm, u, freq_cycles(cols, rows[l // 128]), slice(r, r + ROWS),
                     slice(l, l + 128))
        return carry

    lax.fori_loop(0, 16, middle, 0, unroll=2)

    def level3(half, carry):
        mx, my = parent(u8 + 8 * half)
        p1 = (4.0 * hf + mx + 0.5) / 64.0
        p2 = (my + 0.5) / 64.0
        row = (trig(p1), trig(p2))
        w1, w2 = from_sines(row[0][1], row[0][0], row[1][1], row[1][0])
        for r in range(0, 64, ROWS):
            rows = slice(r, r + ROWS)
            d1 = off_ref[0, rows] / 64.0
            d2 = off_ref[1, rows] / 64.0
            s1, s2 = speeds_sum(row, (trig(d1), trig(d2)))
            for v in range(4):
                f1 = 128.0 * (2.0 * column + (v % 2) + 0.5) - HALF
                f2 = 128.0 * (2.0 * ryf + (v // 2) + 0.5) - HALF
                cycles = space_cycles(d1, d2, s1, s2, w1, w2, f1, f2)
                save(tab3i, half * 4 + v, -cycles, rows, slice(0, 128))
        return carry

    lax.fori_loop(0, 2, level3, 0)

    def level4(i, carry):
        half = lax.div(i, 4)
        jx = tofloat(bit(lax.rem(i, 4), 0))
        jy = tofloat(bit(lax.rem(i, 4), 1))
        mx, my = parent(u8 + 8 * half)
        mx = 4.0 * hf + mx
        w1, w2 = speeds((mx + 0.5) / 64.0, (my + 0.5) / 64.0)
        c1 = (2.0 * mx + jx + 0.5) / 128.0
        c2 = (2.0 * my + jy + 0.5) / 128.0
        row = (trig(c1), trig(c2))
        z1, z2 = from_sines(row[0][1], row[0][0], row[1][1], row[1][0])
        for r in range(0, 64, ROWS):
            rows = slice(r, r + ROWS)
            d1 = off_ref[0, rows] / 128.0
            d2 = off_ref[1, rows] / 128.0
            s1, s2 = speeds_sum(row, (trig(d1), trig(d2)))
            e1 = d1 + (jx - 0.5) / 128.0
            e2 = d2 + (jy - 0.5) / 128.0
            for v in range(4):
                f1 = 128.0 * (2.0 * column + (v % 2) + 0.5) - HALF
                f2 = 128.0 * (2.0 * ryf + (v // 2) + 0.5) - HALF
                cycles = space_cycles(e1, e2, s1, s2, w1, w2, f1, f2)
                save(tab3o, i * 4 + v, cycles, rows, slice(0, 128))
            f1 = 256.0 * (column + 0.5) - HALF
            f2 = 256.0 * (ryf + 0.5) - HALF
            cycles = space_cycles(d1, d2, s1, s2, z1, z2, f1, f2)
            save(tab4i, i, -cycles, rows, slice(0, 128))
        return carry

    lax.fori_loop(0, 8, level4, 0)

    y0 = 2 * lax.rem(lax.div(flat, n_all // 4), 2) + lax.div(flat, n_all // 2)
    x0 = lax.rem(lax.div(flat, 8), 4)
    z0 = lax.rem(lax.div(flat, 2), 4)
    c0 = lax.rem(flat, 2)

    def send_half(half):
        for odd in (1, 0):

            def send(e, carry):
                dz = lax.rem(e, 4)
                dx = lax.rem(lax.div(e, 4) + dz, 4)
                dy = 2 * lax.rem(lax.div(e, 16), 2) + odd
                yy0 = lax.rem(y0 + dy, 4)
                v = (lax.rem(x0 + dx, 4) * 8 + lax.rem(z0 + dz, 4) * 2
                     + lax.rem(c0 + lax.div(e, 32), 2))
                to = lax.rem(yy0, 2) * 64 + lax.div(yy0, 2) * 32 + v
                pltpu.make_async_remote_copy(
                    src_ref=z_ref.at[half, lax.div(to, 16), lax.rem(v, 4)],
                    dst_ref=y_ref.at[half, flat], send_sem=send2,
                    recv_sem=recv2.at[half * 8 + h],
                    device_id=place(to), device_id_type=MESH).start()
                return carry

            lax.fori_loop(1 - odd, 64, send, 0)
        pltpu.make_async_copy(z_ref.at[half, h, lax.rem(flat, 4)], y_ref.at[half, flat],
                              recv2.at[half * 8 + h]).start()

    def stage(b):
        at = slice(b * 128, b * 128 + 128)
        whole = slice(0, 128)

        def turned(slot, source, tab, index):
            for c in range(4):
                for r in range(0, 64, ROWS):
                    rows = slice(r, r + ROWS)
                    re, im = source(c, rows)
                    parts = turn(re, im, tab, index(c), rows, at)
                    for p in range(2):
                        hi, lo = split(parts[p])
                        xh[slot, c * 64 + r:c * 64 + r + ROWS, p * 128:p * 128 + 128] = hi
                        xl[slot, c * 64 + r:c * 64 + r + ROWS, p * 128:p * 128 + 128] = lo

        def mixed(slot, table):
            first = dot(table[...], xh[slot])
            return first[:64] + first[64:] + dot(table[0:64], xl[slot])

        def run1(e, carry):
            ux = lax.rem(lax.div(ry, 8) + lax.div(e, 2), 2)
            uz = lax.rem(lax.div(ry, 4) + e, 2)
            u2 = 2 * ux + uz
            for c in range(4):
                i = (lax.rem(lax.div(ry, 8) + ux, 2) * 8
                     + lax.rem(lax.div(lax.rem(ry, 8), 2) + 4 - 2 * uz - c // 2, 4) * 2
                     + lax.rem(ry + c, 2))
                landed = x_ref.at[b, u2 * 4 + c]
                pltpu.make_async_copy(landed, landed, recv1.at[b * 16 + i]).wait()
            for u1 in range(4):
                turned(u1, lambda c, rows: (x_ref[b, u2 * 4 + c, 0, rows],
                                            x_ref[b, u2 * 4 + c, 1, rows]),
                       tab1, lambda c: (u1 * 4 + c) * 4 + u2)
                y1[u1 * 4 + u2] = mixed(u1, t1s)
            return carry

        lax.fori_loop(0, 4, run1, 0)

        def run2(half, pair):
            for slot in range(4):
                u1 = 2 * pair + slot // 2
                u2 = 2 * half + slot % 2
                u = u1 + 4 * u2
                turned(slot, lambda c, rows: (y1[u1 * 4 + c, rows, 0:128],
                                              y1[u1 * 4 + c, rows, 128:256]),
                       tab2, lambda c: (u1 * 4 + c) * 4 + u2)
                out = mixed(slot, t1_ref)
                to = pl.ds(pl.multiple_of((u1 + 4 * (slot % 2)) * 128, 128), 128)
                for r in range(0, 64, ROWS):
                    rows = slice(r, r + ROWS)
                    parts = turn(out[rows, 0:128], out[rows, 128:256], tabm, u, rows, at)
                    for p in range(2):
                        hi, lo = split(parts[p])
                        y2[p * 64 + r:p * 64 + r + ROWS, to] = hi
                        y2[128 + p * 64 + r:128 + p * 64 + r + ROWS, to] = lo

        def run3(half):
            both = dot(y2[...], wmat[...])
            summed = both[:128] + both[128:]
            for v in range(2):
                for r in range(0, 64, ROWS):
                    rows = slice(r, r + ROWS)
                    l = v * 128
                    parts = turn(summed[r:r + ROWS, l:l + 128],
                                 summed[64 + r:64 + r + ROWS, l:l + 128], tab3i,
                                 half * 4 + 2 * b + v, rows, whole)
                    for p in range(2):
                        hi, lo = split(parts[p])
                        to = slice((v * 2 + p) * 128, (v * 2 + p + 1) * 128)
                        x3[r:r + ROWS, to] = hi
                        x3[64 + r:64 + r + ROWS, to] = lo
                        x3[128 + r:128 + r + ROWS, to] = hi
            for j in range(4):
                out = dot(t3_ref[j * 64:(j + 1) * 64], x3[...])
                for r in range(0, 64, ROWS):
                    rows = slice(r, r + ROWS)
                    low = slice(64 + r, 64 + r + ROWS)
                    if b == 1:
                        re, im = v4[half * 4 + j, rows], v4[half * 4 + j, low]
                    for v in range(2):
                        l = v * 256
                        p, q = turn(out[rows, l:l + 128], out[rows, l + 128:l + 256], tab3o,
                                    (half * 4 + j) * 4 + 2 * b + v, rows, whole)
                        first = b == 0 and v == 0
                        re = p if first else re + p
                        im = q if first else im + q
                    if b == 1:
                        re, im = turn(re, im, tab4i, half * 4 + j, rows, whole)
                    v4[half * 4 + j, rows] = re
                    v4[half * 4 + j, low] = im
                if b == 1:
                    flipped = v4[half * 4 + j].T
                    for k in range(8):
                        z_ref[half, k, j] = flipped[k * 16:(k + 1) * 16]

        def run(half, carry):
            def pairs(pair, carry):
                run2(half, pair)
                return carry

            lax.fori_loop(0, 2, pairs, 0)
            run3(half)
            if b == 1:
                send_half(half)
            return carry

        lax.fori_loop(0, 2, run, 0)

    for b in range(2):
        if b == 1:
            pl.semaphore_wait(ready, n_group - 1)
        stage(b)

    v1d = lax.rem(ry, 4)
    v2d = lax.div(ry, 4)
    zero = jnp.zeros((64, 64), BF16)
    pieces = [dot(onehot, tf_ref[p, pl.ds(pl.multiple_of(v2d * 64, 64), 64), :],
                  TN_DIMS).astype(BF16) for p in range(2)]
    for p in range(2):
        for q in range(2):
            for piece in range(2):
                for low in range(2):
                    lanes = slice(low * 128 + q * 64, low * 128 + q * 64 + 64)
                    rows = slice(piece * 128 + p * 64, piece * 128 + p * 64 + 64)
                    use = p == q and not (piece == 1 and low == 1)
                    tmat[rows, lanes] = pieces[piece] if use else zero
    ids = fiota((512, 16), 0)
    column, _ = columns_of(owner_ref, 2 * h + lax.rem(lax.div(ids, 16), 2))
    jx, jy = tofloat(lax.rem(v2d, 2)), tofloat(lax.div(v2d, 2))
    vx, vy = tofloat(lax.rem(v1d, 2)), tofloat(lax.div(v1d, 2))
    f2 = 256.0 * (tofloat(lax.rem(n, 16)) + 0.5) - HALF

    def level5(src, carry):
        for l in range(0, 512, 128):
            mx, my = parent(lax.div(n + l, 32))
            c1 = (2.0 * (4.0 * tofloat(src) + mx) + vx + 0.5) / 128.0
            c2 = (2.0 * my + vy + 0.5) / 128.0
            row = (trig(c1), trig(c2))
            w1, w2 = from_sines(row[0][1], row[0][0], row[1][1], row[1][0])
            f1 = 256.0 * (column[:, l:l + 128] + 0.5) - HALF
            for r in range(0, 64, ROWS):
                d1 = (doff[0, r:r + ROWS] + (jx - 0.5)) / 256.0
                d2 = (doff[1, r:r + ROWS] + (jy - 0.5)) / 256.0
                s1, s2 = speeds_sum(row, (trig(d1), trig(d2)))
                save(tabf, src, space_cycles(d1, d2, s1, s2, w1, w2, f1, f2),
                     slice(r, r + ROWS), slice(l, l + 128))
        return carry

    lax.fori_loop(0, 8, level5, 0)

    def run4(e, carry):
        half = lax.div(e, 8)
        src = lax.rem(lax.div(h, 4) + 1 + lax.rem(lax.div(e, 4), 2), 2) * 4 + lax.rem(h + e, 4)
        landed = y_ref.at[half, pl.ds(pl.multiple_of(src * 16, 16), 16)]
        pltpu.make_async_copy(landed, landed, recv2.at[half * 8 + src]).wait()
        for m in range(16):
            yy[pl.ds(m, 16, stride=16), :] = y_ref[half, src * 16 + m]
        hi, lo = split(yy[...])
        out = dot(tmat[...], jnp.concatenate([hi, lo], axis=1), NT_DIMS)
        out = out[:128] + out[128:]
        for l in range(0, 256, 128):
            there = pl.ds(pl.multiple_of(half * 256 + l, 128), 128)
            lanes = pl.ds(pl.multiple_of(src * 512 + half * 256 + l, 128), 128)
            for r in range(0, 64, ROWS):
                rows = slice(r, r + ROWS)
                re, im = turn(out[r:r + ROWS, l:l + 128], out[64 + r:64 + r + ROWS, l:l + 128],
                              tabf, src, rows, there)
                o_ref[0, rows, lanes] = re
                o_ref[1, rows, lanes] = im
        return carry

    lax.fori_loop(0, 16, run4, 0)
    sent = y_ref.at[:, pl.ds(0, n_all - 1)]
    pltpu.make_async_copy(sent, sent, send2).wait()
    for b in range(2):
        for i in range(1, 16):
            exchange1(b, i).wait_send()


VMEM_LIMIT = 60 * 1024 * 1024


def body(weights, owner_map, node_index):
    t1, t3, tf, off, off3 = constants()
    n_dev = lax.axis_size("dev")
    n_all = lax.axis_size("grp") * n_dev
    vmem = pl.BlockSpec(memory_space=pltpu.VMEM)
    hbm = pl.BlockSpec(memory_space=pltpu.HBM)
    dma = pltpu.SemaphoreType.DMA
    return pl.pallas_call(
        functools.partial(kernel, n_dev, n_all, n_all // 16),
        out_shape=pltpu.VMEM((2, 64, 4096), F32),
        in_specs=[vmem] * 2 + [hbm] * 6,
        out_specs=vmem,
        scratch_shapes=[
            pltpu.VMEM((2, 16, 2, 64, 128), F32),
            pltpu.VMEM(t1.shape, BF16),
            pltpu.VMEM(t3.shape, BF16),
            pltpu.VMEM(tf.shape, BF16),
            pltpu.VMEM(off.shape, F32),
            pltpu.VMEM(off3.shape, BF16),
            pltpu.VMEM((2, 8, 4, 16, 128), F32),
            pltpu.VMEM((2, 128, 16, 128), F32),
            pltpu.VMEM((64, 2, 64, 256), F32),
            pltpu.VMEM((64, 2, 64, 256), F32),
            pltpu.VMEM((16, 2, 64, 256), F32),
            pltpu.VMEM((8, 2, 64, 128), F32),
            pltpu.VMEM((32, 2, 64, 128), F32),
            pltpu.VMEM((8, 2, 64, 128), F32),
            pltpu.VMEM((8, 2, 64, 512), F32),
            pltpu.VMEM((4, 2, 64, 128), F32),
            pltpu.VMEM((64, 128), F32),
            pltpu.VMEM((2, 8, 64, 256), F32),
            pltpu.VMEM((64, 256), F32),
            pltpu.VMEM((2, 64, 128), F32),
            pltpu.VMEM((128, 256), BF16),
            pltpu.VMEM((4, 256, 256), BF16),
            pltpu.VMEM((4, 256, 256), BF16),
            pltpu.VMEM((16, 64, 256), F32),
            pltpu.VMEM((256, 1024), BF16),
            pltpu.VMEM((1024, 256), BF16),
            pltpu.VMEM((192, 512), BF16),
            pltpu.VMEM((8, 128, 128), F32),
            pltpu.VMEM((256, 256), BF16),
            pltpu.VMEM((256, 128), F32),
            dma((32,)),
            dma((32,)),
            dma(()),
            dma((16,)),
            dma((5,)),
            pltpu.SemaphoreType.REGULAR,
        ],
        compiler_params=pltpu.CompilerParams(
            vmem_limit_bytes=VMEM_LIMIT, collective_id=0, has_side_effects=True),
        name="butterfly",
    )(node_index, owner_map.reshape(1, 16), weights, t1, t3, tf, off, off3)


def solution(mesh):
    in_specs = (P(None, None, ("grp", "dev")), P(), P())
    out_specs = P(None, None, ("grp", "dev"))
    return jax.shard_map(body, mesh=mesh, in_specs=in_specs, out_specs=out_specs, check_vma=False)
```

```python
import functools
import math

import jax
import jax.numpy as jnp
import numpy as np
from jax import lax
from jax.experimental import pallas as pl
from jax.experimental.pallas import tpu as pltpu
from jax.sharding import PartitionSpec as P

F32 = jnp.float32
BF16 = jnp.bfloat16
HALF = 2048.0
NT_DIMS = (((1,), (1,)), ((), ()))
TN_DIMS = (((0,), (0,)), ((), ()))
NN_DIMS = (((1,), (0,)), ((), ()))


def fit(function, count):
    angle = (np.arange(64) + 0.5) * np.pi / 64
    points = 0.125 + 0.125 * np.cos(angle)
    cheb = np.polynomial.chebyshev.Chebyshev.fit(
        points, function(np.sqrt(points)), count - 1, domain=[0.0, 0.25]
    )
    return [float(c) for c in cheb.convert(kind=np.polynomial.Polynomial).coef]


ROOT2 = math.sqrt(2.0)
SIN_COEF = fit(lambda r: ROOT2 * np.sin(np.pi * r) / r, 5)
COS_COEF = fit(lambda r: ROOT2 * np.cos(np.pi * r), 5)


def horner(coef, u):
    total = coef[-1] * u + coef[-2]
    for c in coef[-3::-1]:
        total = total * u + c
    return total


def trig(cycles):
    r = cycles - jnp.round(cycles)
    u = r * r
    s = horner(SIN_COEF, u) * r
    c = horner(COS_COEF, u)
    return 1.0 - s * s, s * c


def cheb_nodes():
    return 0.5 * np.cos(np.pi * (2.0 * np.arange(8) + 1.0) / 16.0)


def canon_tables():
    z = cheb_nodes()
    basis = np.zeros((2, 8, 8))
    for c in range(2):
        places = z / 2 + c / 2 - 0.25
        for i in range(8):
            value = np.ones(8)
            for k in range(8):
                if k != i:
                    value = value * (places - z[k]) / (z[i] - z[k])
            basis[c, i] = value
    return [np.kron(basis[c % 2], basis[c // 2]) for c in range(4)]


def split_np(a):
    hi = np.asarray(a, np.float32).astype(BF16)
    lo = (np.asarray(a, np.float64) - hi.astype(np.float64)).astype(np.float32).astype(BF16)
    return hi, lo


def constants():
    z = cheb_nodes().astype(np.float32)
    tables = canon_tables()
    t_in = np.concatenate(tables, axis=1)
    t_out = np.concatenate([t.T for t in tables], axis=0)
    in_h, in_l = split_np(t_in)
    out_h, out_l = split_np(t_out)
    t1 = np.concatenate([in_h, in_l], axis=0)
    t3 = np.concatenate([out_h, out_h, out_l], axis=1)
    tf = np.stack([out_h, out_l])
    ox = np.repeat(z, 8)
    oy = np.tile(z, 8)
    off = np.stack([np.broadcast_to(o[:, None], (64, 128)) for o in (ox, oy)])
    pieces = []
    rest = off.astype(np.float32)
    for _ in range(3):
        piece = rest.astype(BF16)
        pieces.append(piece)
        rest = rest - piece.astype(np.float32)
    return t1, t3, tf, np.ascontiguousarray(off, np.float32), np.stack(pieces)


def fiota(shape, axis):
    return lax.broadcasted_iota(jnp.int32, shape, axis)


def node_onehot(node_ref):
    flat = node_ref[0:1, :] * 8 + node_ref[1:2, :]
    return (fiota((64, 64), 0) == flat).astype(F32).astype(BF16)


def dot(a, b, dims=NN_DIMS):
    return lax.dot_general(a, b, dims, preferred_element_type=F32)


def split(x):
    hi = x.astype(BF16)
    return hi, (x - hi.astype(F32)).astype(BF16)


def from_sines(s1, c1, s2, c2):
    one = (2.0 + s1 * s2) * 0.0625
    two = (2.0 + c1 * c2) * 0.0625
    return one * one, two * two


def speeds(x1, x2):
    c1, s1 = trig(x1)
    c2, s2 = trig(x2)
    return from_sines(s1, c1, s2, c2)


def speeds_sum(row, col):
    sines = []
    for (ca, sa), (cb, sb) in zip(row, col):
        sines += [sa * cb + ca * sb, ca * cb - sa * sb]
    return from_sines(*sines)


def root(x):
    return x * lax.rsqrt(x)


def freq_columns(d1, d2, a1, a2, v1, v2):
    e1 = v1 * d1
    e2 = v2 * d2
    linear = a2 * d2 if isinstance(a1, float) and a1 == 0.0 else a1 * d1 + a2 * d2
    return 2.0 * e1, 2.0 * e2, e1 * d1 + e2 * d2, linear


def freq_row(g1, g2, v1, v2):
    square = v1 * g1 * g1 + v2 * g2 * g2 + 1.0
    return g1, g2, square, root(square)


def freq_cycles(columns, row):
    e1, e2, e0, linear = columns
    g1, g2, square, base = row
    numer = e1 * g1 + e2 * g2 + e0
    return linear + numer / (root(square + numer) + base)


def space_cycles(d1, d2, v1, v2, w1, w2, f1, f2):
    q1 = f1 * f1
    q2 = f2 * f2
    base = w1 * q1 + w2 * q2 + 1.0
    numer = (v1 - w1) * q1 + (v2 - w2) * q2
    return d1 * f1 + d2 * f2 + numer / (root(base + numer) + root(base))


ROWS = 32
MESH = pl.DeviceIdType.MESH


def bit(value, place):
    return lax.rem(lax.div(value, 1 << place), 2)


def tofloat(value):
    return value.astype(F32)


def splat(value):
    return jnp.full((1, 128), value, F32)


def save(tab, index, cycles, rows, lanes):
    cs, sn = trig(cycles)
    tab[index, 0, rows, lanes] = cs
    tab[index, 1, rows, lanes] = sn


def turn(re, im, tab, index, rows, lanes):
    cs = tab[index, 0, rows, lanes]
    sn = tab[index, 1, rows, lanes]
    return re * cs - im * sn, re * sn + im * cs


def columns_of(owner_ref, slot):
    owner = (owner_ref[0:1, :] == slot).astype(F32).astype(BF16)
    numbers = fiota((8, 16), 1).astype(F32).astype(BF16)
    return dot(numbers, owner, NT_DIMS)[0:1, :], owner


def kernel(n_dev, n_all, n_group, node_ref, owner_ref, w_hbm, t1_hbm, t3_hbm, tf_hbm, off_hbm, off3_hbm,
           o_ref, e_ref, x_ref, t1_ref, t3_ref, tf_ref, off_ref, off3_ref, z_ref, y_ref, tab1, tab2,
           tabm, tab3i, tab3o, tab4i, tabf, lin2, line, prod, part, doff, t1s, xh, xl, y1, y2, wmat, x3, v4, tmat,
           yy, send1, recv1, sea, ea, seb, eb, sec, ec, sxa,
           xa, sxb, xb, local, ready):
    flat = lax.axis_index("grp") * n_dev + lax.axis_index("dev")
    h = lax.div(flat, 16)
    ry = lax.rem(flat, 16)
    hf = tofloat(h)
    ryf = tofloat(ry)

    def place(device):
        return lax.div(device, n_dev), lax.rem(device, n_dev)

    barrier = pltpu.get_barrier_semaphore()

    def tell(semaphore, device):
        pl.semaphore_signal(semaphore, inc=1, device_id=place(device), device_id_type=MESH)

    for i in range(1, 16):
        tell(barrier, h * 16 + lax.rem(ry + i, 16))
    for g in range(1, n_group):
        tell(barrier, lax.rem(h + g, n_group) * 16 + ry)
    loads = [pltpu.make_async_copy(a, b, local.at[i]) for i, (a, b) in enumerate(
        [(t1_hbm, t1_ref), (t3_hbm, t3_ref), (tf_hbm, tf_ref), (off_hbm, off_ref),
         (off3_hbm, off3_ref)])]
    for load in loads:
        load.start()
    for load in loads:
        load.wait()

    onehot = node_onehot(node_ref)
    for axis in range(2):
        doff[axis] = sum(dot(onehot, off3_ref[p, axis], TN_DIMS) for p in (2, 1, 0))
    for c in range(4):
        t1s[:, c * 64:(c + 1) * 64] = dot(t1_ref[:, c * 64:(c + 1) * 64], onehot).astype(BF16)

    lane = [fiota((1, 128), 1) + k for k in (0, 128)]
    bx = [tofloat(lax.rem(v, 64)) for v in lane]
    by = [4.0 * ryf + tofloat(lax.div(v, 64)) for v in lane]

    def products(index, offsets, scale, shift, width, child):
        for l in range(0, 256, 128):
            for axis, at in ((0, bx[l // 128]), (1, by[l // 128])):
                g = width * at + child - HALF
                for r in range(0, 64, ROWS):
                    d = scale * offsets[axis, r:r + ROWS] + shift
                    prod[axis, index, r:r + ROWS, l:l + 128] = d * (2.0 * g + d)

    def products1(i, carry):
        child = tofloat(lax.div(i, 2))
        products(i, doff, 16.0, 16.0 * (child - 0.5), 64.0, 32.0 * (tofloat(lax.rem(i, 2)) + 0.5))
        return carry

    def products2(i, carry):
        products(4 + i, off_ref, 32.0, 32.0 * (tofloat(i) - 0.5), 64.0, 32.0)
        products(6 + i, off_ref, 32.0, 0.0, 64.0, 32.0 * (tofloat(i) + 0.5))
        return carry

    lax.fori_loop(0, 4, products1, 0)
    lax.fori_loop(0, 2, products2, 0)

    def linear2(i, carry):
        ux = tofloat(lax.div(i, 2))
        a1 = (2.0 * hf + ux + 0.5) / 32.0
        b1 = (4.0 * hf + 2.0 * ux + tofloat(lax.rem(i, 2)) + 0.5) / 64.0
        for r in range(0, 64, ROWS):
            rows = slice(r, r + ROWS)
            o = off_ref[0, rows]
            save(lin2, i, 32.0 * (a1 * o - b1 * (o - 0.5)), rows, slice(0, 128))
        return carry

    lax.fori_loop(0, 4, linear2, 0)

    n = fiota((1, 128), 1)
    nrow = fiota((128, 16), 0)
    column, owner = columns_of(owner_ref, 2 * lax.div(nrow, 16) + lax.rem(nrow, 2))
    erow = fiota((128, 16), 0)
    picks = (lax.rem(lax.div(erow, 4), 16) == fiota((128, 16), 1)).astype(F32).astype(BF16)
    wcol = dot(picks, owner, NT_DIMS)
    wu = lax.rem(lax.div(fiota((128, 128), 1), 2), 8)
    for v in range(2):
        keep = jnp.where(lax.rem(lax.div(fiota((128, 128), 0), 2), 2) == v, wcol, 0.0)
        for u in range(8):
            wmat[u * 128:(u + 1) * 128, v * 128:(v + 1) * 128] = jnp.where(
                wu == u, keep, 0.0).astype(BF16)

    u8 = lax.rem(lax.div(n, 2), 8)

    def parent(u):
        u1 = lax.rem(u, 4)
        u2 = lax.div(u, 4)
        return (tofloat(2 * lax.rem(u1, 2) + lax.rem(u2, 2)),
                tofloat(2 * lax.div(u1, 2) + lax.div(u2, 2)))

    pl.semaphore_wait(barrier, 14 + n_group)
    for g in range(1, n_group):
        tell(ready, lax.rem(h + g, n_group) * 16 + ry)

    def chunk(m, b):
        return w_hbm.at[:, :, pl.ds(pl.multiple_of(m * 256 + b * 128, 128), 128)]

    def exchange1(b, i):
        m = (lax.rem(lax.div(ry, 8) + i // 8, 2) * 8
             + lax.rem(lax.div(lax.rem(ry, 8), 2) + i // 2 % 4, 4) * 2 + lax.rem(ry + i, 2))
        return pltpu.make_async_remote_copy(
            src_ref=chunk(m, b), dst_ref=x_ref.at[b, ry], send_sem=send1.at[b * 16 + i],
            recv_sem=recv1.at[b * 16 + i], device_id=place(h * 16 + m), device_id_type=MESH)

    for b in range(2):
        for i in range(1, 16):
            exchange1(b, i).start()
    own1 = [pltpu.make_async_copy(chunk(ry, b), x_ref.at[b, ry], recv1.at[b * 16])
            for b in range(2)]
    for copy in own1:
        copy.start()

    def freq_rest(row, ix, iy, v1, v2, rows, lanes):
        square, base = row
        numer = v1 * prod[0, ix, rows, lanes] + v2 * prod[1, iy, rows, lanes]
        return numer / (root(square + numer) + base)

    def level1(i, carry):
        c = lax.rem(i, 4)
        u1 = lax.div(i, 4)
        a1 = (2.0 * hf + tofloat(bit(u1, 0)) + 0.5) / 32.0
        a2 = (tofloat(bit(u1, 1)) + 0.5) / 32.0
        v1, v2 = speeds(splat(a1), splat(a2))
        sx = 16.0 * (tofloat(bit(c, 0)) - 0.5)
        sy = 16.0 * (tofloat(bit(c, 1)) - 0.5)
        for r in range(0, 64, ROWS):
            line[r:r + ROWS] = -(a1 * (sx + 16.0 * doff[0, r:r + ROWS])
                                 + a2 * (sy + 16.0 * doff[1, r:r + ROWS]))

        def inner(u2, carry):
            for l in range(0, 256, 128):
                k = l // 128
                row = freq_row(32.0 * (2.0 * bx[k] + tofloat(bit(u2, 0)) + 0.5) - HALF,
                               32.0 * (2.0 * by[k] + tofloat(bit(u2, 1)) + 0.5) - HALF, v1, v2)
                for r in range(0, 64, ROWS):
                    rows = slice(r, r + ROWS)
                    lanes = slice(l, l + 128)
                    rest = freq_rest(row[2:], 2 * bit(c, 0) + bit(u2, 0),
                                     2 * bit(c, 1) + bit(u2, 1), v1, v2, rows, lanes)
                    save(tab1, i * 4 + u2, line[rows] - rest, rows, lanes)
            return carry

        lax.fori_loop(0, 4, inner, 0, unroll=2)
        return carry

    lax.fori_loop(0, 16, level1, 0)

    mirror = fiota((ROWS, 128), 1)
    mirror = lax.div(mirror, 64) * 64 + 63 - lax.rem(mirror, 64)

    def mirrored(tab, index, other, cycles, lin, which, r, lanes):
        cs, sn = trig(cycles)
        cl = lin[which, 0, r:r + ROWS]
        sl = lin[which, 1, r:r + ROWS]
        p, q, s, t = cs * cl, sn * sl, sn * cl, cs * sl
        tab[index, 0, r:r + ROWS, lanes] = p - q
        tab[index, 1, r:r + ROWS, lanes] = s + t
        for part_id, value in enumerate((p + q, s - t)):
            value = jnp.take_along_axis(value, mirror, axis=1, mode="promise_in_bounds")
            for k in range(0, ROWS, 8):
                to = 56 - r - k
                tab[other, part_id, to:to + 8, lanes] = value[k:k + 8]

    def level2(i, carry):
        u1 = lax.div(i, 2)
        a1 = (2.0 * hf + tofloat(bit(u1, 0)) + 0.5) / 32.0
        a2 = (tofloat(bit(u1, 1)) + 0.5) / 32.0
        v1, v2 = speeds(splat(a1), splat(a2))
        cy = tofloat(lax.rem(i, 2))
        cyi = lax.rem(i, 2)
        for r in range(0, 64, ROWS):
            rows = slice(r, r + ROWS)
            for l in range(0, 256, 128):
                k = l // 128
                lanes = slice(l, l + 128)
                row = freq_row(32.0 * (2.0 * bx[k] + 0.5) - HALF,
                               32.0 * (2.0 * by[k] + cy + 0.5) - HALF, v1, v2)
                part[rows, lanes] = (a2 * (32.0 * off_ref[1, rows])
                                     + freq_rest(row[2:], 6, 6 + cyi, v1, v2, rows, lanes))
        index = (u1 * 4 + 2 * cyi) * 4

        def inner(u2, carry):
            b1 = (4.0 * hf + 2.0 * tofloat(bit(u1, 0)) + tofloat(bit(u2, 0)) + 0.5) / 64.0
            b2 = (2.0 * tofloat(bit(u1, 1)) + tofloat(bit(u2, 1)) + 0.5) / 64.0
            w1, w2 = speeds(splat(b1), splat(b2))
            for l in range(0, 256, 128):
                k = l // 128
                lanes = slice(l, l + 128)
                row = freq_row(64.0 * (bx[k] + 0.5) - HALF, 64.0 * (by[k] + 0.5) - HALF, w1, w2)
                for r in range(0, 64, ROWS):
                    rows = slice(r, r + ROWS)
                    rest = freq_rest(row[2:], 4, 4 + cyi, w1, w2, rows, lanes)
                    down = (b2 * 32.0) * (off_ref[1, rows] + (cy - 0.5))
                    mirrored(tab2, index + u2, index + 4 + u2, part[rows, lanes] - down - rest,
                             lin2, bit(u1, 0) * 2 + bit(u2, 0), r, lanes)
            return carry

        lax.fori_loop(0, 4, inner, 0, unroll=2)
        return carry

    lax.fori_loop(0, 8, level2, 0)

    def middle(u, carry):
        u1 = lax.rem(u, 4)
        u2 = lax.div(u, 4)
        b1 = (4.0 * hf + 2.0 * tofloat(bit(u1, 0)) + tofloat(bit(u2, 0)) + 0.5) / 64.0
        b2 = (2.0 * tofloat(bit(u1, 1)) + tofloat(bit(u2, 1)) + 0.5) / 64.0
        w1, w2 = speeds(splat(b1), splat(b2))
        rows = [freq_row(64.0 * (bx[k] + 0.5) - HALF, 64.0 * (by[k] + 0.5) - HALF, w1, w2)
                for k in range(2)]
        for r in range(0, 64, ROWS):
            cols = freq_columns(64.0 * off_ref[0, r:r + ROWS], 64.0 * off_ref[1, r:r + ROWS],
                                b1, b2, w1, w2)
            for l in range(0, 256, 128):
                save(tabm, u, freq_cycles(cols, rows[l // 128]), slice(r, r + ROWS),
                     slice(l, l + 128))
        return carry

    lax.fori_loop(0, 16, middle, 0, unroll=2)

    def level3(half, carry):
        mx, my = parent(u8 + 8 * half)
        p1 = (4.0 * hf + mx + 0.5) / 64.0
        p2 = (my + 0.5) / 64.0
        row = (trig(p1), trig(p2))
        w1, w2 = from_sines(row[0][1], row[0][0], row[1][1], row[1][0])
        for r in range(0, 64, ROWS):
            rows = slice(r, r + ROWS)
            d1 = off_ref[0, rows] / 64.0
            d2 = off_ref[1, rows] / 64.0
            s1, s2 = speeds_sum(row, (trig(d1), trig(d2)))
            for v in range(4):
                f1 = 128.0 * (2.0 * column + (v % 2) + 0.5) - HALF
                f2 = 128.0 * (2.0 * ryf + (v // 2) + 0.5) - HALF
                cycles = space_cycles(d1, d2, s1, s2, w1, w2, f1, f2)
                save(tab3i, half * 4 + v, -cycles, rows, slice(0, 128))
        return carry

    lax.fori_loop(0, 2, level3, 0)

    def level4(i, carry):
        half = lax.div(i, 4)
        jx = tofloat(bit(lax.rem(i, 4), 0))
        jy = tofloat(bit(lax.rem(i, 4), 1))
        mx, my = parent(u8 + 8 * half)
        mx = 4.0 * hf + mx
        w1, w2 = speeds((mx + 0.5) / 64.0, (my + 0.5) / 64.0)
        c1 = (2.0 * mx + jx + 0.5) / 128.0
        c2 = (2.0 * my + jy + 0.5) / 128.0
        row = (trig(c1), trig(c2))
        z1, z2 = from_sines(row[0][1], row[0][0], row[1][1], row[1][0])
        for r in range(0, 64, ROWS):
            rows = slice(r, r + ROWS)
            d1 = off_ref[0, rows] / 128.0
            d2 = off_ref[1, rows] / 128.0
            s1, s2 = speeds_sum(row, (trig(d1), trig(d2)))
            e1 = d1 + (jx - 0.5) / 128.0
            e2 = d2 + (jy - 0.5) / 128.0
            for v in range(4):
                f1 = 128.0 * (2.0 * column + (v % 2) + 0.5) - HALF
                f2 = 128.0 * (2.0 * ryf + (v // 2) + 0.5) - HALF
                cycles = space_cycles(e1, e2, s1, s2, w1, w2, f1, f2)
                save(tab3o, i * 4 + v, cycles, rows, slice(0, 128))
            f1 = 256.0 * (column + 0.5) - HALF
            f2 = 256.0 * (ryf + 0.5) - HALF
            cycles = space_cycles(d1, d2, s1, s2, z1, z2, f1, f2)
            save(tab4i, i, -cycles, rows, slice(0, 128))
        return carry

    lax.fori_loop(0, 8, level4, 0)

    yi = lax.div(flat, 32)
    x0 = lax.rem(lax.div(flat, 8), 4)
    zc = lax.rem(flat, 8)
    z0 = lax.div(zc, 2)
    c0 = lax.rem(zc, 2)
    x1 = x0 + 1 - 2 * lax.rem(x0, 2)

    def at_device(y, x, m):
        return place(y * 32 + x * 8 + m)

    def near(x, o):
        return 3 - x if o else x

    def remote(source, target, sender, receiver, device):
        return pltpu.make_async_remote_copy(
            src_ref=source, dst_ref=target, send_sem=sender, recv_sem=receiver,
            device_id=device, device_id_type=MESH)

    def arrive(ref, semaphore):
        pltpu.make_async_copy(ref, ref, semaphore).wait()

    pairs_of = [(t, o) for t in (2, 1, 3, 0) for o in (1, 0)]

    def spread(d):
        return lax.rem(z0 + d // 2, 4) * 2 + lax.rem(c0 + d, 2)

    def e_first():
        for t, o in pairs_of:
            yk = lax.rem(yi + t, 4)
            xk = near(x0, o)
            block = z_ref.at[0, yk * 2 + lax.div(xk, 2)]
            s = o * 4 + t
            if s == 0:
                pltpu.make_async_copy(block, e_ref.at[yi, x0], ea.at[s]).start()
            else:
                remote(block, e_ref.at[yi, x0], sea.at[s], ea.at[s],
                       at_device(yk, xk, zc)).start()

    def x_first():
        for t, o in pairs_of:
            yk = lax.rem(yi + t, 4)
            xk = near(x0, o)
            k = yk * 2 + lax.div(xk, 2)
            s = o * 4 + t
            for d in (4, 5, 2, 3, 6, 7, 0, 1):
                m = spread(d)
                block = z_ref.at[1, k, lax.rem(m, 4)]
                if s == 0 and d == 0:
                    pltpu.make_async_copy(block, y_ref.at[1, yi, x0, zc], xa.at[s]).start()
                else:
                    remote(block, y_ref.at[1, yi, x0, zc], sxa.at[s], xa.at[s],
                           at_device(yk, xk, m)).start()

    def e_pass():
        for t, o in pairs_of:
            s = o * 4 + t
            block = e_ref.at[lax.rem(yi + 4 - t, 4), near(x0, o)]
            arrive(block, ea.at[s])
            remote(block, block, seb.at[s], eb.at[s], at_device(yi, x1, zc)).start()

    def x_pass():
        for t, o in pairs_of:
            s = o * 4 + t
            block = y_ref.at[1, lax.rem(yi + 4 - t, 4), near(x0, o)]
            arrive(block, xa.at[s])
            remote(block, block, sxb.at[s], xb.at[s], at_device(yi, x1, zc)).start()

    def e_last(x, o):
        xs = near(x, o)
        for d in (4, 5, 2, 3, 6, 7, 1, 0):
            m = spread(d)
            block = e_ref.at[:, xs, lax.rem(m, 4)]
            if d == 0:
                pltpu.make_async_copy(block, y_ref.at[0, :, xs, zc], ec.at[xs]).start()
            else:
                remote(block, y_ref.at[0, :, xs, zc], sec, ec.at[xs],
                       at_device(yi, x0, m)).start()

    def send_half(half):
        pl.when(half == 0)(e_first)
        pl.when(half == 1)(x_first)

    def stage(b):
        at = slice(b * 128, b * 128 + 128)
        whole = slice(0, 128)

        def turned(slot, source, tab, index):
            for c in range(4):
                for r in range(0, 64, ROWS):
                    rows = slice(r, r + ROWS)
                    re, im = source(c, rows)
                    parts = turn(re, im, tab, index(c), rows, at)
                    for p in range(2):
                        hi, lo = split(parts[p])
                        xh[slot, c * 64 + r:c * 64 + r + ROWS, p * 128:p * 128 + 128] = hi
                        xl[slot, c * 64 + r:c * 64 + r + ROWS, p * 128:p * 128 + 128] = lo

        def mixed(slot, table):
            first = dot(table[...], xh[slot])
            return first[:64] + first[64:] + dot(table[0:64], xl[slot])

        def run1(e, carry):
            ux = lax.rem(lax.div(ry, 8) + lax.div(e, 2), 2)
            uz = lax.rem(lax.div(ry, 4) + e, 2)
            u2 = 2 * ux + uz
            for c in range(4):
                i = (lax.rem(lax.div(ry, 8) + ux, 2) * 8
                     + lax.rem(lax.div(lax.rem(ry, 8), 2) + 4 - 2 * uz - c // 2, 4) * 2
                     + lax.rem(ry + c, 2))
                landed = x_ref.at[b, u2 * 4 + c]
                pltpu.make_async_copy(landed, landed, recv1.at[b * 16 + i]).wait()
            for u1 in range(4):
                turned(u1, lambda c, rows: (x_ref[b, u2 * 4 + c, 0, rows],
                                            x_ref[b, u2 * 4 + c, 1, rows]),
                       tab1, lambda c: (u1 * 4 + c) * 4 + u2)
                y1[u1 * 4 + u2] = mixed(u1, t1s)
            return carry

        lax.fori_loop(0, 4, run1, 0)

        def run2(half, pair):
            for slot in range(4):
                u1 = 2 * pair + slot // 2
                u2 = 2 * half + slot % 2
                u = u1 + 4 * u2
                turned(slot, lambda c, rows: (y1[u1 * 4 + c, rows, 0:128],
                                              y1[u1 * 4 + c, rows, 128:256]),
                       tab2, lambda c: (u1 * 4 + c) * 4 + u2)
                out = mixed(slot, t1_ref)
                to = pl.ds(pl.multiple_of((u1 + 4 * (slot % 2)) * 128, 128), 128)
                for r in range(0, 64, ROWS):
                    rows = slice(r, r + ROWS)
                    parts = turn(out[rows, 0:128], out[rows, 128:256], tabm, u, rows, at)
                    for p in range(2):
                        hi, lo = split(parts[p])
                        y2[p * 64 + r:p * 64 + r + ROWS, to] = hi
                        y2[128 + p * 64 + r:128 + p * 64 + r + ROWS, to] = lo

        def run3(half):
            both = dot(y2[...], wmat[...])
            summed = both[:128] + both[128:]
            for v in range(2):
                for r in range(0, 64, ROWS):
                    rows = slice(r, r + ROWS)
                    l = v * 128
                    parts = turn(summed[r:r + ROWS, l:l + 128],
                                 summed[64 + r:64 + r + ROWS, l:l + 128], tab3i,
                                 half * 4 + 2 * b + v, rows, whole)
                    for p in range(2):
                        hi, lo = split(parts[p])
                        to = slice((v * 2 + p) * 128, (v * 2 + p + 1) * 128)
                        x3[r:r + ROWS, to] = hi
                        x3[64 + r:64 + r + ROWS, to] = lo
                        x3[128 + r:128 + r + ROWS, to] = hi
            for j in range(4):
                out = dot(t3_ref[j * 64:(j + 1) * 64], x3[...])
                for r in range(0, 64, ROWS):
                    rows = slice(r, r + ROWS)
                    low = slice(64 + r, 64 + r + ROWS)
                    if b == 1:
                        re, im = v4[half * 4 + j, rows], v4[half * 4 + j, low]
                    for v in range(2):
                        l = v * 256
                        p, q = turn(out[rows, l:l + 128], out[rows, l + 128:l + 256], tab3o,
                                    (half * 4 + j) * 4 + 2 * b + v, rows, whole)
                        first = b == 0 and v == 0
                        re = p if first else re + p
                        im = q if first else im + q
                    if b == 1:
                        re, im = turn(re, im, tab4i, half * 4 + j, rows, whole)
                    v4[half * 4 + j, rows] = re
                    v4[half * 4 + j, low] = im
                if b == 1:
                    flipped = v4[half * 4 + j].T
                    for k in range(8):
                        z_ref[half, k, j] = flipped[k * 16:(k + 1) * 16]

        def run(half, carry):
            def pairs(pair, carry):
                run2(half, pair)
                return carry

            lax.fori_loop(0, 2, pairs, 0)
            run3(half)
            if b == 1:
                send_half(half)
            return carry

        lax.fori_loop(0, 2, run, 0)

    for b in range(2):
        if b == 1:
            pl.semaphore_wait(ready, n_group - 1)
        stage(b)

    e_pass()
    e_last(x0, 0)
    e_last(x0, 1)
    x_pass()
    for o in range(2):
        for t in (2, 1, 3, 0):
            arrive(e_ref.at[lax.rem(yi + 4 - t, 4), near(x1, o)], eb.at[o * 4 + t])
        e_last(x1, o)

    v1d = lax.rem(ry, 4)
    v2d = lax.div(ry, 4)
    zero = jnp.zeros((64, 64), BF16)
    pieces = [dot(onehot, tf_ref[p, pl.ds(pl.multiple_of(v2d * 64, 64), 64), :],
                  TN_DIMS).astype(BF16) for p in range(2)]
    for p in range(2):
        for q in range(2):
            for piece in range(2):
                for low in range(2):
                    lanes = slice(low * 128 + q * 64, low * 128 + q * 64 + 64)
                    rows = slice(piece * 128 + p * 64, piece * 128 + p * 64 + 64)
                    use = p == q and not (piece == 1 and low == 1)
                    tmat[rows, lanes] = pieces[piece] if use else zero
    ids = fiota((512, 16), 0)
    column, _ = columns_of(owner_ref, 2 * h + lax.rem(lax.div(ids, 16), 2))
    jx, jy = tofloat(lax.rem(v2d, 2)), tofloat(lax.div(v2d, 2))
    vx, vy = tofloat(lax.rem(v1d, 2)), tofloat(lax.div(v1d, 2))
    f2 = 256.0 * (tofloat(lax.rem(n, 16)) + 0.5) - HALF

    def level5(src, carry):
        for l in range(0, 512, 128):
            mx, my = parent(lax.div(n + l, 32))
            c1 = (2.0 * (4.0 * tofloat(src) + mx) + vx + 0.5) / 128.0
            c2 = (2.0 * my + vy + 0.5) / 128.0
            row = (trig(c1), trig(c2))
            w1, w2 = from_sines(row[0][1], row[0][0], row[1][1], row[1][0])
            f1 = 256.0 * (column[:, l:l + 128] + 0.5) - HALF
            for r in range(0, 64, ROWS):
                d1 = (doff[0, r:r + ROWS] + (jx - 0.5)) / 256.0
                d2 = (doff[1, r:r + ROWS] + (jy - 0.5)) / 256.0
                s1, s2 = speeds_sum(row, (trig(d1), trig(d2)))
                save(tabf, src, space_cycles(d1, d2, s1, s2, w1, w2, f1, f2),
                     slice(r, r + ROWS), slice(l, l + 128))
        return carry

    lax.fori_loop(0, 8, level5, 0)

    def run4(half, src):
        for m in range(16):
            yy[pl.ds(m, 16, stride=16), :] = y_ref[half, lax.div(src, 2),
                                                  lax.rem(src, 2) * 2 + m // 8, m % 8]
        hi, lo = split(yy[...])
        out = dot(tmat[...], jnp.concatenate([hi, lo], axis=1), NT_DIMS)
        out = out[:128] + out[128:]
        for l in range(0, 256, 128):
            there = slice(half * 256 + l, half * 256 + l + 128)
            lanes = pl.ds(pl.multiple_of(src * 512 + half * 256 + l, 128), 128)
            for r in range(0, 64, ROWS):
                rows = slice(r, r + ROWS)
                re, im = turn(out[r:r + ROWS, l:l + 128], out[64 + r:64 + r + ROWS, l:l + 128],
                              tabf, src, rows, there)
                o_ref[0, rows, lanes] = re
                o_ref[1, rows, lanes] = im

    for o in range(2):
        pair = lax.div(near(x0, o), 2)

        def half1(t, carry):
            ys = lax.rem(yi + 4 - t, 4)
            arrive(y_ref.at[1, ys, near(x1, o)], xb.at[o * 4 + t])
            run4(1, ys * 2 + pair)
            return carry

        def half0(ys, carry):
            run4(0, ys * 2 + pair)
            return carry

        lax.fori_loop(0, 4, half1, 0)
        for x in (x0, x1):
            arrive(y_ref.at[0, :, near(x, o)], ec.at[near(x, o)])
        lax.fori_loop(0, 4, half0, 0)
    sent = y_ref.at[0, :, :, pl.ds(0, 7)]
    arrive(sent, sec)
    for s in range(8):
        if s > 0:
            arrive(e_ref.at[0, 0], sea.at[s])
            arrive(y_ref.at[1, 0, 0], sxa.at[s])
        arrive(e_ref.at[0, 0], seb.at[s])
        arrive(y_ref.at[1, 0, 0], sxb.at[s])
    arrive(y_ref.at[1, 0, 0, pl.ds(0, 7)], sxa.at[0])
    for b in range(2):
        for i in range(1, 16):
            exchange1(b, i).wait_send()


VMEM_LIMIT = 60 * 1024 * 1024


def body(weights, owner_map, node_index):
    t1, t3, tf, off, off3 = constants()
    n_dev = lax.axis_size("dev")
    n_all = lax.axis_size("grp") * n_dev
    vmem = pl.BlockSpec(memory_space=pltpu.VMEM)
    hbm = pl.BlockSpec(memory_space=pltpu.HBM)
    dma = pltpu.SemaphoreType.DMA
    return pl.pallas_call(
        functools.partial(kernel, n_dev, n_all, n_all // 16),
        out_shape=pltpu.VMEM((2, 64, 4096), F32),
        in_specs=[vmem] * 2 + [hbm] * 6,
        out_specs=vmem,
        scratch_shapes=[
            pltpu.VMEM((4, 4, 4, 16, 128), F32),
            pltpu.VMEM((2, 16, 2, 64, 128), F32),
            pltpu.VMEM(t1.shape, BF16),
            pltpu.VMEM(t3.shape, BF16),
            pltpu.VMEM(tf.shape, BF16),
            pltpu.VMEM(off.shape, F32),
            pltpu.VMEM(off3.shape, BF16),
            pltpu.VMEM((2, 8, 4, 16, 128), F32),
            pltpu.VMEM((2, 4, 4, 8, 16, 128), F32),
            pltpu.VMEM((64, 2, 64, 256), F32),
            pltpu.VMEM((64, 2, 64, 256), F32),
            pltpu.VMEM((16, 2, 64, 256), F32),
            pltpu.VMEM((8, 2, 64, 128), F32),
            pltpu.VMEM((32, 2, 64, 128), F32),
            pltpu.VMEM((8, 2, 64, 128), F32),
            pltpu.VMEM((8, 2, 64, 512), F32),
            pltpu.VMEM((4, 2, 64, 128), F32),
            pltpu.VMEM((64, 128), F32),
            pltpu.VMEM((2, 8, 64, 256), F32),
            pltpu.VMEM((64, 256), F32),
            pltpu.VMEM((2, 64, 128), F32),
            pltpu.VMEM((128, 256), BF16),
            pltpu.VMEM((4, 256, 256), BF16),
            pltpu.VMEM((4, 256, 256), BF16),
            pltpu.VMEM((16, 64, 256), F32),
            pltpu.VMEM((256, 1024), BF16),
            pltpu.VMEM((1024, 256), BF16),
            pltpu.VMEM((192, 512), BF16),
            pltpu.VMEM((8, 128, 128), F32),
            pltpu.VMEM((256, 256), BF16),
            pltpu.VMEM((256, 128), F32),
            dma((32,)),
            dma((32,)),
            dma((8,)),
            dma((8,)),
            dma((8,)),
            dma((8,)),
            dma(()),
            dma((4,)),
            dma((8,)),
            dma((8,)),
            dma((8,)),
            dma((8,)),
            dma((5,)),
            pltpu.SemaphoreType.REGULAR,
        ],
        compiler_params=pltpu.CompilerParams(
            vmem_limit_bytes=VMEM_LIMIT, collective_id=0, has_side_effects=True),
        name="butterfly",
    )(node_index, owner_map.reshape(1, 16), weights, t1, t3, tf, off, off3)


def solution(mesh):
    in_specs = (P(None, None, ("grp", "dev")), P(), P())
    out_specs = P(None, None, ("grp", "dev"))
    return jax.shard_map(body, mesh=mesh, in_specs=in_specs, out_specs=out_specs, check_vma=False)
```

```python
import functools
import math

import jax
import jax.numpy as jnp
import numpy as np
from jax import lax
from jax.experimental import pallas as pl
from jax.experimental.pallas import tpu as pltpu
from jax.sharding import PartitionSpec as P

F32 = jnp.float32
BF16 = jnp.bfloat16
HALF = 2048.0
NT_DIMS = (((1,), (1,)), ((), ()))
TN_DIMS = (((0,), (0,)), ((), ()))
NN_DIMS = (((1,), (0,)), ((), ()))


def fit(function, count):
    angle = (np.arange(64) + 0.5) * np.pi / 64
    points = 0.125 + 0.125 * np.cos(angle)
    cheb = np.polynomial.chebyshev.Chebyshev.fit(
        points, function(np.sqrt(points)), count - 1, domain=[0.0, 0.25]
    )
    return [float(c) for c in cheb.convert(kind=np.polynomial.Polynomial).coef]


ROOT2 = math.sqrt(2.0)
SIN_COEF = fit(lambda r: ROOT2 * np.sin(np.pi * r) / r, 5)
COS_COEF = fit(lambda r: ROOT2 * np.cos(np.pi * r), 5)


def horner(coef, u):
    total = coef[-1] * u + coef[-2]
    for c in coef[-3::-1]:
        total = total * u + c
    return total


def trig(cycles):
    r = cycles - jnp.round(cycles)
    u = r * r
    s = horner(SIN_COEF, u) * r
    c = horner(COS_COEF, u)
    return 1.0 - s * s, s * c


def cheb_nodes():
    return 0.5 * np.cos(np.pi * (2.0 * np.arange(8) + 1.0) / 16.0)


def canon_tables():
    z = cheb_nodes()
    basis = np.zeros((2, 8, 8))
    for c in range(2):
        places = z / 2 + c / 2 - 0.25
        for i in range(8):
            value = np.ones(8)
            for k in range(8):
                if k != i:
                    value = value * (places - z[k]) / (z[i] - z[k])
            basis[c, i] = value
    return [np.kron(basis[c % 2], basis[c // 2]) for c in range(4)]


def split_np(a):
    hi = np.asarray(a, np.float32).astype(BF16)
    lo = (np.asarray(a, np.float64) - hi.astype(np.float64)).astype(np.float32).astype(BF16)
    return hi, lo


def constants():
    z = cheb_nodes().astype(np.float32)
    tables = canon_tables()
    t_in = np.concatenate(tables, axis=1)
    t_out = np.concatenate([t.T for t in tables], axis=0)
    in_h, in_l = split_np(t_in)
    out_h, out_l = split_np(t_out)
    t1 = np.concatenate([in_h, in_l], axis=0)
    t3 = np.concatenate([out_h, out_h, out_l], axis=1)
    tf = np.stack([out_h, out_l])
    ox = np.repeat(z, 8)
    oy = np.tile(z, 8)
    off = np.stack([np.broadcast_to(o[:, None], (64, 128)) for o in (ox, oy)])
    pieces = []
    rest = off.astype(np.float32)
    for _ in range(3):
        piece = rest.astype(BF16)
        pieces.append(piece)
        rest = rest - piece.astype(np.float32)
    return t1, t3, tf, np.ascontiguousarray(off, np.float32), np.stack(pieces)


def fiota(shape, axis):
    return lax.broadcasted_iota(jnp.int32, shape, axis)


def node_onehot(node_ref):
    flat = node_ref[0:1, :] * 8 + node_ref[1:2, :]
    return (fiota((64, 64), 0) == flat).astype(F32).astype(BF16)


def dot(a, b, dims=NN_DIMS):
    return lax.dot_general(a, b, dims, preferred_element_type=F32)


def split(x):
    hi = x.astype(BF16)
    return hi, (x - hi.astype(F32)).astype(BF16)


def from_sines(s1, c1, s2, c2):
    one = (2.0 + s1 * s2) * 0.0625
    two = (2.0 + c1 * c2) * 0.0625
    return one * one, two * two


def speeds(x1, x2):
    c1, s1 = trig(x1)
    c2, s2 = trig(x2)
    return from_sines(s1, c1, s2, c2)


def speeds_sum(row, col):
    sines = []
    for (ca, sa), (cb, sb) in zip(row, col):
        sines += [sa * cb + ca * sb, ca * cb - sa * sb]
    return from_sines(*sines)


def root(x):
    return x * lax.rsqrt(x)


def freq_columns(d1, d2, a1, a2, v1, v2):
    e1 = v1 * d1
    e2 = v2 * d2
    linear = a2 * d2 if isinstance(a1, float) and a1 == 0.0 else a1 * d1 + a2 * d2
    return 2.0 * e1, 2.0 * e2, e1 * d1 + e2 * d2, linear


def freq_row(g1, g2, v1, v2):
    square = v1 * g1 * g1 + v2 * g2 * g2 + 1.0
    return g1, g2, square, root(square)


def freq_cycles(columns, row):
    e1, e2, e0, linear = columns
    g1, g2, square, base = row
    numer = e1 * g1 + e2 * g2 + e0
    return linear + numer / (root(square + numer) + base)


def space_cycles(d1, d2, v1, v2, w1, w2, f1, f2):
    q1 = f1 * f1
    q2 = f2 * f2
    base = w1 * q1 + w2 * q2 + 1.0
    numer = (v1 - w1) * q1 + (v2 - w2) * q2
    return d1 * f1 + d2 * f2 + numer / (root(base + numer) + root(base))


ROWS = 32
MESH = pl.DeviceIdType.MESH


def bit(value, place):
    return lax.rem(lax.div(value, 1 << place), 2)


def tofloat(value):
    return value.astype(F32)


def splat(value):
    return jnp.full((1, 128), value, F32)


def save(tab, index, cycles, rows, lanes):
    cs, sn = trig(cycles)
    tab[index, 0, rows, lanes] = cs
    tab[index, 1, rows, lanes] = sn


def turn(re, im, tab, index, rows, lanes):
    cs = tab[index, 0, rows, lanes]
    sn = tab[index, 1, rows, lanes]
    return re * cs - im * sn, re * sn + im * cs


def columns_of(owner_ref, slot):
    owner = (owner_ref[0:1, :] == slot).astype(F32).astype(BF16)
    numbers = fiota((8, 16), 1).astype(F32).astype(BF16)
    return dot(numbers, owner, NT_DIMS)[0:1, :], owner


def kernel(n_dev, n_all, n_group, node_ref, owner_ref, w_hbm, t1_hbm, t3_hbm, tf_hbm, off_hbm, off3_hbm,
           o_ref, e_ref, x_ref, t1_ref, t3_ref, tf_ref, off_ref, off3_ref, z_ref, y_ref, tab1, tab2,
           tabm, tab3i, tab3o, tab4i, tabf, lin2, line, prod, part, doff, t1s, xh, xl, y1, y2, wmat, x3, v4, tmat,
           yy, send1, recv1, sea, ea, seb, eb, sec, ec, sxa,
           xa, sxb, xb, local, ready):
    flat = lax.axis_index("grp") * n_dev + lax.axis_index("dev")
    h = lax.div(flat, 16)
    ry = lax.rem(flat, 16)
    hf = tofloat(h)
    ryf = tofloat(ry)

    def place(device):
        return lax.div(device, n_dev), lax.rem(device, n_dev)

    barrier = pltpu.get_barrier_semaphore()

    def tell(semaphore, device):
        pl.semaphore_signal(semaphore, inc=1, device_id=place(device), device_id_type=MESH)

    for i in range(1, 16):
        tell(barrier, h * 16 + lax.rem(ry + i, 16))
    for g in range(1, n_group):
        tell(barrier, lax.rem(h + g, n_group) * 16 + ry)
    loads = [pltpu.make_async_copy(a, b, local.at[i]) for i, (a, b) in enumerate(
        [(t1_hbm, t1_ref), (t3_hbm, t3_ref), (tf_hbm, tf_ref), (off_hbm, off_ref),
         (off3_hbm, off3_ref)])]
    for load in loads:
        load.start()
    for load in loads:
        load.wait()

    onehot = node_onehot(node_ref)
    for axis in range(2):
        doff[axis] = sum(dot(onehot, off3_ref[p, axis], TN_DIMS) for p in (2, 1, 0))
    for c in range(4):
        t1s[:, c * 64:(c + 1) * 64] = dot(t1_ref[:, c * 64:(c + 1) * 64], onehot).astype(BF16)

    lane = [fiota((1, 128), 1) + k for k in (0, 128)]
    bx = [tofloat(lax.rem(v, 64)) for v in lane]
    by = [4.0 * ryf + tofloat(lax.div(v, 64)) for v in lane]

    def products(index, offsets, scale, shift, width, child):
        for l in range(0, 256, 128):
            for axis, at in ((0, bx[l // 128]), (1, by[l // 128])):
                g = width * at + child - HALF
                for r in range(0, 64, ROWS):
                    d = scale * offsets[axis, r:r + ROWS] + shift
                    prod[axis, index, r:r + ROWS, l:l + 128] = d * (2.0 * g + d)

    def products1(i, carry):
        child = tofloat(lax.div(i, 2))
        products(i, doff, 16.0, 16.0 * (child - 0.5), 64.0, 32.0 * (tofloat(lax.rem(i, 2)) + 0.5))
        return carry

    def products2(i, carry):
        products(4 + i, off_ref, 32.0, 32.0 * (tofloat(i) - 0.5), 64.0, 32.0)
        products(6 + i, off_ref, 32.0, 0.0, 64.0, 32.0 * (tofloat(i) + 0.5))
        return carry

    lax.fori_loop(0, 4, products1, 0)
    lax.fori_loop(0, 2, products2, 0)

    def linear2(i, carry):
        ux = tofloat(lax.div(i, 2))
        a1 = (2.0 * hf + ux + 0.5) / 32.0
        b1 = (4.0 * hf + 2.0 * ux + tofloat(lax.rem(i, 2)) + 0.5) / 64.0
        for r in range(0, 64, ROWS):
            rows = slice(r, r + ROWS)
            o = off_ref[0, rows]
            save(lin2, i, 32.0 * (a1 * o - b1 * (o - 0.5)), rows, slice(0, 128))
        return carry

    lax.fori_loop(0, 4, linear2, 0)

    n = fiota((1, 128), 1)
    nrow = fiota((128, 16), 0)
    column, owner = columns_of(owner_ref, 2 * lax.div(nrow, 16) + lax.rem(nrow, 2))
    erow = fiota((128, 16), 0)
    picks = (lax.rem(lax.div(erow, 4), 16) == fiota((128, 16), 1)).astype(F32).astype(BF16)
    wcol = dot(picks, owner, NT_DIMS)
    wu = lax.rem(lax.div(fiota((128, 128), 1), 2), 8)
    for v in range(2):
        keep = jnp.where(lax.rem(lax.div(fiota((128, 128), 0), 2), 2) == v, wcol, 0.0)
        for u in range(8):
            wmat[u * 128:(u + 1) * 128, v * 128:(v + 1) * 128] = jnp.where(
                wu == u, keep, 0.0).astype(BF16)

    u8 = lax.rem(lax.div(n, 2), 8)

    def parent(u):
        u1 = lax.rem(u, 4)
        u2 = lax.div(u, 4)
        return (tofloat(2 * lax.rem(u1, 2) + lax.rem(u2, 2)),
                tofloat(2 * lax.div(u1, 2) + lax.div(u2, 2)))

    pl.semaphore_wait(barrier, 14 + n_group)
    for g in range(1, n_group):
        tell(ready, lax.rem(h + g, n_group) * 16 + ry)

    def chunk(m, b):
        return w_hbm.at[:, :, pl.ds(pl.multiple_of(m * 256 + b * 128, 128), 128)]

    def exchange1(b, i):
        m = (lax.rem(lax.div(ry, 8) + i // 8, 2) * 8
             + lax.rem(lax.div(lax.rem(ry, 8), 2) + i // 2 % 4, 4) * 2 + lax.rem(ry + i, 2))
        return pltpu.make_async_remote_copy(
            src_ref=chunk(m, b), dst_ref=x_ref.at[b, ry], send_sem=send1.at[b * 16 + i],
            recv_sem=recv1.at[b * 16 + i], device_id=place(h * 16 + m), device_id_type=MESH)

    for b in range(2):
        for i in range(1, 16):
            exchange1(b, i).start()
    own1 = [pltpu.make_async_copy(chunk(ry, b), x_ref.at[b, ry], recv1.at[b * 16])
            for b in range(2)]
    for copy in own1:
        copy.start()

    def freq_rest(row, ix, iy, v1, v2, rows, lanes):
        square, base = row
        numer = v1 * prod[0, ix, rows, lanes] + v2 * prod[1, iy, rows, lanes]
        return numer / (root(square + numer) + base)

    def level1(i, carry):
        c = lax.rem(i, 4)
        u1 = lax.div(i, 4)
        a1 = (2.0 * hf + tofloat(bit(u1, 0)) + 0.5) / 32.0
        a2 = (tofloat(bit(u1, 1)) + 0.5) / 32.0
        v1, v2 = speeds(splat(a1), splat(a2))
        sx = 16.0 * (tofloat(bit(c, 0)) - 0.5)
        sy = 16.0 * (tofloat(bit(c, 1)) - 0.5)
        for r in range(0, 64, ROWS):
            line[r:r + ROWS] = -(a1 * (sx + 16.0 * doff[0, r:r + ROWS])
                                 + a2 * (sy + 16.0 * doff[1, r:r + ROWS]))

        def inner(u2, carry):
            for l in range(0, 256, 128):
                k = l // 128
                row = freq_row(32.0 * (2.0 * bx[k] + tofloat(bit(u2, 0)) + 0.5) - HALF,
                               32.0 * (2.0 * by[k] + tofloat(bit(u2, 1)) + 0.5) - HALF, v1, v2)
                for r in range(0, 64, ROWS):
                    rows = slice(r, r + ROWS)
                    lanes = slice(l, l + 128)
                    rest = freq_rest(row[2:], 2 * bit(c, 0) + bit(u2, 0),
                                     2 * bit(c, 1) + bit(u2, 1), v1, v2, rows, lanes)
                    save(tab1, i * 4 + u2, line[rows] - rest, rows, lanes)
            return carry

        lax.fori_loop(0, 4, inner, 0, unroll=2)
        return carry

    lax.fori_loop(0, 16, level1, 0)

    mirror = fiota((ROWS, 128), 1)
    mirror = lax.div(mirror, 64) * 64 + 63 - lax.rem(mirror, 64)

    def mirrored(tab, index, other, cycles, lin, which, r, lanes):
        cs, sn = trig(cycles)
        cl = lin[which, 0, r:r + ROWS]
        sl = lin[which, 1, r:r + ROWS]
        p, q, s, t = cs * cl, sn * sl, sn * cl, cs * sl
        tab[index, 0, r:r + ROWS, lanes] = p - q
        tab[index, 1, r:r + ROWS, lanes] = s + t
        for part_id, value in enumerate((p + q, s - t)):
            value = jnp.take_along_axis(value, mirror, axis=1, mode="promise_in_bounds")
            for k in range(0, ROWS, 8):
                to = 56 - r - k
                tab[other, part_id, to:to + 8, lanes] = value[k:k + 8]

    def level2(i, carry):
        u1 = lax.div(i, 2)
        a1 = (2.0 * hf + tofloat(bit(u1, 0)) + 0.5) / 32.0
        a2 = (tofloat(bit(u1, 1)) + 0.5) / 32.0
        v1, v2 = speeds(splat(a1), splat(a2))
        cy = tofloat(lax.rem(i, 2))
        cyi = lax.rem(i, 2)
        for r in range(0, 64, ROWS):
            rows = slice(r, r + ROWS)
            for l in range(0, 256, 128):
                k = l // 128
                lanes = slice(l, l + 128)
                row = freq_row(32.0 * (2.0 * bx[k] + 0.5) - HALF,
                               32.0 * (2.0 * by[k] + cy + 0.5) - HALF, v1, v2)
                part[rows, lanes] = (a2 * (32.0 * off_ref[1, rows])
                                     + freq_rest(row[2:], 6, 6 + cyi, v1, v2, rows, lanes))
        index = (u1 * 4 + 2 * cyi) * 4

        def inner(u2, carry):
            b1 = (4.0 * hf + 2.0 * tofloat(bit(u1, 0)) + tofloat(bit(u2, 0)) + 0.5) / 64.0
            b2 = (2.0 * tofloat(bit(u1, 1)) + tofloat(bit(u2, 1)) + 0.5) / 64.0
            w1, w2 = speeds(splat(b1), splat(b2))
            for l in range(0, 256, 128):
                k = l // 128
                lanes = slice(l, l + 128)
                row = freq_row(64.0 * (bx[k] + 0.5) - HALF, 64.0 * (by[k] + 0.5) - HALF, w1, w2)
                for r in range(0, 64, ROWS):
                    rows = slice(r, r + ROWS)
                    rest = freq_rest(row[2:], 4, 4 + cyi, w1, w2, rows, lanes)
                    down = (b2 * 32.0) * (off_ref[1, rows] + (cy - 0.5))
                    mirrored(tab2, index + u2, index + 4 + u2, part[rows, lanes] - down - rest,
                             lin2, bit(u1, 0) * 2 + bit(u2, 0), r, lanes)
            return carry

        lax.fori_loop(0, 4, inner, 0, unroll=2)
        return carry

    lax.fori_loop(0, 8, level2, 0)

    def middle(u, carry):
        u1 = lax.rem(u, 4)
        u2 = lax.div(u, 4)
        b1 = (4.0 * hf + 2.0 * tofloat(bit(u1, 0)) + tofloat(bit(u2, 0)) + 0.5) / 64.0
        b2 = (2.0 * tofloat(bit(u1, 1)) + tofloat(bit(u2, 1)) + 0.5) / 64.0
        w1, w2 = speeds(splat(b1), splat(b2))
        rows = [freq_row(64.0 * (bx[k] + 0.5) - HALF, 64.0 * (by[k] + 0.5) - HALF, w1, w2)
                for k in range(2)]
        for r in range(0, 64, ROWS):
            cols = freq_columns(64.0 * off_ref[0, r:r + ROWS], 64.0 * off_ref[1, r:r + ROWS],
                                b1, b2, w1, w2)
            for l in range(0, 256, 128):
                save(tabm, u, freq_cycles(cols, rows[l // 128]), slice(r, r + ROWS),
                     slice(l, l + 128))
        return carry

    lax.fori_loop(0, 16, middle, 0, unroll=2)

    def level3(half, carry):
        mx, my = parent(u8 + 8 * half)
        p1 = (4.0 * hf + mx + 0.5) / 64.0
        p2 = (my + 0.5) / 64.0
        row = (trig(p1), trig(p2))
        w1, w2 = from_sines(row[0][1], row[0][0], row[1][1], row[1][0])
        for r in range(0, 64, ROWS):
            rows = slice(r, r + ROWS)
            d1 = off_ref[0, rows] / 64.0
            d2 = off_ref[1, rows] / 64.0
            s1, s2 = speeds_sum(row, (trig(d1), trig(d2)))
            for v in range(4):
                f1 = 128.0 * (2.0 * column + (v % 2) + 0.5) - HALF
                f2 = 128.0 * (2.0 * ryf + (v // 2) + 0.5) - HALF
                cycles = space_cycles(d1, d2, s1, s2, w1, w2, f1, f2)
                save(tab3i, half * 4 + v, -cycles, rows, slice(0, 128))
        return carry

    lax.fori_loop(0, 2, level3, 0)

    def level4(i, carry):
        half = lax.div(i, 4)
        jx = tofloat(bit(lax.rem(i, 4), 0))
        jy = tofloat(bit(lax.rem(i, 4), 1))
        mx, my = parent(u8 + 8 * half)
        mx = 4.0 * hf + mx
        w1, w2 = speeds((mx + 0.5) / 64.0, (my + 0.5) / 64.0)
        c1 = (2.0 * mx + jx + 0.5) / 128.0
        c2 = (2.0 * my + jy + 0.5) / 128.0
        row = (trig(c1), trig(c2))
        z1, z2 = from_sines(row[0][1], row[0][0], row[1][1], row[1][0])
        for r in range(0, 64, ROWS):
            rows = slice(r, r + ROWS)
            d1 = off_ref[0, rows] / 128.0
            d2 = off_ref[1, rows] / 128.0
            s1, s2 = speeds_sum(row, (trig(d1), trig(d2)))
            e1 = d1 + (jx - 0.5) / 128.0
            e2 = d2 + (jy - 0.5) / 128.0
            for v in range(4):
                f1 = 128.0 * (2.0 * column + (v % 2) + 0.5) - HALF
                f2 = 128.0 * (2.0 * ryf + (v // 2) + 0.5) - HALF
                cycles = space_cycles(e1, e2, s1, s2, w1, w2, f1, f2)
                save(tab3o, i * 4 + v, cycles, rows, slice(0, 128))
            f1 = 256.0 * (column + 0.5) - HALF
            f2 = 256.0 * (ryf + 0.5) - HALF
            cycles = space_cycles(d1, d2, s1, s2, z1, z2, f1, f2)
            save(tab4i, i, -cycles, rows, slice(0, 128))
        return carry

    lax.fori_loop(0, 8, level4, 0)

    yi = lax.div(flat, 32)
    x0 = lax.rem(lax.div(flat, 8), 4)
    zc = lax.rem(flat, 8)
    z0 = lax.div(zc, 2)
    c0 = lax.rem(zc, 2)
    x1 = x0 + 1 - 2 * lax.rem(x0, 2)

    def at_device(y, x, m):
        return place(y * 32 + x * 8 + m)

    def near(x, o):
        return 3 - x if o else x

    def remote(source, target, sender, receiver, device):
        return pltpu.make_async_remote_copy(
            src_ref=source, dst_ref=target, send_sem=sender, recv_sem=receiver,
            device_id=device, device_id_type=MESH)

    def arrive(ref, semaphore):
        pltpu.make_async_copy(ref, ref, semaphore).wait()

    pairs_of = [(t, o) for t in (0, 1, 3, 2) for o in (0, 1)]

    def spread(d):
        return lax.rem(z0 + d // 2, 4) * 2 + lax.rem(c0 + d, 2)

    def e_first():
        for t, o in pairs_of:
            yk = lax.rem(yi + t, 4)
            xk = near(x0, o)
            block = z_ref.at[0, yk * 2 + lax.div(xk, 2)]
            s = o * 4 + t
            if s == 0:
                pltpu.make_async_copy(block, e_ref.at[yi, x0], ea.at[s]).start()
            else:
                remote(block, e_ref.at[yi, x0], sea.at[s], ea.at[s],
                       at_device(yk, xk, zc)).start()

    def x_first():
        for t, o in pairs_of:
            yk = lax.rem(yi + t, 4)
            xk = near(x0, o)
            k = yk * 2 + lax.div(xk, 2)
            s = o * 4 + t
            for d in (4, 5, 2, 3, 6, 7, 0, 1):
                m = spread(d)
                block = z_ref.at[1, k, lax.rem(m, 4)]
                if s == 0 and d == 0:
                    pltpu.make_async_copy(block, y_ref.at[1, yi, x0, zc], xa.at[s]).start()
                else:
                    remote(block, y_ref.at[1, yi, x0, zc], sxa.at[s], xa.at[s],
                           at_device(yk, xk, m)).start()

    def e_pass():
        for t, o in pairs_of:
            s = o * 4 + t
            block = e_ref.at[lax.rem(yi + 4 - t, 4), near(x0, o)]
            arrive(block, ea.at[s])
            remote(block, block, seb.at[s], eb.at[s], at_device(yi, x1, zc)).start()

    def x_pass():
        for t, o in pairs_of:
            s = o * 4 + t
            block = y_ref.at[1, lax.rem(yi + 4 - t, 4), near(x0, o)]
            arrive(block, xa.at[s])
            remote(block, block, sxb.at[s], xb.at[s], at_device(yi, x1, zc)).start()

    def e_last(x, o):
        xs = near(x, o)
        for d in (4, 5, 2, 3, 6, 7, 1, 0):
            m = spread(d)
            block = e_ref.at[:, xs, lax.rem(m, 4)]
            if d == 0:
                pltpu.make_async_copy(block, y_ref.at[0, :, xs, zc], ec.at[xs]).start()
            else:
                remote(block, y_ref.at[0, :, xs, zc], sec, ec.at[xs],
                       at_device(yi, x0, m)).start()

    def send_half(half):
        pl.when(half == 0)(e_first)
        pl.when(half == 1)(x_first)

    def stage(b):
        at = slice(b * 128, b * 128 + 128)
        whole = slice(0, 128)

        def turned(slot, source, tab, index):
            for c in range(4):
                for r in range(0, 64, ROWS):
                    rows = slice(r, r + ROWS)
                    re, im = source(c, rows)
                    parts = turn(re, im, tab, index(c), rows, at)
                    for p in range(2):
                        hi, lo = split(parts[p])
                        xh[slot, c * 64 + r:c * 64 + r + ROWS, p * 128:p * 128 + 128] = hi
                        xl[slot, c * 64 + r:c * 64 + r + ROWS, p * 128:p * 128 + 128] = lo

        def mixed(slot, table):
            first = dot(table[...], xh[slot])
            return first[:64] + first[64:] + dot(table[0:64], xl[slot])

        def run1(e, carry):
            ux = lax.rem(lax.div(ry, 8) + lax.div(e, 2), 2)
            uz = lax.rem(lax.div(ry, 4) + e, 2)
            u2 = 2 * ux + uz
            for c in range(4):
                i = (lax.rem(lax.div(ry, 8) + ux, 2) * 8
                     + lax.rem(lax.div(lax.rem(ry, 8), 2) + 4 - 2 * uz - c // 2, 4) * 2
                     + lax.rem(ry + c, 2))
                landed = x_ref.at[b, u2 * 4 + c]
                pltpu.make_async_copy(landed, landed, recv1.at[b * 16 + i]).wait()
            for u1 in range(4):
                turned(u1, lambda c, rows: (x_ref[b, u2 * 4 + c, 0, rows],
                                            x_ref[b, u2 * 4 + c, 1, rows]),
                       tab1, lambda c: (u1 * 4 + c) * 4 + u2)
                y1[u1 * 4 + u2] = mixed(u1, t1s)
            return carry

        lax.fori_loop(0, 4, run1, 0)

        def run2(half, pair):
            for slot in range(4):
                u1 = 2 * pair + slot // 2
                u2 = 2 * half + slot % 2
                u = u1 + 4 * u2
                turned(slot, lambda c, rows: (y1[u1 * 4 + c, rows, 0:128],
                                              y1[u1 * 4 + c, rows, 128:256]),
                       tab2, lambda c: (u1 * 4 + c) * 4 + u2)
                out = mixed(slot, t1_ref)
                to = pl.ds(pl.multiple_of((u1 + 4 * (slot % 2)) * 128, 128), 128)
                for r in range(0, 64, ROWS):
                    rows = slice(r, r + ROWS)
                    parts = turn(out[rows, 0:128], out[rows, 128:256], tabm, u, rows, at)
                    for p in range(2):
                        hi, lo = split(parts[p])
                        y2[p * 64 + r:p * 64 + r + ROWS, to] = hi
                        y2[128 + p * 64 + r:128 + p * 64 + r + ROWS, to] = lo

        def run3(half):
            both = dot(y2[...], wmat[...])
            summed = both[:128] + both[128:]
            for v in range(2):
                for r in range(0, 64, ROWS):
                    rows = slice(r, r + ROWS)
                    l = v * 128
                    parts = turn(summed[r:r + ROWS, l:l + 128],
                                 summed[64 + r:64 + r + ROWS, l:l + 128], tab3i,
                                 half * 4 + 2 * b + v, rows, whole)
                    for p in range(2):
                        hi, lo = split(parts[p])
                        to = slice((v * 2 + p) * 128, (v * 2 + p + 1) * 128)
                        x3[r:r + ROWS, to] = hi
                        x3[64 + r:64 + r + ROWS, to] = lo
                        x3[128 + r:128 + r + ROWS, to] = hi
            for j in range(4):
                out = dot(t3_ref[j * 64:(j + 1) * 64], x3[...])
                for r in range(0, 64, ROWS):
                    rows = slice(r, r + ROWS)
                    low = slice(64 + r, 64 + r + ROWS)
                    if b == 1:
                        re, im = v4[half * 4 + j, rows], v4[half * 4 + j, low]
                    for v in range(2):
                        l = v * 256
                        p, q = turn(out[rows, l:l + 128], out[rows, l + 128:l + 256], tab3o,
                                    (half * 4 + j) * 4 + 2 * b + v, rows, whole)
                        first = b == 0 and v == 0
                        re = p if first else re + p
                        im = q if first else im + q
                    if b == 1:
                        re, im = turn(re, im, tab4i, half * 4 + j, rows, whole)
                    v4[half * 4 + j, rows] = re
                    v4[half * 4 + j, low] = im
                if b == 1:
                    flipped = v4[half * 4 + j].T
                    for k in range(8):
                        z_ref[half, k, j] = flipped[k * 16:(k + 1) * 16]

        def run(half, carry):
            def pairs(pair, carry):
                run2(half, pair)
                return carry

            lax.fori_loop(0, 2, pairs, 0)
            run3(half)
            if b == 1:
                send_half(half)
            return carry

        lax.fori_loop(0, 2, run, 0)

    for b in range(2):
        if b == 1:
            pl.semaphore_wait(ready, n_group - 1)
        stage(b)

    e_pass()
    e_last(x0, 0)
    e_last(x0, 1)
    x_pass()
    for o in range(2):
        for t in (0, 1, 3, 2):
            arrive(e_ref.at[lax.rem(yi + 4 - t, 4), near(x1, o)], eb.at[o * 4 + t])
        e_last(x1, o)

    v1d = lax.rem(ry, 4)
    v2d = lax.div(ry, 4)
    zero = jnp.zeros((64, 64), BF16)
    pieces = [dot(onehot, tf_ref[p, pl.ds(pl.multiple_of(v2d * 64, 64), 64), :],
                  TN_DIMS).astype(BF16) for p in range(2)]
    for p in range(2):
        for q in range(2):
            for piece in range(2):
                for low in range(2):
                    lanes = slice(low * 128 + q * 64, low * 128 + q * 64 + 64)
                    rows = slice(piece * 128 + p * 64, piece * 128 + p * 64 + 64)
                    use = p == q and not (piece == 1 and low == 1)
                    tmat[rows, lanes] = pieces[piece] if use else zero
    ids = fiota((512, 16), 0)
    column, _ = columns_of(owner_ref, 2 * h + lax.rem(lax.div(ids, 16), 2))
    jx, jy = tofloat(lax.rem(v2d, 2)), tofloat(lax.div(v2d, 2))
    vx, vy = tofloat(lax.rem(v1d, 2)), tofloat(lax.div(v1d, 2))
    f2 = 256.0 * (tofloat(lax.rem(n, 16)) + 0.5) - HALF

    def level5(src, carry):
        for l in range(0, 512, 128):
            mx, my = parent(lax.div(n + l, 32))
            c1 = (2.0 * (4.0 * tofloat(src) + mx) + vx + 0.5) / 128.0
            c2 = (2.0 * my + vy + 0.5) / 128.0
            row = (trig(c1), trig(c2))
            w1, w2 = from_sines(row[0][1], row[0][0], row[1][1], row[1][0])
            f1 = 256.0 * (column[:, l:l + 128] + 0.5) - HALF
            for r in range(0, 64, ROWS):
                d1 = (doff[0, r:r + ROWS] + (jx - 0.5)) / 256.0
                d2 = (doff[1, r:r + ROWS] + (jy - 0.5)) / 256.0
                s1, s2 = speeds_sum(row, (trig(d1), trig(d2)))
                save(tabf, src, space_cycles(d1, d2, s1, s2, w1, w2, f1, f2),
                     slice(r, r + ROWS), slice(l, l + 128))
        return carry

    lax.fori_loop(0, 8, level5, 0)

    def run4(half, src):
        for m in range(16):
            yy[pl.ds(m, 16, stride=16), :] = y_ref[half, lax.div(src, 2),
                                                  lax.rem(src, 2) * 2 + m // 8, m % 8]
        hi, lo = split(yy[...])
        out = dot(tmat[...], jnp.concatenate([hi, lo], axis=1), NT_DIMS)
        out = out[:128] + out[128:]
        for l in range(0, 256, 128):
            there = slice(half * 256 + l, half * 256 + l + 128)
            lanes = pl.ds(pl.multiple_of(src * 512 + half * 256 + l, 128), 128)
            for r in range(0, 64, ROWS):
                rows = slice(r, r + ROWS)
                re, im = turn(out[r:r + ROWS, l:l + 128], out[64 + r:64 + r + ROWS, l:l + 128],
                              tabf, src, rows, there)
                o_ref[0, rows, lanes] = re
                o_ref[1, rows, lanes] = im

    for o in range(2):
        pair = lax.div(near(x0, o), 2)

        def half1(t, carry):
            ys = lax.rem(yi + 4 - t, 4)
            arrive(y_ref.at[1, ys, near(x1, o)], xb.at[o * 4 + t])
            run4(1, ys * 2 + pair)
            return carry

        def half0(ys, carry):
            run4(0, ys * 2 + pair)
            return carry

        lax.fori_loop(0, 4, half1, 0)
        for x in (x0, x1):
            arrive(y_ref.at[0, :, near(x, o)], ec.at[near(x, o)])
        lax.fori_loop(0, 4, half0, 0)
    sent = y_ref.at[0, :, :, pl.ds(0, 7)]
    arrive(sent, sec)
    for s in range(8):
        if s > 0:
            arrive(e_ref.at[0, 0], sea.at[s])
            arrive(y_ref.at[1, 0, 0], sxa.at[s])
        arrive(e_ref.at[0, 0], seb.at[s])
        arrive(y_ref.at[1, 0, 0], sxb.at[s])
    arrive(y_ref.at[1, 0, 0, pl.ds(0, 7)], sxa.at[0])
    for b in range(2):
        for i in range(1, 16):
            exchange1(b, i).wait_send()


VMEM_LIMIT = 60 * 1024 * 1024


def body(weights, owner_map, node_index):
    t1, t3, tf, off, off3 = constants()
    n_dev = lax.axis_size("dev")
    n_all = lax.axis_size("grp") * n_dev
    vmem = pl.BlockSpec(memory_space=pltpu.VMEM)
    hbm = pl.BlockSpec(memory_space=pltpu.HBM)
    dma = pltpu.SemaphoreType.DMA
    return pl.pallas_call(
        functools.partial(kernel, n_dev, n_all, n_all // 16),
        out_shape=pltpu.VMEM((2, 64, 4096), F32),
        in_specs=[vmem] * 2 + [hbm] * 6,
        out_specs=vmem,
        scratch_shapes=[
            pltpu.VMEM((4, 4, 4, 16, 128), F32),
            pltpu.VMEM((2, 16, 2, 64, 128), F32),
            pltpu.VMEM(t1.shape, BF16),
            pltpu.VMEM(t3.shape, BF16),
            pltpu.VMEM(tf.shape, BF16),
            pltpu.VMEM(off.shape, F32),
            pltpu.VMEM(off3.shape, BF16),
            pltpu.VMEM((2, 8, 4, 16, 128), F32),
            pltpu.VMEM((2, 4, 4, 8, 16, 128), F32),
            pltpu.VMEM((64, 2, 64, 256), F32),
            pltpu.VMEM((64, 2, 64, 256), F32),
            pltpu.VMEM((16, 2, 64, 256), F32),
            pltpu.VMEM((8, 2, 64, 128), F32),
            pltpu.VMEM((32, 2, 64, 128), F32),
            pltpu.VMEM((8, 2, 64, 128), F32),
            pltpu.VMEM((8, 2, 64, 512), F32),
            pltpu.VMEM((4, 2, 64, 128), F32),
            pltpu.VMEM((64, 128), F32),
            pltpu.VMEM((2, 8, 64, 256), F32),
            pltpu.VMEM((64, 256), F32),
            pltpu.VMEM((2, 64, 128), F32),
            pltpu.VMEM((128, 256), BF16),
            pltpu.VMEM((4, 256, 256), BF16),
            pltpu.VMEM((4, 256, 256), BF16),
            pltpu.VMEM((16, 64, 256), F32),
            pltpu.VMEM((256, 1024), BF16),
            pltpu.VMEM((1024, 256), BF16),
            pltpu.VMEM((192, 512), BF16),
            pltpu.VMEM((8, 128, 128), F32),
            pltpu.VMEM((256, 256), BF16),
            pltpu.VMEM((256, 128), F32),
            dma((32,)),
            dma((32,)),
            dma((8,)),
            dma((8,)),
            dma((8,)),
            dma((8,)),
            dma(()),
            dma((4,)),
            dma((8,)),
            dma((8,)),
            dma((8,)),
            dma((8,)),
            dma((5,)),
            pltpu.SemaphoreType.REGULAR,
        ],
        compiler_params=pltpu.CompilerParams(
            vmem_limit_bytes=VMEM_LIMIT, collective_id=0, has_side_effects=True),
        name="butterfly",
    )(node_index, owner_map.reshape(1, 16), weights, t1, t3, tf, off, off3)


def solution(mesh):
    in_specs = (P(None, None, ("grp", "dev")), P(), P())
    out_specs = P(None, None, ("grp", "dev"))
    return jax.shard_map(body, mesh=mesh, in_specs=in_specs, out_specs=out_specs, check_vma=False)
```

```python
import functools
import math

import jax
import jax.numpy as jnp
import numpy as np
from jax import lax
from jax.experimental import pallas as pl
from jax.experimental.pallas import tpu as pltpu
from jax.sharding import PartitionSpec as P

F32 = jnp.float32
BF16 = jnp.bfloat16
HALF = 2048.0
NT_DIMS = (((1,), (1,)), ((), ()))
TN_DIMS = (((0,), (0,)), ((), ()))
NN_DIMS = (((1,), (0,)), ((), ()))


def fit(function, count):
    angle = (np.arange(64) + 0.5) * np.pi / 64
    points = 0.125 + 0.125 * np.cos(angle)
    cheb = np.polynomial.chebyshev.Chebyshev.fit(
        points, function(np.sqrt(points)), count - 1, domain=[0.0, 0.25]
    )
    return [float(c) for c in cheb.convert(kind=np.polynomial.Polynomial).coef]


ROOT2 = math.sqrt(2.0)
SIN_COEF = fit(lambda r: ROOT2 * np.sin(np.pi * r) / r, 5)
COS_COEF = fit(lambda r: ROOT2 * np.cos(np.pi * r), 5)


def horner(coef, u):
    total = coef[-1] * u + coef[-2]
    for c in coef[-3::-1]:
        total = total * u + c
    return total


def trig(cycles):
    r = cycles - jnp.round(cycles)
    u = r * r
    s = horner(SIN_COEF, u) * r
    c = horner(COS_COEF, u)
    return 1.0 - s * s, s * c


def cheb_nodes():
    return 0.5 * np.cos(np.pi * (2.0 * np.arange(8) + 1.0) / 16.0)


def canon_tables():
    z = cheb_nodes()
    basis = np.zeros((2, 8, 8))
    for c in range(2):
        places = z / 2 + c / 2 - 0.25
        for i in range(8):
            value = np.ones(8)
            for k in range(8):
                if k != i:
                    value = value * (places - z[k]) / (z[i] - z[k])
            basis[c, i] = value
    return [np.kron(basis[c % 2], basis[c // 2]) for c in range(4)]


def split_np(a):
    hi = np.asarray(a, np.float32).astype(BF16)
    lo = (np.asarray(a, np.float64) - hi.astype(np.float64)).astype(np.float32).astype(BF16)
    return hi, lo


def constants():
    z = cheb_nodes().astype(np.float32)
    tables = canon_tables()
    t_in = np.concatenate(tables, axis=1)
    t_out = np.concatenate([t.T for t in tables], axis=0)
    in_h, in_l = split_np(t_in)
    out_h, out_l = split_np(t_out)
    t1 = np.concatenate([in_h, in_l], axis=0)
    t3 = np.concatenate([out_h, out_h, out_l], axis=1)
    tf = np.stack([out_h, out_l])
    ox = np.repeat(z, 8)
    oy = np.tile(z, 8)
    off = np.stack([np.broadcast_to(o[:, None], (64, 128)) for o in (ox, oy)])
    pieces = []
    rest = off.astype(np.float32)
    for _ in range(3):
        piece = rest.astype(BF16)
        pieces.append(piece)
        rest = rest - piece.astype(np.float32)
    return t1, t3, tf, np.ascontiguousarray(off, np.float32), np.stack(pieces)


def fiota(shape, axis):
    return lax.broadcasted_iota(jnp.int32, shape, axis)


def node_onehot(node_ref):
    flat = node_ref[0:1, :] * 8 + node_ref[1:2, :]
    return (fiota((64, 64), 0) == flat).astype(F32).astype(BF16)


def dot(a, b, dims=NN_DIMS):
    return lax.dot_general(a, b, dims, preferred_element_type=F32)


def split(x):
    hi = x.astype(BF16)
    return hi, (x - hi.astype(F32)).astype(BF16)


def from_sines(s1, c1, s2, c2):
    one = (2.0 + s1 * s2) * 0.0625
    two = (2.0 + c1 * c2) * 0.0625
    return one * one, two * two


def speeds(x1, x2):
    c1, s1 = trig(x1)
    c2, s2 = trig(x2)
    return from_sines(s1, c1, s2, c2)


def speeds_sum(row, col):
    sines = []
    for (ca, sa), (cb, sb) in zip(row, col):
        sines += [sa * cb + ca * sb, ca * cb - sa * sb]
    return from_sines(*sines)


def root(x):
    return x * lax.rsqrt(x)


def freq_columns(d1, d2, a1, a2, v1, v2):
    e1 = v1 * d1
    e2 = v2 * d2
    linear = a2 * d2 if isinstance(a1, float) and a1 == 0.0 else a1 * d1 + a2 * d2
    return 2.0 * e1, 2.0 * e2, e1 * d1 + e2 * d2, linear


def freq_row(g1, g2, v1, v2):
    square = v1 * g1 * g1 + v2 * g2 * g2 + 1.0
    return g1, g2, square, root(square)


def freq_cycles(columns, row):
    e1, e2, e0, linear = columns
    g1, g2, square, base = row
    numer = e1 * g1 + e2 * g2 + e0
    return linear + numer / (root(square + numer) + base)


def space_cycles(d1, d2, v1, v2, w1, w2, f1, f2):
    q1 = f1 * f1
    q2 = f2 * f2
    base = w1 * q1 + w2 * q2 + 1.0
    numer = (v1 - w1) * q1 + (v2 - w2) * q2
    return d1 * f1 + d2 * f2 + numer / (root(base + numer) + root(base))


ROWS = 32
MESH = pl.DeviceIdType.MESH


def bit(value, place):
    return lax.rem(lax.div(value, 1 << place), 2)


def tofloat(value):
    return value.astype(F32)


def splat(value):
    return jnp.full((1, 128), value, F32)


def save(tab, index, cycles, rows, lanes):
    cs, sn = trig(cycles)
    tab[index, 0, rows, lanes] = cs
    tab[index, 1, rows, lanes] = sn


def turn(re, im, tab, index, rows, lanes):
    cs = tab[index, 0, rows, lanes]
    sn = tab[index, 1, rows, lanes]
    return re * cs - im * sn, re * sn + im * cs


def columns_of(owner_ref, slot):
    owner = (owner_ref[0:1, :] == slot).astype(F32).astype(BF16)
    numbers = fiota((8, 16), 1).astype(F32).astype(BF16)
    return dot(numbers, owner, NT_DIMS)[0:1, :], owner


def kernel(n_dev, n_all, n_group, node_ref, owner_ref, w_hbm, t1_hbm, t3_hbm, tf_hbm, off_hbm, off3_hbm,
           o_ref, e_ref, x_ref, t1_ref, t3_ref, tf_ref, off_ref, off3_ref, z_ref, y_ref, tab1, tab2,
           tabm, tab3i, tab3o, tab4i, tabf, lin2, line, prod, part, doff, t1s, xh, xl, y1, y2, wmat, x3, v4, tmat,
           yy, send1, recv1, sea, ea, seb, eb, sec, ec, sxa,
           xa, sxb, xb, local, ready):
    flat = lax.axis_index("grp") * n_dev + lax.axis_index("dev")
    h = lax.div(flat, 16)
    ry = lax.rem(flat, 16)
    hf = tofloat(h)
    ryf = tofloat(ry)

    def place(device):
        return lax.div(device, n_dev), lax.rem(device, n_dev)

    barrier = pltpu.get_barrier_semaphore()

    def tell(semaphore, device):
        pl.semaphore_signal(semaphore, inc=1, device_id=place(device), device_id_type=MESH)

    for i in range(1, 16):
        tell(barrier, h * 16 + lax.rem(ry + i, 16))
    for g in range(1, n_group):
        tell(barrier, lax.rem(h + g, n_group) * 16 + ry)
    loads = [pltpu.make_async_copy(a, b, local.at[i]) for i, (a, b) in enumerate(
        [(t1_hbm, t1_ref), (t3_hbm, t3_ref), (tf_hbm, tf_ref), (off_hbm, off_ref),
         (off3_hbm, off3_ref)])]
    for load in loads:
        load.start()
    for load in loads:
        load.wait()

    onehot = node_onehot(node_ref)
    for axis in range(2):
        doff[axis] = sum(dot(onehot, off3_ref[p, axis], TN_DIMS) for p in (2, 1, 0))
    for c in range(4):
        t1s[:, c * 64:(c + 1) * 64] = dot(t1_ref[:, c * 64:(c + 1) * 64], onehot).astype(BF16)

    lane = [fiota((1, 128), 1) + k for k in (0, 128)]
    bx = [tofloat(lax.rem(v, 64)) for v in lane]
    by = [4.0 * ryf + tofloat(lax.div(v, 64)) for v in lane]

    def products(index, offsets, scale, shift, width, child):
        for l in range(0, 256, 128):
            for axis, at in ((0, bx[l // 128]), (1, by[l // 128])):
                g = width * at + child - HALF
                for r in range(0, 64, ROWS):
                    d = scale * offsets[axis, r:r + ROWS] + shift
                    prod[axis, index, r:r + ROWS, l:l + 128] = d * (2.0 * g + d)

    def products1(i, carry):
        child = tofloat(lax.div(i, 2))
        products(i, doff, 16.0, 16.0 * (child - 0.5), 64.0, 32.0 * (tofloat(lax.rem(i, 2)) + 0.5))
        return carry

    def products2(i, carry):
        products(4 + i, off_ref, 32.0, 32.0 * (tofloat(i) - 0.5), 64.0, 32.0)
        products(6 + i, off_ref, 32.0, 0.0, 64.0, 32.0 * (tofloat(i) + 0.5))
        return carry

    lax.fori_loop(0, 4, products1, 0)
    lax.fori_loop(0, 2, products2, 0)

    def linear2(i, carry):
        ux = tofloat(lax.div(i, 2))
        a1 = (2.0 * hf + ux + 0.5) / 32.0
        b1 = (4.0 * hf + 2.0 * ux + tofloat(lax.rem(i, 2)) + 0.5) / 64.0
        for r in range(0, 64, ROWS):
            rows = slice(r, r + ROWS)
            o = off_ref[0, rows]
            save(lin2, i, 32.0 * (a1 * o - b1 * (o - 0.5)), rows, slice(0, 128))
        return carry

    lax.fori_loop(0, 4, linear2, 0)

    n = fiota((1, 128), 1)
    nrow = fiota((128, 16), 0)
    column, owner = columns_of(owner_ref, 2 * lax.div(nrow, 16) + lax.rem(nrow, 2))
    erow = fiota((128, 16), 0)
    picks = (lax.rem(lax.div(erow, 4), 16) == fiota((128, 16), 1)).astype(F32).astype(BF16)
    wcol = dot(picks, owner, NT_DIMS)
    wu = lax.rem(lax.div(fiota((128, 128), 1), 2), 8)
    for v in range(2):
        keep = jnp.where(lax.rem(lax.div(fiota((128, 128), 0), 2), 2) == v, wcol, 0.0)
        for u in range(8):
            wmat[u * 128:(u + 1) * 128, v * 128:(v + 1) * 128] = jnp.where(
                wu == u, keep, 0.0).astype(BF16)

    u8 = lax.rem(lax.div(n, 2), 8)

    def parent(u):
        u1 = lax.rem(u, 4)
        u2 = lax.div(u, 4)
        return (tofloat(2 * lax.rem(u1, 2) + lax.rem(u2, 2)),
                tofloat(2 * lax.div(u1, 2) + lax.div(u2, 2)))

    pl.semaphore_wait(barrier, 14 + n_group)
    for g in range(1, n_group):
        tell(ready, lax.rem(h + g, n_group) * 16 + ry)

    def chunk(m, b):
        return w_hbm.at[:, :, pl.ds(pl.multiple_of(m * 256 + b * 128, 128), 128)]

    def exchange1(b, i):
        m = (lax.rem(lax.div(ry, 8) + i // 8, 2) * 8
             + lax.rem(lax.div(lax.rem(ry, 8), 2) + i // 2 % 4, 4) * 2 + lax.rem(ry + i, 2))
        return pltpu.make_async_remote_copy(
            src_ref=chunk(m, b), dst_ref=x_ref.at[b, ry], send_sem=send1.at[b * 16 + i],
            recv_sem=recv1.at[b * 16 + i], device_id=place(h * 16 + m), device_id_type=MESH)

    for b in range(2):
        for i in range(1, 16):
            exchange1(b, i).start()
    own1 = [pltpu.make_async_copy(chunk(ry, b), x_ref.at[b, ry], recv1.at[b * 16])
            for b in range(2)]
    for copy in own1:
        copy.start()

    def freq_rest(row, ix, iy, v1, v2, rows, lanes):
        square, base = row
        numer = v1 * prod[0, ix, rows, lanes] + v2 * prod[1, iy, rows, lanes]
        return numer / (root(square + numer) + base)

    def level1(i, carry):
        c = lax.rem(i, 4)
        u1 = lax.div(i, 4)
        a1 = (2.0 * hf + tofloat(bit(u1, 0)) + 0.5) / 32.0
        a2 = (tofloat(bit(u1, 1)) + 0.5) / 32.0
        v1, v2 = speeds(splat(a1), splat(a2))
        sx = 16.0 * (tofloat(bit(c, 0)) - 0.5)
        sy = 16.0 * (tofloat(bit(c, 1)) - 0.5)
        for r in range(0, 64, ROWS):
            line[r:r + ROWS] = -(a1 * (sx + 16.0 * doff[0, r:r + ROWS])
                                 + a2 * (sy + 16.0 * doff[1, r:r + ROWS]))

        def inner(u2, carry):
            for l in range(0, 256, 128):
                k = l // 128
                row = freq_row(32.0 * (2.0 * bx[k] + tofloat(bit(u2, 0)) + 0.5) - HALF,
                               32.0 * (2.0 * by[k] + tofloat(bit(u2, 1)) + 0.5) - HALF, v1, v2)
                for r in range(0, 64, ROWS):
                    rows = slice(r, r + ROWS)
                    lanes = slice(l, l + 128)
                    rest = freq_rest(row[2:], 2 * bit(c, 0) + bit(u2, 0),
                                     2 * bit(c, 1) + bit(u2, 1), v1, v2, rows, lanes)
                    save(tab1, i * 4 + u2, line[rows] - rest, rows, lanes)
            return carry

        lax.fori_loop(0, 4, inner, 0, unroll=2)
        return carry

    lax.fori_loop(0, 16, level1, 0)

    mirror = fiota((ROWS, 128), 1)
    mirror = lax.div(mirror, 64) * 64 + 63 - lax.rem(mirror, 64)

    def mirrored(tab, index, other, cycles, lin, which, r, lanes):
        cs, sn = trig(cycles)
        cl = lin[which, 0, r:r + ROWS]
        sl = lin[which, 1, r:r + ROWS]
        p, q, s, t = cs * cl, sn * sl, sn * cl, cs * sl
        tab[index, 0, r:r + ROWS, lanes] = p - q
        tab[index, 1, r:r + ROWS, lanes] = s + t
        for part_id, value in enumerate((p + q, s - t)):
            value = jnp.take_along_axis(value, mirror, axis=1, mode="promise_in_bounds")
            for k in range(0, ROWS, 8):
                to = 56 - r - k
                tab[other, part_id, to:to + 8, lanes] = value[k:k + 8]

    def level2(i, carry):
        u1 = lax.div(i, 2)
        a1 = (2.0 * hf + tofloat(bit(u1, 0)) + 0.5) / 32.0
        a2 = (tofloat(bit(u1, 1)) + 0.5) / 32.0
        v1, v2 = speeds(splat(a1), splat(a2))
        cy = tofloat(lax.rem(i, 2))
        cyi = lax.rem(i, 2)
        for r in range(0, 64, ROWS):
            rows = slice(r, r + ROWS)
            for l in range(0, 256, 128):
                k = l // 128
                lanes = slice(l, l + 128)
                row = freq_row(32.0 * (2.0 * bx[k] + 0.5) - HALF,
                               32.0 * (2.0 * by[k] + cy + 0.5) - HALF, v1, v2)
                part[rows, lanes] = (a2 * (32.0 * off_ref[1, rows])
                                     + freq_rest(row[2:], 6, 6 + cyi, v1, v2, rows, lanes))
        index = (u1 * 4 + 2 * cyi) * 4

        def inner(u2, carry):
            b1 = (4.0 * hf + 2.0 * tofloat(bit(u1, 0)) + tofloat(bit(u2, 0)) + 0.5) / 64.0
            b2 = (2.0 * tofloat(bit(u1, 1)) + tofloat(bit(u2, 1)) + 0.5) / 64.0
            w1, w2 = speeds(splat(b1), splat(b2))
            for l in range(0, 256, 128):
                k = l // 128
                lanes = slice(l, l + 128)
                row = freq_row(64.0 * (bx[k] + 0.5) - HALF, 64.0 * (by[k] + 0.5) - HALF, w1, w2)
                for r in range(0, 64, ROWS):
                    rows = slice(r, r + ROWS)
                    rest = freq_rest(row[2:], 4, 4 + cyi, w1, w2, rows, lanes)
                    down = (b2 * 32.0) * (off_ref[1, rows] + (cy - 0.5))
                    mirrored(tab2, index + u2, index + 4 + u2, part[rows, lanes] - down - rest,
                             lin2, bit(u1, 0) * 2 + bit(u2, 0), r, lanes)
            return carry

        lax.fori_loop(0, 4, inner, 0, unroll=2)
        return carry

    lax.fori_loop(0, 8, level2, 0)

    def middle(u, carry):
        u1 = lax.rem(u, 4)
        u2 = lax.div(u, 4)
        b1 = (4.0 * hf + 2.0 * tofloat(bit(u1, 0)) + tofloat(bit(u2, 0)) + 0.5) / 64.0
        b2 = (2.0 * tofloat(bit(u1, 1)) + tofloat(bit(u2, 1)) + 0.5) / 64.0
        w1, w2 = speeds(splat(b1), splat(b2))
        rows = [freq_row(64.0 * (bx[k] + 0.5) - HALF, 64.0 * (by[k] + 0.5) - HALF, w1, w2)
                for k in range(2)]
        for r in range(0, 64, ROWS):
            cols = freq_columns(64.0 * off_ref[0, r:r + ROWS], 64.0 * off_ref[1, r:r + ROWS],
                                b1, b2, w1, w2)
            for l in range(0, 256, 128):
                save(tabm, u, freq_cycles(cols, rows[l // 128]), slice(r, r + ROWS),
                     slice(l, l + 128))
        return carry

    lax.fori_loop(0, 16, middle, 0, unroll=2)

    def level3(half, carry):
        mx, my = parent(u8 + 8 * half)
        p1 = (4.0 * hf + mx + 0.5) / 64.0
        p2 = (my + 0.5) / 64.0
        row = (trig(p1), trig(p2))
        w1, w2 = from_sines(row[0][1], row[0][0], row[1][1], row[1][0])
        for r in range(0, 64, ROWS):
            rows = slice(r, r + ROWS)
            d1 = off_ref[0, rows] / 64.0
            d2 = off_ref[1, rows] / 64.0
            s1, s2 = speeds_sum(row, (trig(d1), trig(d2)))
            for v in range(4):
                f1 = 128.0 * (2.0 * column + (v % 2) + 0.5) - HALF
                f2 = 128.0 * (2.0 * ryf + (v // 2) + 0.5) - HALF
                cycles = space_cycles(d1, d2, s1, s2, w1, w2, f1, f2)
                save(tab3i, half * 4 + v, -cycles, rows, slice(0, 128))
        return carry

    lax.fori_loop(0, 2, level3, 0)

    def level4(i, carry):
        half = lax.div(i, 4)
        jx = tofloat(bit(lax.rem(i, 4), 0))
        jy = tofloat(bit(lax.rem(i, 4), 1))
        mx, my = parent(u8 + 8 * half)
        mx = 4.0 * hf + mx
        w1, w2 = speeds((mx + 0.5) / 64.0, (my + 0.5) / 64.0)
        c1 = (2.0 * mx + jx + 0.5) / 128.0
        c2 = (2.0 * my + jy + 0.5) / 128.0
        row = (trig(c1), trig(c2))
        z1, z2 = from_sines(row[0][1], row[0][0], row[1][1], row[1][0])
        for r in range(0, 64, ROWS):
            rows = slice(r, r + ROWS)
            d1 = off_ref[0, rows] / 128.0
            d2 = off_ref[1, rows] / 128.0
            s1, s2 = speeds_sum(row, (trig(d1), trig(d2)))
            e1 = d1 + (jx - 0.5) / 128.0
            e2 = d2 + (jy - 0.5) / 128.0
            for v in range(4):
                f1 = 128.0 * (2.0 * column + (v % 2) + 0.5) - HALF
                f2 = 128.0 * (2.0 * ryf + (v // 2) + 0.5) - HALF
                cycles = space_cycles(e1, e2, s1, s2, w1, w2, f1, f2)
                save(tab3o, i * 4 + v, cycles, rows, slice(0, 128))
            f1 = 256.0 * (column + 0.5) - HALF
            f2 = 256.0 * (ryf + 0.5) - HALF
            cycles = space_cycles(d1, d2, s1, s2, z1, z2, f1, f2)
            save(tab4i, i, -cycles, rows, slice(0, 128))
        return carry

    lax.fori_loop(0, 8, level4, 0)

    yi = lax.div(flat, 32)
    x0 = lax.rem(lax.div(flat, 8), 4)
    zc = lax.rem(flat, 8)
    z0 = lax.div(zc, 2)
    c0 = lax.rem(zc, 2)
    x1 = x0 + 1 - 2 * lax.rem(x0, 2)

    def at_device(y, x, m):
        return place(y * 32 + x * 8 + m)

    def near(x, o):
        return 3 - x if o else x

    def remote(source, target, sender, receiver, device):
        return pltpu.make_async_remote_copy(
            src_ref=source, dst_ref=target, send_sem=sender, recv_sem=receiver,
            device_id=device, device_id_type=MESH)

    def arrive(ref, semaphore):
        pltpu.make_async_copy(ref, ref, semaphore).wait()

    pairs_of = [(t, o) for t in (0, 1, 3, 2) for o in (0, 1)]

    def spread(d):
        return lax.rem(z0 + d // 2, 4) * 2 + lax.rem(c0 + d, 2)

    def e_first():
        for t, o in pairs_of:
            yk = lax.rem(yi + t, 4)
            xk = near(x0, o)
            block = z_ref.at[0, yk * 2 + lax.div(xk, 2)]
            s = o * 4 + t
            if s == 0:
                pltpu.make_async_copy(block, e_ref.at[yi, x0], ea.at[s]).start()
            else:
                remote(block, e_ref.at[yi, x0], sea.at[s], ea.at[s],
                       at_device(yk, xk, zc)).start()

    def x_first():
        for t, o in pairs_of:
            yk = lax.rem(yi + t, 4)
            xk = near(x0, o)
            k = yk * 2 + lax.div(xk, 2)
            s = o * 4 + t
            for d in (4, 5, 2, 3, 6, 7, 0, 1):
                m = spread(d)
                block = z_ref.at[1, k, lax.rem(m, 4)]
                if s == 0 and d == 0:
                    pltpu.make_async_copy(block, y_ref.at[1, yi, x0, zc], xa.at[s]).start()
                else:
                    remote(block, y_ref.at[1, yi, x0, zc], sxa.at[s], xa.at[s],
                           at_device(yk, xk, m)).start()

    def e_pass():
        for t, o in pairs_of:
            s = o * 4 + t
            block = e_ref.at[lax.rem(yi + 4 - t, 4), near(x0, o)]
            arrive(block, ea.at[s])
            remote(block, block, seb.at[s], eb.at[s], at_device(yi, x1, zc)).start()

    def x_pass():
        for t, o in pairs_of:
            s = o * 4 + t
            block = y_ref.at[1, lax.rem(yi + 4 - t, 4), near(x0, o)]
            arrive(block, xa.at[s])
            remote(block, block, sxb.at[s], xb.at[s], at_device(yi, x1, zc)).start()

    def e_last(x, o):
        xs = near(x, o)
        for d in (4, 5, 2, 3, 6, 7, 1, 0):
            m = spread(d)
            block = e_ref.at[:, xs, lax.rem(m, 4)]
            if d == 0:
                pltpu.make_async_copy(block, y_ref.at[0, :, xs, zc], ec.at[xs]).start()
            else:
                remote(block, y_ref.at[0, :, xs, zc], sec, ec.at[xs],
                       at_device(yi, x0, m)).start()

    def send_half(half):
        pl.when(half == 0)(e_first)
        pl.when(half == 1)(x_first)

    def stage(b):
        at = slice(b * 128, b * 128 + 128)
        whole = slice(0, 128)

        def turned(slot, source, tab, index):
            for c in range(4):
                for r in range(0, 64, ROWS):
                    rows = slice(r, r + ROWS)
                    re, im = source(c, rows)
                    parts = turn(re, im, tab, index(c), rows, at)
                    for p in range(2):
                        hi, lo = split(parts[p])
                        xh[slot, c * 64 + r:c * 64 + r + ROWS, p * 128:p * 128 + 128] = hi
                        xl[slot, c * 64 + r:c * 64 + r + ROWS, p * 128:p * 128 + 128] = lo

        def mixed(slot, table):
            first = dot(table[...], xh[slot])
            return first[:64] + first[64:] + dot(table[0:64], xl[slot])

        def run1(e, carry):
            ux = lax.rem(lax.div(ry, 8) + lax.div(e, 2), 2)
            uz = lax.rem(lax.div(ry, 4) + e, 2)
            u2 = 2 * ux + uz
            for c in range(4):
                i = (lax.rem(lax.div(ry, 8) + ux, 2) * 8
                     + lax.rem(lax.div(lax.rem(ry, 8), 2) + 4 - 2 * uz - c // 2, 4) * 2
                     + lax.rem(ry + c, 2))
                landed = x_ref.at[b, u2 * 4 + c]
                pltpu.make_async_copy(landed, landed, recv1.at[b * 16 + i]).wait()
            for u1 in range(4):
                turned(u1, lambda c, rows: (x_ref[b, u2 * 4 + c, 0, rows],
                                            x_ref[b, u2 * 4 + c, 1, rows]),
                       tab1, lambda c: (u1 * 4 + c) * 4 + u2)
                y1[u1 * 4 + u2] = mixed(u1, t1s)
            return carry

        lax.fori_loop(0, 4, run1, 0)

        def run2(half, pair):
            for slot in range(4):
                u1 = 2 * pair + slot // 2
                u2 = 2 * half + slot % 2
                u = u1 + 4 * u2
                turned(slot, lambda c, rows: (y1[u1 * 4 + c, rows, 0:128],
                                              y1[u1 * 4 + c, rows, 128:256]),
                       tab2, lambda c: (u1 * 4 + c) * 4 + u2)
                out = mixed(slot, t1_ref)
                to = pl.ds(pl.multiple_of((u1 + 4 * (slot % 2)) * 128, 128), 128)
                for r in range(0, 64, ROWS):
                    rows = slice(r, r + ROWS)
                    parts = turn(out[rows, 0:128], out[rows, 128:256], tabm, u, rows, at)
                    for p in range(2):
                        hi, lo = split(parts[p])
                        y2[p * 64 + r:p * 64 + r + ROWS, to] = hi
                        y2[128 + p * 64 + r:128 + p * 64 + r + ROWS, to] = lo

        def run3(half):
            both = dot(y2[...], wmat[...])
            summed = both[:128] + both[128:]
            for v in range(2):
                for r in range(0, 64, ROWS):
                    rows = slice(r, r + ROWS)
                    l = v * 128
                    parts = turn(summed[r:r + ROWS, l:l + 128],
                                 summed[64 + r:64 + r + ROWS, l:l + 128], tab3i,
                                 half * 4 + 2 * b + v, rows, whole)
                    for p in range(2):
                        hi, lo = split(parts[p])
                        to = slice((v * 2 + p) * 128, (v * 2 + p + 1) * 128)
                        x3[r:r + ROWS, to] = hi
                        x3[64 + r:64 + r + ROWS, to] = lo
                        x3[128 + r:128 + r + ROWS, to] = hi
            for j in range(4):
                out = dot(t3_ref[j * 64:(j + 1) * 64], x3[...])
                for r in range(0, 64, ROWS):
                    rows = slice(r, r + ROWS)
                    low = slice(64 + r, 64 + r + ROWS)
                    if b == 1:
                        re, im = v4[half * 4 + j, rows], v4[half * 4 + j, low]
                    for v in range(2):
                        l = v * 256
                        p, q = turn(out[rows, l:l + 128], out[rows, l + 128:l + 256], tab3o,
                                    (half * 4 + j) * 4 + 2 * b + v, rows, whole)
                        first = b == 0 and v == 0
                        re = p if first else re + p
                        im = q if first else im + q
                    if b == 1:
                        re, im = turn(re, im, tab4i, half * 4 + j, rows, whole)
                    v4[half * 4 + j, rows] = re
                    v4[half * 4 + j, low] = im
                if b == 1:
                    flipped = v4[half * 4 + j].T
                    for k in range(8):
                        z_ref[half, k, j] = flipped[k * 16:(k + 1) * 16]

        def run(half, carry):
            def pairs(pair, carry):
                run2(half, pair)
                return carry

            lax.fori_loop(0, 2, pairs, 0)
            run3(half)
            if b == 1:
                send_half(half)
            return carry

        lax.fori_loop(0, 2, run, 0)

    for b in range(2):
        if b == 1:
            pl.semaphore_wait(ready, n_group - 1)
        stage(b)

    e_pass()
    e_last(x0, 0)
    e_last(x0, 1)
    x_pass()
    for o in range(2):
        for t in (0, 1, 3, 2):
            arrive(e_ref.at[lax.rem(yi + 4 - t, 4), near(x1, o)], eb.at[o * 4 + t])
        e_last(x1, o)

    v1d = lax.rem(ry, 4)
    v2d = lax.div(ry, 4)
    zero = jnp.zeros((64, 64), BF16)
    pieces = [dot(onehot, tf_ref[p, pl.ds(pl.multiple_of(v2d * 64, 64), 64), :],
                  TN_DIMS).astype(BF16) for p in range(2)]
    for p in range(2):
        for q in range(2):
            for piece in range(2):
                for low in range(2):
                    lanes = slice(low * 128 + q * 64, low * 128 + q * 64 + 64)
                    rows = slice(piece * 128 + p * 64, piece * 128 + p * 64 + 64)
                    use = p == q and not (piece == 1 and low == 1)
                    tmat[rows, lanes] = pieces[piece] if use else zero
    ids = fiota((512, 16), 0)
    column, _ = columns_of(owner_ref, 2 * h + lax.rem(lax.div(ids, 16), 2))
    jx, jy = tofloat(lax.rem(v2d, 2)), tofloat(lax.div(v2d, 2))
    vx, vy = tofloat(lax.rem(v1d, 2)), tofloat(lax.div(v1d, 2))
    f2 = 256.0 * (tofloat(lax.rem(n, 16)) + 0.5) - HALF

    def level5(src, carry):
        for l in range(0, 512, 128):
            mx, my = parent(lax.div(n + l, 32))
            c1 = (2.0 * (4.0 * tofloat(src) + mx) + vx + 0.5) / 128.0
            c2 = (2.0 * my + vy + 0.5) / 128.0
            row = (trig(c1), trig(c2))
            w1, w2 = from_sines(row[0][1], row[0][0], row[1][1], row[1][0])
            f1 = 256.0 * (column[:, l:l + 128] + 0.5) - HALF
            for r in range(0, 64, ROWS):
                d1 = (doff[0, r:r + ROWS] + (jx - 0.5)) / 256.0
                d2 = (doff[1, r:r + ROWS] + (jy - 0.5)) / 256.0
                s1, s2 = speeds_sum(row, (trig(d1), trig(d2)))
                save(tabf, src, space_cycles(d1, d2, s1, s2, w1, w2, f1, f2),
                     slice(r, r + ROWS), slice(l, l + 128))
        return carry

    lax.fori_loop(0, 8, level5, 0)

    def run4(half, src):
        for m in range(16):
            yy[pl.ds(m, 16, stride=16), :] = y_ref[half, lax.div(src, 2),
                                                  lax.rem(src, 2) * 2 + m // 8, m % 8]
        hi, lo = split(yy[...])
        out = dot(tmat[...], jnp.concatenate([hi, lo], axis=1), NT_DIMS)
        out = out[:128] + out[128:]
        for l in range(0, 256, 128):
            there = slice(half * 256 + l, half * 256 + l + 128)
            lanes = pl.ds(pl.multiple_of(src * 512 + half * 256 + l, 128), 128)
            for r in range(0, 64, ROWS):
                rows = slice(r, r + ROWS)
                re, im = turn(out[r:r + ROWS, l:l + 128], out[64 + r:64 + r + ROWS, l:l + 128],
                              tabf, src, rows, there)
                o_ref[0, rows, lanes] = re
                o_ref[1, rows, lanes] = im

    for o in range(2):
        pair = lax.div(near(x0, o), 2)

        def half1(e, carry):
            t = e + lax.div(e, 2) - 2 * lax.div(e, 3)
            ys = lax.rem(yi + 4 - t, 4)
            arrive(y_ref.at[1, ys, near(x1, o)], xb.at[o * 4 + t])
            run4(1, ys * 2 + pair)
            return carry

        def half0(ys, carry):
            run4(0, ys * 2 + pair)
            return carry

        lax.fori_loop(0, 4, half1, 0)
        for x in (x0, x1):
            arrive(y_ref.at[0, :, near(x, o)], ec.at[near(x, o)])
        lax.fori_loop(0, 4, half0, 0)
    sent = y_ref.at[0, :, :, pl.ds(0, 7)]
    arrive(sent, sec)
    for s in range(8):
        if s > 0:
            arrive(e_ref.at[0, 0], sea.at[s])
            arrive(y_ref.at[1, 0, 0], sxa.at[s])
        arrive(e_ref.at[0, 0], seb.at[s])
        arrive(y_ref.at[1, 0, 0], sxb.at[s])
    arrive(y_ref.at[1, 0, 0, pl.ds(0, 7)], sxa.at[0])
    for b in range(2):
        for i in range(1, 16):
            exchange1(b, i).wait_send()


VMEM_LIMIT = 60 * 1024 * 1024


def body(weights, owner_map, node_index):
    t1, t3, tf, off, off3 = constants()
    n_dev = lax.axis_size("dev")
    n_all = lax.axis_size("grp") * n_dev
    vmem = pl.BlockSpec(memory_space=pltpu.VMEM)
    hbm = pl.BlockSpec(memory_space=pltpu.HBM)
    dma = pltpu.SemaphoreType.DMA
    return pl.pallas_call(
        functools.partial(kernel, n_dev, n_all, n_all // 16),
        out_shape=pltpu.VMEM((2, 64, 4096), F32),
        in_specs=[vmem] * 2 + [hbm] * 6,
        out_specs=vmem,
        scratch_shapes=[
            pltpu.VMEM((4, 4, 4, 16, 128), F32),
            pltpu.VMEM((2, 16, 2, 64, 128), F32),
            pltpu.VMEM(t1.shape, BF16),
            pltpu.VMEM(t3.shape, BF16),
            pltpu.VMEM(tf.shape, BF16),
            pltpu.VMEM(off.shape, F32),
            pltpu.VMEM(off3.shape, BF16),
            pltpu.VMEM((2, 8, 4, 16, 128), F32),
            pltpu.VMEM((2, 4, 4, 8, 16, 128), F32),
            pltpu.VMEM((64, 2, 64, 256), F32),
            pltpu.VMEM((64, 2, 64, 256), F32),
            pltpu.VMEM((16, 2, 64, 256), F32),
            pltpu.VMEM((8, 2, 64, 128), F32),
            pltpu.VMEM((32, 2, 64, 128), F32),
            pltpu.VMEM((8, 2, 64, 128), F32),
            pltpu.VMEM((8, 2, 64, 512), F32),
            pltpu.VMEM((4, 2, 64, 128), F32),
            pltpu.VMEM((64, 128), F32),
            pltpu.VMEM((2, 8, 64, 256), F32),
            pltpu.VMEM((64, 256), F32),
            pltpu.VMEM((2, 64, 128), F32),
            pltpu.VMEM((128, 256), BF16),
            pltpu.VMEM((4, 256, 256), BF16),
            pltpu.VMEM((4, 256, 256), BF16),
            pltpu.VMEM((16, 64, 256), F32),
            pltpu.VMEM((256, 1024), BF16),
            pltpu.VMEM((1024, 256), BF16),
            pltpu.VMEM((192, 512), BF16),
            pltpu.VMEM((8, 128, 128), F32),
            pltpu.VMEM((256, 256), BF16),
            pltpu.VMEM((256, 128), F32),
            dma((32,)),
            dma((32,)),
            dma((8,)),
            dma((8,)),
            dma((8,)),
            dma((8,)),
            dma(()),
            dma((4,)),
            dma((8,)),
            dma((8,)),
            dma((8,)),
            dma((8,)),
            dma((5,)),
            pltpu.SemaphoreType.REGULAR,
        ],
        compiler_params=pltpu.CompilerParams(
            vmem_limit_bytes=VMEM_LIMIT, collective_id=0, has_side_effects=True),
        name="butterfly",
    )(node_index, owner_map.reshape(1, 16), weights, t1, t3, tf, off, off3)


def solution(mesh):
    in_specs = (P(None, None, ("grp", "dev")), P(), P())
    out_specs = P(None, None, ("grp", "dev"))
    return jax.shard_map(body, mesh=mesh, in_specs=in_specs, out_specs=out_specs, check_vma=False)
```
